32 devices in a mesh: groups: 2 (over y), blk: 8 (over z, x), sub: 2 (over core).
Axes of the slice: x: 2, y: 2, z: 4, core: 2. Of those that a mesh axis runs over, the one named last changes fastest.
Arguments:
- embeddings: bfloat16 [16384, 1024], P(('groups', 'blk', 'sub')), parts along dimension 0, may hold values from -0.1875 to 0.1875
- start_panel: bfloat16 [16384, 128], P(('groups', 'blk', 'sub')), parts along dimension 0, may hold values from -6 to 6
- tile_mask: int32 [128, 56], P(('groups', 'blk', 'sub')), parts along dimension 0, may hold values from 0 to 1, as said below
- inv_width: float32 [1], replicated, may hold values from 0.5 to 1.5
Outputs:
- basis: float32 [16384, 128], P(('groups', 'blk', 'sub')), parts along dimension 0
- upper: float32 [256, 128], P('groups'), parts along dimension 0
The draws below stay inside these ranges and needn't reach their ends.
There are 2 independent parts, one for each index of `groups`. The reference program is written for one: setup_inputs(seed, part) draws one part's arguments, and reference() takes and returns one part's arrays. A program takes and returns all parts, laid end to end along the dimension named above; an argument that names none is the same for every part. Nothing has to cross between parts.
Inputs may be any that keep to these rules, and one draw needn't show every extreme that they name: `tile_mask`: 0 or 1; the entry of every tile for its own tile is 1.
All inputs are finite; a program needn't handle non-finite values.
Results may differ from the reference program's by a relative error of at most 0.0088.
Values may be sent and summed in bfloat16 or wider, within the bound.
No kernel may reach another device: no remote copies, remote signals or barrier semaphores. Data moves between devices by JAX's collectives and lax.ppermute only.
A program may use at most 64 MiB of HBM per device.

```python
import jax
import jax.numpy as jnp
from jax import lax

D = 1024
C = 128
TILE = 128
REACH = 3
RB_DEV = 4
NB = 64
RECORDS = 8192
WINB = 56
N_BLK = 8
N_SUB = 2


def draw_tile_mask(key, part):
    blk_blocks = N_SUB * RB_DEV
    width = 2 * REACH + 1
    key_level, key_entry, key_active = jax.random.split(key, 3)
    levels = jax.random.randint(key_level, (NB, 1), 1, 17)
    entries = jax.random.randint(key_entry, (NB, WINB), 0, 16) < levels
    active = jax.random.randint(key_active, (N_BLK, width), 0, 3) > 0
    row_blk = jnp.arange(NB) // blk_blocks
    col_off = jnp.arange(WINB) // blk_blocks
    active_rows = active[row_blk][:, col_off] | (col_off[None, :] == REACH)
    diagonal = jnp.arange(WINB)[None, :] == REACH * blk_blocks + (jnp.arange(NB) % blk_blocks)[:, None]
    return jnp.where(diagonal | entries & active_rows, 1, 0).astype(jnp.int32)


def draw_embeddings(key, part):
    base = jax.random.fold_in(key, 7321)
    key_centre = jax.random.fold_in(base, 0)
    key_offset = jax.random.fold_in(base, 2)
    key_pick = jax.random.fold_in(base, 3)
    key_noise = jax.random.fold_in(base, 4)
    key_level = jax.random.fold_in(base, 5)
    blk_rows = N_SUB * RB_DEV * TILE
    pool_size = blk_rows // 2
    unit = D ** (-0.5)
    centres = jax.random.normal(key_centre, (N_BLK * pool_size, D), jnp.float32)
    noise_lo, noise_hi = (0.11, 0.5)
    offsets = jax.random.randint(key_offset, (RECORDS,), -REACH, REACH + 1)
    picks = jax.random.randint(key_pick, (RECORDS,), 0, pool_size)
    row_blk = jnp.arange(RECORDS) // blk_rows
    owner = ((row_blk + offsets) % N_BLK * pool_size + picks).astype(jnp.int32)
    noise_level = jnp.exp(jax.random.uniform(key_level, (RECORDS, 1), jnp.float32, jnp.log(noise_lo), jnp.log(noise_hi)))
    noise = jax.random.normal(key_noise, (RECORDS, D), jnp.float32)
    values = (centres[owner] + noise_level * noise) * unit
    return jnp.clip(values, -6.0 * unit, 6.0 * unit).astype(jnp.bfloat16)


def level_of(key, dims, cuts, smallest, top_value):
    gain = 1.0
    for axis_at, shards_of in cuts:
        draws = jax.random.uniform(jax.random.fold_in(jax.random.fold_in(key, 6), axis_at), (shards_of,), jnp.float32, smallest / len(cuts), top_value / len(cuts))
        gain = gain * jnp.repeat(jnp.exp(draws), dims[axis_at] // shards_of).reshape((-1,) + (1,) * (len(dims) - 1 - axis_at))
    return gain


def bell_draw(own_key, extent, spread, bound, shards=(), kind=jnp.bfloat16):
    values = spread * jax.random.normal(own_key, extent, jnp.float32)
    if shards:
        values = values * level_of(own_key, extent, shards, -0.22, 0.18)
    return jnp.clip(values, -bound, bound).astype(kind)


def setup_inputs(seed: int = 0, part: int = 0) -> dict:
    arg_keys = jax.random.split(jax.random.key(seed), 5)
    part_splits = jax.random.split(jax.random.fold_in(arg_keys[4], part), 5)
    return {
        "embeddings": draw_embeddings(jax.random.fold_in(jax.random.fold_in(arg_keys[4], part), 71), part),
        "start_panel": bell_draw(part_splits[1], (RECORDS, C), 1.0, 6.0, ((0, 16),)),
        "tile_mask": draw_tile_mask(jax.random.fold_in(jax.random.fold_in(arg_keys[4], part), 71), part),
        "inv_width": jnp.clip(jax.random.uniform(arg_keys[3], (1,), jnp.float32, 0.5, 1.5), 0.5, 1.5),
    }


def reference(embeddings, start_panel, tile_mask, inv_width):
    blk_blocks = N_SUB * RB_DEV
    blk_rows = blk_blocks * TILE
    width = 2 * REACH + 1
    embed_cube = embeddings.reshape(N_BLK, blk_rows, D)
    panel_cube = start_panel.reshape(N_BLK, blk_rows, C)
    mask_cube = tile_mask.reshape(N_BLK, blk_blocks, width * blk_blocks)
    sq_all = jnp.sum(jnp.square(embeddings.astype(jnp.float32)), axis=1).reshape(N_BLK, blk_rows)

    def block_rows(blk_index):
        source_idx = ((blk_index - REACH + jnp.arange(width, dtype=jnp.int32)) % N_BLK).astype(jnp.int32)
        row_embed = embed_cube[blk_index].astype(jnp.float32)
        col_embed = embed_cube[source_idx].reshape(width * blk_rows, D).astype(jnp.float32)
        col_panel = panel_cube[source_idx].reshape(width * blk_rows, C)
        col_sq = sq_all[source_idx].reshape(width * blk_rows)
        gram_tile = jnp.dot(row_embed.astype(jnp.float32), col_embed.T.astype(jnp.float32), preferred_element_type=jnp.float32)
        distance = jnp.maximum(sq_all[blk_index][:, None] + col_sq[None, :] - 2.0 * gram_tile, 0.0)
        kernel = jnp.exp(-inv_width[0] * distance).reshape(blk_blocks, TILE, width * blk_blocks, TILE)
        kernel = kernel * mask_cube[blk_index].astype(jnp.float32)[:, None, :, None]
        kernel = kernel.reshape(blk_rows, width * blk_rows).astype(jnp.bfloat16)
        return jnp.dot(kernel.astype(jnp.float32), col_panel.astype(jnp.float32), preferred_element_type=jnp.float32)
    image = lax.map(block_rows, jnp.arange(N_BLK, dtype=jnp.int32)).reshape(RECORDS, C)
    gram_full = jnp.dot(image.T.astype(jnp.float32), image.astype(jnp.float32), precision=lax.Precision.HIGHEST, preferred_element_type=jnp.float32)
    lower_factor = jnp.linalg.cholesky(gram_full)
    basis = lax.linalg.triangular_solve(lower_factor, image, left_side=False, lower=True, transpose_a=True)
    return (basis, lower_factor.T)
```

```python
import functools

import jax
import jax.numpy as jnp
from jax import lax
from jax.experimental import pallas as pl
from jax.experimental.pallas import tpu as pltpu
from jax.sharding import PartitionSpec as P

TILE = 128
REACH = 3
F32 = jnp.float32
BF16 = jnp.bfloat16
VMEM = pltpu.VMEM


def vmem_call(body, out_shapes, *operands, smem=0):
    spec = lambda space: pl.BlockSpec(memory_space=space)
    return pl.pallas_call(
        body,
        out_shape=out_shapes,
        in_specs=[spec(pltpu.SMEM)] * smem + [spec(VMEM)] * (len(operands) - smem),
        out_specs=jax.tree.map(lambda _: spec(VMEM), out_shapes),
        compiler_params=pltpu.CompilerParams(vmem_limit_bytes=48 << 20),
    )(*operands)


def shape(*dims):
    return jax.ShapeDtypeStruct(dims, F32)


def kernel_tile(inverse, rows2, row_sq, cols, col_sq):
    gram2 = lax.dot_general(rows2, cols, (((1,), (1,)), ((), ())), preferred_element_type=F32)
    return jnp.exp(-inverse * jnp.maximum(row_sq + col_sq - gram2, 0.0))


def masked(kernel, mask, first):
    tiles = kernel.shape[0] // TILE
    return jnp.concatenate(
        [kernel[i * TILE : (i + 1) * TILE] * mask[first + i : first + i + 1] for i in range(tiles)], axis=0
    ).astype(BF16)


def row_squares(rows):
    wide = rows.astype(F32)
    return jnp.sum(wide * wide, axis=1, keepdims=True)


def pair_products(inverse, rows_ref, rows_panel_ref, start, size, others, transposed):
    rows = rows_ref[start : start + size]
    row_sq = row_squares(rows)
    rows2 = rows * 2
    panel_t = None
    if transposed is not None:
        panel_t = rows_panel_ref[start : start + size].astype(F32).T.astype(BF16)
    half = 4
    image = None
    first = start // TILE
    for k, (cols, panel, col_sq, mask_ref) in enumerate(others):
        mask = mask_ref[...]
        kernel = kernel_tile(inverse, rows2, row_sq, cols[...], col_sq[...])
        term = jnp.dot(masked(kernel, mask, first), panel[...], preferred_element_type=F32)
        image = term if image is None else image + term
        if transposed is not None:
            back = jnp.dot(panel_t, masked(kernel, mask, half + first), preferred_element_type=F32)
            transposed[k] = back if transposed[k] is None else transposed[k] + back
    return image


def self_body(inverse_ref, e0, p0, s0, e1, p1, s1, m0, m1, image):
    rows = e0.shape[0]
    step = rows // 2
    for start in range(0, rows, step):
        image[start : start + step] = pair_products(
            inverse_ref[0], e0, p0, start, step, [(e0, p0, s0, m0), (e1, p1, s1, m1)], None
        )


def below_body(inverse_ref, x, xp, e0, p0, s0, m0, e1, p1, s1, m1, image, t0, t1):
    rows = x.shape[0]
    step = rows // 2
    back = [None, None]
    for start in range(0, rows, step):
        image[start : start + step] = pair_products(
            inverse_ref[0], x, xp, start, step, [(e0, p0, s0, m0), (e1, p1, s1, m1)], back
        )
    t0[...] = back[0]
    t1[...] = back[1]


def above_body(part, last, inverse_ref, x, xp, *refs):
    others = [refs[4 * k : 4 * k + 4] for k in range(4)]
    refs = refs[16:]
    sums = refs[: (2 if part == 0 else 4)]
    refs = refs[len(sums) :]
    rows = x.shape[0]
    back = [s[...] for s in sums] + [None] * (4 - len(sums))
    first = part * rows
    inverse = inverse_ref[0]
    if last:
        own_image, below_image = refs[:2]
        refs = refs[2:]
    image = refs[0]
    image[...] = above_products(inverse, x, xp, first, others, back)
    if not last:
        for out, value in zip(refs[1:], back):
            out[...] = value
        return
    own_out, below_out, cross_out = refs[1:]
    half = own_image.shape[0]
    own_out[...] = own_image[...] + back[0].T
    below_out[...] = below_image[...] + back[2].T
    cross_out[:half] = back[3].T
    cross_out[half:] = back[1].T


def above_products(inverse, x, xp, first, others, back):
    rows = x[...]
    row_sq = row_squares(rows)
    rows2 = rows * 2
    panel_t = xp[...].astype(F32).T.astype(BF16)
    image = None
    tile = first // TILE
    for k, (cols, panel, col_sq, mask_ref) in enumerate(others):
        mask = mask_ref[...]
        kernel = kernel_tile(inverse, rows2, row_sq, cols[...], col_sq[...])
        term = jnp.dot(masked(kernel, mask, tile), panel[...], preferred_element_type=F32)
        image = term if image is None else image + term
        term = jnp.dot(panel_t, masked(kernel, mask, 4 + tile), preferred_element_type=F32)
        back[k] = term if back[k] is None else back[k] + term
    return image


def gram_body(own, cross, below, above0, above1, image, gram):
    half = own.shape[0]
    part = above0.shape[0]
    total = own[...] + cross[half:] + below[...]
    total = total + jnp.concatenate([above0[...], above1[...]], axis=0)
    image[...] = total
    gram[...] = lax.dot_general(
        total, total, (((0,), (0,)), ((), ())), precision=lax.Precision.HIGHEST, preferred_element_type=F32
    )


def per_device(embeddings, start_panel, tile_mask, inv_width):
    n_blk, n_sub = lax.axis_size("blk"), lax.axis_size("sub")
    half, width = start_panel.shape
    tiles = half // TILE
    part = half // 2
    sub = lax.axis_index("sub")
    ring = lambda by: [(i, (i + by) % n_blk) for i in range(n_blk)]
    swap = [(0, 1), (1, 0)]
    blk_move = lambda v, by: lax.ppermute(v, "blk", ring(by))
    sub_move = lambda v: lax.ppermute(v, "sub", swap)

    below_e, below_p = blk_move(embeddings, 1), blk_move(start_panel, 1)
    above = [
        (blk_move(embeddings[i * part : (i + 1) * part], -2), blk_move(start_panel[i * part : (i + 1) * part], -2))
        for i in range(2)
    ]
    other_e, other_p = sub_move(embeddings), sub_move(start_panel)
    other_mask = sub_move(tile_mask)
    own_mask = jnp.concatenate([tile_mask, other_mask], axis=0).reshape(2, tiles, 2 * REACH + 1, 2, tiles)
    own_mask = jnp.where(sub == 0, own_mask, own_mask[:, :, :, ::-1]).astype(F32)
    own_mask = own_mask.reshape(2 * tiles, -1)
    below_mask, above_mask = blk_move(own_mask, 1), blk_move(own_mask, -2)
    split = lambda m: m.reshape(2, tiles, 2 * REACH + 1, 2, tiles)
    own_mask, below_mask, above_mask = split(own_mask), split(below_mask), split(above_mask)

    def pair_mask(rows, cols, offset, which):
        forward = rows[0, :, REACH + offset, which, :]
        backward = cols[which, :, REACH - offset, 0, :].T
        return jnp.repeat(jnp.concatenate([forward, backward], axis=0), TILE, axis=1)

    squares = lambda e: jnp.sum(jnp.square(e.astype(F32)), axis=1)[None, :]
    own = (embeddings, start_panel, squares(embeddings))
    other = (other_e, other_p, squares(other_e))
    own_image = vmem_call(
        self_body,
        shape(half, width),
        inv_width,
        *own,
        *other,
        pair_mask(own_mask, own_mask, 0, 0),
        pair_mask(own_mask, own_mask, 0, 1),
        smem=1,
    )
    below_other_e, below_other_p = sub_move(below_e), sub_move(below_p)
    below_image, t_own, t_other = vmem_call(
        below_body,
        (shape(half, width), shape(width, half), shape(width, half)),
        inv_width,
        below_e,
        below_p,
        *own,
        pair_mask(below_mask, own_mask, 1, 0),
        *other,
        pair_mask(below_mask, own_mask, 1, 1),
        smem=1,
    )
    below = (below_e, below_p, squares(below_e))
    below_other = (below_other_e, below_other_p, squares(below_other_e))
    others = [
        *own,
        pair_mask(above_mask, own_mask, -2, 0),
        *other,
        pair_mask(above_mask, own_mask, -2, 1),
        *below,
        pair_mask(above_mask, below_mask, -3, 0),
        *below_other,
        pair_mask(above_mask, below_mask, -3, 1),
    ]
    above_image0, *sums = vmem_call(
        functools.partial(above_body, 0, False),
        (shape(part, width),) + (shape(width, half),) * 4,
        inv_width,
        *above[0],
        *others,
        t_own,
        t_other,
        smem=1,
    )
    above_image1, own_image, below_image, cross = vmem_call(
        functools.partial(above_body, 1, True),
        (shape(part, width), shape(half, width), shape(half, width), shape(2 * half, width)),
        inv_width,
        *above[1],
        *others,
        *sums,
        own_image,
        below_image,
        smem=1,
    )
    cross = sub_move(cross)
    above_image0, above_image1 = blk_move(above_image0, 2), blk_move(above_image1, 2)
    below_image = blk_move(below_image + cross[:half], -1)
    image, gram = vmem_call(
        gram_body, (shape(half, width), shape(width, width)), own_image, cross, below_image, above_image0, above_image1
    )
    if n_blk & (n_blk - 1):
        gram = lax.psum(gram, ("blk", "sub"))
    else:
        gram = gram + sub_move(gram)
        hop = 1
        while hop < n_blk:
            gram = gram + lax.ppermute(gram, "blk", [(i, i ^ hop) for i in range(n_blk)])
            hop *= 2
    lower_factor = jnp.linalg.cholesky(gram)
    basis = lax.linalg.triangular_solve(lower_factor, image, left_side=False, lower=True, transpose_a=True)
    return (basis, lower_factor.T)


def solution(mesh):
    return jax.shard_map(
        per_device,
        mesh=mesh,
        in_specs=(
            P(("groups", "blk", "sub"), None),
            P(("groups", "blk", "sub"), None),
            P(("groups", "blk", "sub"), None),
            P(),
        ),
        out_specs=(P(("groups", "blk", "sub"), None), P("groups", None)),
        check_vma=False,
    )
```

```python
import functools

import jax
import jax.numpy as jnp
from jax import lax
from jax.experimental import pallas as pl
from jax.experimental.pallas import tpu as pltpu
from jax.sharding import PartitionSpec as P

TILE = 128
REACH = 3
F32 = jnp.float32
BF16 = jnp.bfloat16
HIGHEST = lax.Precision.HIGHEST


def vmem_call(body, out_shapes, *operands, scalars=0):
    in_vmem = pl.BlockSpec(memory_space=pltpu.VMEM)
    in_smem = pl.BlockSpec(memory_space=pltpu.SMEM)
    return pl.pallas_call(
        body,
        out_shape=out_shapes,
        in_specs=[in_smem] * scalars + [in_vmem] * (len(operands) - scalars),
        out_specs=jax.tree.map(lambda _: in_vmem, out_shapes),
        compiler_params=pltpu.CompilerParams(vmem_limit_bytes=48 << 20),
    )(*operands)


def shape(*dims):
    return jax.ShapeDtypeStruct(dims, F32)


def contract(a, b, dims, precision=None):
    return lax.dot_general(a, b, (dims, ((), ())), precision=precision, preferred_element_type=F32)


PAIRS = (
    (0, 0, 0, 0),
    (0, 0, 0, 1),
    (1, 0, 1, 0),
    (1, 0, 1, 1),
    (2, 0, -2, 0),
    (2, 0, -2, 1),
    (2, 1, -3, 0),
    (2, 1, -3, 1),
)
SELF, BELOW, ABOVE_OWN, ABOVE_BELOW = 0, 2, 4, 6


def mask_body(sub_ref, own, below, above, out):
    sub = sub_ref[0]
    blocks = [own[...], below[...], above[...]]
    both, window = blocks[0].shape
    tiles = both // 2
    lanes = tiles * TILE
    window_at = lax.broadcasted_iota(jnp.int32, (window, lanes), 0)
    tile_of = lax.broadcasted_iota(jnp.int32, (window, lanes), 1) // TILE
    spread = (lax.broadcasted_iota(jnp.int32, (tiles, lanes), 0) == tile_of[:tiles]).astype(F32)
    row_at = lax.broadcasted_iota(jnp.int32, (tiles, window), 0)
    column_at = lax.broadcasted_iota(jnp.int32, (tiles, window), 1)
    for k, (rows, cols, offset, which) in enumerate(PAIRS):
        actual = sub if which == 0 else 1 - sub
        chosen = (window_at == (REACH + offset) * both + actual * tiles + tile_of).astype(F32)
        out[k, :tiles] = contract(blocks[rows][:tiles], chosen, ((1,), (0,)))
        own_columns = (column_at == (REACH - offset) * both + sub * tiles + row_at).astype(F32)
        back = contract(own_columns, blocks[cols][which * tiles : (which + 1) * tiles], ((1,), (1,)))
        out[k, tiles:] = contract(back, spread, ((1,), (0,)))


def squares(piece, features):
    wide = piece[:, :features].astype(F32)
    return jnp.sum(wide * wide, axis=1, keepdims=True)


def as_row(column):
    return jnp.broadcast_to(column, (column.shape[0], TILE)).T[:1]


def products(inverse, piece, tile, columns, back):
    size, width = piece.shape
    features = width - TILE
    row_sq = squares(piece, features)
    doubled = piece[:, :features] * 2
    panel_t = piece[:, features:].astype(F32).T.astype(BF16)
    image = None
    for k, (other, col_sq, mask_ref, lane) in enumerate(columns):
        count = other.shape[0]
        mask = mask_ref[:, lane : lane + count]
        tiles = mask.shape[0] // 2
        gram2 = contract(doubled, other[:, :features], ((1,), (1,)))
        kernel = jnp.exp(-inverse * jnp.maximum(row_sq + col_sq - gram2, 0.0))

        def masked(first):
            return jnp.concatenate(
                [kernel[i * TILE : (i + 1) * TILE] * mask[first + i : first + i + 1] for i in range(size // TILE)], axis=0
            ).astype(BF16)

        term = contract(masked(tile), other[:, features:], ((1,), (0,)))
        image = term if image is None else image + term
        if back is not None:
            term = contract(panel_t, masked(tiles + tile), ((1,), (0,)))
            back[k] = term if back[k] is None else back[k] + term
    return image


def with_masks(pieces, sq_rows, masks, first):
    per_half = len(pieces) // 2
    return [
        (p[...], sq, masks.at[first + k // per_half], (k % per_half) * p.shape[0])
        for k, (p, sq) in enumerate(zip(pieces, sq_rows))
    ]


def self_body(inverse, masks, o0, o1, x0, x1, image, sq):
    pieces = (o0, o1, x0, x1)
    size, width = o0.shape
    rows = [as_row(squares(p[...], width - TILE)) for p in pieces]
    for k, row in enumerate(rows):
        sq[k : k + 1] = row
    columns = with_masks(pieces, rows, masks, SELF)
    for k, piece in enumerate((o0, o1)):
        image[k * size : (k + 1) * size] = products(inverse[0], piece[...], k * size // TILE, columns, None)


def below_body(part, inverse, masks, sq, x, o0, o1, x0, x1, *refs):
    pieces = (o0, o1, x0, x1)
    back = [r[...] for r in refs[: len(refs) - 5]] or [None] * 4
    outs = refs[-5:]
    columns = with_masks(pieces, [sq[k : k + 1] for k in range(4)], masks, BELOW)
    outs[0][...] = products(inverse[0], x[...], part * x.shape[0] // TILE, columns, back)
    for out, value in zip(outs[1:], back):
        out[...] = value


def above_first_body(inverse, masks, sq, x, o0, o1, x0, x1, b0, b1, y0, y1, t0, t1, t2, t3, image, below_sq, *outs):
    size, width = x.shape
    below = (b0, b1, y0, y1)
    rows = [as_row(squares(p[...], width - TILE)) for p in below]
    for k, row in enumerate(rows):
        below_sq[k : k + 1] = row
    columns = with_masks((o0, o1, x0, x1), [sq[k : k + 1] for k in range(4)], masks, ABOVE_OWN)
    columns += with_masks(below, rows, masks, ABOVE_BELOW)
    back = [t0[...], t1[...], t2[...], t3[...]] + [None] * 4
    image[...] = products(inverse[0], x[...], 0, columns, back)
    for out, value in zip(outs, back):
        out[...] = value


def above_below_body(inverse, masks, below_sq, x, b0, b1, y0, y1, t0, t1, t2, t3, i0, i1, image, own, cross):
    size = x.shape[0]
    columns = with_masks((b0, b1, y0, y1), [below_sq[k : k + 1] for k in range(4)], masks, ABOVE_BELOW)
    back = [t0[...], t1[...], t2[...], t3[...]]
    image[...] = products(inverse[0], x[...], size // TILE, columns, back)
    own[:size] = i0[...] + back[0].T
    own[size:] = i1[...] + back[1].T
    cross[:size] = back[2].T
    cross[size:] = back[3].T


def above_own_body(inverse, masks, sq, x, o0, o1, x0, x1, t0, t1, t2, t3, self_image, above_image, image, own, cross):
    size = x.shape[0]
    columns = with_masks((o0, o1, x0, x1), [sq[k : k + 1] for k in range(4)], masks, ABOVE_OWN)
    back = [t0[...], t1[...], t2[...], t3[...]]
    image[...] = above_image[...] + products(inverse[0], x[...], size // TILE, columns, back)
    own[:size] = self_image[:size] + back[0].T
    own[size:] = self_image[size:] + back[1].T
    cross[:size] = back[2].T
    cross[size:] = back[3].T


def gram_body(own, cross, below, above0, above1, image, gram):
    total = own[...] + cross[...] + below[...] + jnp.concatenate([above0[...], above1[...]], axis=0)
    image[...] = total
    gram[...] = contract(total, total, ((0,), (0,)), HIGHEST)


GROUP = 8


def full(value):
    return jnp.broadcast_to(value, (GROUP, value.shape[1] if value.shape[1] > 1 else TILE))


def factor(gram, block):
    size = gram.shape[0]
    groups = size // GROUP
    upper = [gram[GROUP * r : GROUP * (r + 1)] for r in range(groups)]
    row = lax.broadcasted_iota(jnp.int32, (GROUP, size), 0)
    col = lax.broadcasted_iota(jnp.int32, (GROUP, size), 1)
    inverse = [jnp.where(col == row + GROUP * r, 1.0, 0.0).astype(F32) for r in range(groups)]
    for b in range(0, groups, block):
        if b:
            done_upper, done_inverse = jnp.concatenate(upper[:b], axis=0), jnp.concatenate(inverse[:b], axis=0)
            coefficients = done_upper[:, GROUP * b : GROUP * (b + block)]
            less_upper = contract(coefficients, done_upper, ((0,), (0,)), HIGHEST)
            less_inverse = contract(coefficients, done_inverse, ((0,), (0,)), HIGHEST)
            for k in range(block):
                upper[b + k] = upper[b + k] - less_upper[GROUP * k : GROUP * (k + 1)]
                inverse[b + k] = inverse[b + k] - less_inverse[GROUP * k : GROUP * (k + 1)]
        for r in range(b, b + block):
            lane = GROUP * r
            columns = [full(upper[r][:, lane + k : lane + k + 1]) for k in range(GROUP)]
            diag = [[full(columns[j][i : i + 1]) for j in range(i + 1)] for i in range(GROUP)]
            lower = [[None] * GROUP for _ in range(GROUP)]
            scale = [None] * GROUP
            for i in range(GROUP):
                scale[i] = lax.rsqrt(diag[i][i])
                for k in range(i + 1, GROUP):
                    lower[k][i] = diag[k][i] * scale[i]
                for k in range(i + 1, GROUP):
                    for j in range(i + 1, k + 1):
                        diag[k][j] = diag[k][j] - lower[k][i] * lower[j][i]
            u = [full(upper[r][i : i + 1]) for i in range(GROUP)]
            v = [full(inverse[r][i : i + 1]) for i in range(GROUP)]
            for i in range(GROUP):
                u[i], v[i] = u[i] * scale[i], v[i] * scale[i]
                for k in range(i + 1, GROUP):
                    u[k], v[k] = u[k] - lower[k][i] * u[i], v[k] - lower[k][i] * v[i]
            upper[r], inverse[r] = u[0], v[0]
            for i in range(1, GROUP):
                upper[r] = jnp.where(row == i, u[i], upper[r])
                inverse[r] = jnp.where(row == i, v[i], inverse[r])
            for later in range(r + 1, b + block):
                left = [full(upper[later][:, lane + k : lane + k + 1]) for k in range(GROUP)]
                for i in range(GROUP):
                    left[i] = left[i] * scale[i]
                    for k in range(i + 1, GROUP):
                        left[k] = left[k] - lower[k][i] * left[i]
                    upper[later] = upper[later] - left[i] * u[i]
                    inverse[later] = inverse[later] - left[i] * v[i]
    at_row = lax.broadcasted_iota(jnp.int32, (size, size), 0)
    at_col = lax.broadcasted_iota(jnp.int32, (size, size), 1)
    return jnp.where(at_col >= at_row, jnp.concatenate(upper, axis=0), 0.0), jnp.concatenate(inverse, axis=0)


def basis_body(image, gram, basis, upper):
    upper[...], inverse = factor(gram[...], 4)
    basis[...] = contract(image[...], inverse, ((1,), (1,)), HIGHEST)


def per_device(embeddings, start_panel, tile_mask, inv_width):
    n_blk = lax.axis_size("blk")
    half, width = start_panel.shape
    tiles = half // TILE
    size = half // 2
    sub_move = lambda v: lax.ppermute(v, "sub", [(0, 1), (1, 0)])
    blk_route = lambda v, to: lax.ppermute(v, "blk", [(i, to(i) % n_blk) for i in range(n_blk)])
    blk_move = lambda v, by: blk_route(v, lambda i: i + by)

    own = [jnp.concatenate([embeddings[i : i + size], start_panel[i : i + size]], axis=1) for i in (0, size)]
    mask = tile_mask.astype(F32)
    own_mask = jnp.concatenate([mask, sub_move(mask)], axis=0)
    if n_blk == 8:
        swapped = blk_route(own[1], lambda i: i ^ 1)
        below = [blk_move(own[0], 1), blk_route(swapped, lambda i: i if i & 1 else i + 2)]
    else:
        below = [blk_move(own[0], 1), blk_move(own[1], 1)]
    above = [blk_move(own[0], -2), blk_move(own[1], -2)]
    other = [sub_move(own[0]), sub_move(own[1])]
    below_mask, above_mask = blk_move(own_mask, 1), blk_move(own_mask, -2)
    sub = lax.axis_index("sub").astype(jnp.int32).reshape(1)
    masks = vmem_call(mask_body, shape(len(PAIRS), 2 * tiles, half), sub, own_mask, below_mask, above_mask, scalars=1)

    image = shape(size, width)
    turned = (shape(width, size),) * 4
    sq_rows = shape(4, size)
    block = own + other
    self_image, sq = vmem_call(self_body, (shape(half, width), sq_rows), inv_width, masks, *block, scalars=1)
    below_image, back = [], []
    for part in range(2):
        out, *back = vmem_call(
            functools.partial(below_body, part), (image, *turned), inv_width, masks, sq, below[part], *block, *back, scalars=1
        )
        below_image.append(out)
    below += [sub_move(below[0]), sub_move(below[1])]
    above_image0, below_sq, *back = vmem_call(
        above_first_body, (image, sq_rows, *turned, *turned), inv_width, masks, sq, above[0], *block, *below, *back, scalars=1
    )
    above_image0 = blk_move(above_image0, 2)
    above_image1, below_image, below_cross = vmem_call(
        above_below_body,
        (image, shape(half, width), shape(half, width)),
        inv_width,
        masks,
        below_sq,
        above[1],
        *below,
        *back[4:],
        *below_image,
        scalars=1,
    )
    below_image = blk_move(below_image + sub_move(below_cross), -1)
    above_image1, own_image, own_cross = vmem_call(
        above_own_body,
        (image, shape(half, width), shape(half, width)),
        inv_width,
        masks,
        sq,
        above[1],
        *block,
        *back[:4],
        self_image,
        above_image1,
        scalars=1,
    )
    above_image1 = blk_move(above_image1, 2)
    image, gram = vmem_call(
        gram_body,
        (shape(half, width), shape(width, width)),
        own_image,
        sub_move(own_cross),
        below_image,
        above_image0,
        above_image1,
    )
    if n_blk & (n_blk - 1):
        gram = lax.psum(gram, ("blk", "sub"))
    else:
        gram = gram + sub_move(gram)
        hop = 1
        while hop < n_blk:
            gram = gram + blk_route(gram, lambda i: i ^ hop)
            hop *= 2
    return vmem_call(basis_body, (shape(half, width), shape(width, width)), image, gram)


def solution(mesh):
    return jax.shard_map(
        per_device,
        mesh=mesh,
        in_specs=(
            P(("groups", "blk", "sub"), None),
            P(("groups", "blk", "sub"), None),
            P(("groups", "blk", "sub"), None),
            P(),
        ),
        out_specs=(P(("groups", "blk", "sub"), None), P("groups", None)),
        check_vma=False,
    )
```

```python
import functools

import jax
import jax.numpy as jnp
from jax import lax
from jax.experimental import pallas as pl
from jax.experimental.pallas import tpu as pltpu
from jax.sharding import PartitionSpec as P

TILE = 128
REACH = 3
F32 = jnp.float32
BF16 = jnp.bfloat16
HIGHEST = lax.Precision.HIGHEST


def vmem_call(body, out_shapes, *operands, scalars=0):
    in_vmem = pl.BlockSpec(memory_space=pltpu.VMEM)
    in_smem = pl.BlockSpec(memory_space=pltpu.SMEM)
    return pl.pallas_call(
        body,
        out_shape=out_shapes,
        in_specs=[in_smem] * scalars + [in_vmem] * (len(operands) - scalars),
        out_specs=jax.tree.map(lambda _: in_vmem, out_shapes),
        compiler_params=pltpu.CompilerParams(vmem_limit_bytes=48 << 20),
    )(*operands)


def shape(*dims):
    return jax.ShapeDtypeStruct(dims, F32)


def contract(a, b, dims, precision=None):
    return lax.dot_general(a, b, (dims, ((), ())), precision=precision, preferred_element_type=F32)


MARK = 8
OWN, BELOW, ABOVE = 0, 1, -2


def pair_mask(sub, rows, cols, offset, which):
    tiles = rows.shape[0]
    padded, lanes = rows.shape[1], tiles * TILE
    tile_of = lax.broadcasted_iota(jnp.int32, (padded, lanes), 1) // TILE
    first = (REACH + offset) * 2 * tiles + (sub if which == 0 else 1 - sub) * tiles
    chosen = (lax.broadcasted_iota(jnp.int32, (padded, lanes), 0) == first + tile_of).astype(F32)
    ahead = contract(rows, chosen, ((1,), (0,)))
    first = (REACH - offset) * 2 * tiles + sub * tiles
    row_at = lax.broadcasted_iota(jnp.int32, (tiles, padded), 0)
    chosen = (lax.broadcasted_iota(jnp.int32, (tiles, padded), 1) == first + row_at).astype(F32)
    spread = (lax.broadcasted_iota(jnp.int32, (tiles, lanes), 0) == tile_of[:tiles]).astype(F32)
    back = contract(contract(chosen, cols, ((1,), (1,))), spread, ((1,), (0,)))
    return jnp.concatenate([ahead, back], axis=0)


def marks(ref, size):
    return ref[size : size + MARK, :TILE].astype(F32)[: 2 * size // TILE]


def pieces(ref):
    size = (ref.shape[0] - MARK) // 2
    return [ref[:size], ref[size + MARK :]]


def squares(piece, features):
    wide = piece[:, :features].astype(F32)
    return jnp.sum(wide * wide, axis=1, keepdims=True)


def as_row(column):
    return jnp.broadcast_to(column, (column.shape[0], TILE)).T[:1]


def square_rows(blocks, out):
    rows = [as_row(squares(p, p.shape[1] - TILE)) for block in blocks for p in pieces(block)]
    for k, row in enumerate(rows):
        out[k : k + 1] = row
    return rows


def read_rows(ref):
    return [ref[k : k + 1] for k in range(ref.shape[0])]


def columns_of(blocks, sq_rows, masks):
    out = []
    for h, block in enumerate(blocks):
        for k, piece in enumerate(pieces(block)):
            size = piece.shape[0]
            out.append((piece, sq_rows[2 * h + k], masks[h][:, k * size : (k + 1) * size]))
    return out


def products(inverse, piece, tile, columns, back):
    size, width = piece.shape
    features = width - TILE
    row_sq = squares(piece, features)
    doubled = piece[:, :features] * 2
    panel_t = piece[:, features:].astype(F32).T.astype(BF16)
    image = None
    for k, (other, col_sq, mask) in enumerate(columns):
        tiles = mask.shape[0] // 2
        gram2 = contract(doubled, other[:, :features], ((1,), (1,)))
        kernel = jnp.exp(-inverse * jnp.maximum(row_sq + col_sq - gram2, 0.0))

        def masked(first):
            return jnp.concatenate(
                [kernel[i * TILE : (i + 1) * TILE] * mask[first + i : first + i + 1] for i in range(size // TILE)], axis=0
            ).astype(BF16)

        term = contract(masked(tile), other[:, features:], ((1,), (0,)))
        image = term if image is None else image + term
        if back is not None:
            term = contract(panel_t, masked(tiles + tile), ((1,), (0,)))
            back[k] = term if back[k] is None else back[k] + term
    return image


def store_all(outs, values):
    for out, value in zip(outs, values):
        out[...] = value


def self_body(inverse, sub, own, other, image, sq):
    rows = square_rows((own, other), sq)
    size = rows[0].shape[1]
    masks = [pair_mask(sub[0], marks(own, size), marks(r, size), OWN, h) for h, r in enumerate((own, other))]
    columns = columns_of((own, other), rows, masks)
    for k, piece in enumerate(pieces(own)):
        image[k * size : (k + 1) * size] = products(inverse[0], piece, k * size // TILE, columns, None)


def below_first_body(inverse, sub, sq, x, own, other, image, masks_out, *outs):
    size = x.shape[0] - MARK
    masks = [pair_mask(sub[0], marks(x, size), marks(r, size), BELOW, h) for h, r in enumerate((own, other))]
    back = [None] * 4
    image[...] = products(inverse[0], x[:size], 0, columns_of((own, other), read_rows(sq), masks), back)
    store_all_at(masks_out, masks)
    store_all(outs, back)


def store_all_at(ref, values):
    for k, value in enumerate(values):
        ref[k] = value


def below_last_body(inverse, masks, sq, x, own, other, t0, t1, t2, t3, image, *outs):
    back = [t0[...], t1[...], t2[...], t3[...]]
    columns = columns_of((own, other), read_rows(sq), [masks[0], masks[1]])
    image[...] = products(inverse[0], x[...], x.shape[0] // TILE, columns, back)
    store_all(outs, back)


def above_first_body(inverse, sub, sq, x, own, other, below, below_other, t0, t1, t2, t3, image, below_sq, masks_out, *outs):
    rows = square_rows((below, below_other), below_sq)
    size = x.shape[0] - MARK
    mine = marks(x, size)
    masks = [pair_mask(sub[0], mine, marks(r, size), ABOVE, h) for h, r in enumerate((own, other))]
    masks += [pair_mask(sub[0], mine, marks(r, size), ABOVE - BELOW, h) for h, r in enumerate((below, below_other))]
    columns = columns_of((own, other), read_rows(sq), masks[:2]) + columns_of((below, below_other), rows, masks[2:])
    back = [t0[...], t1[...], t2[...], t3[...]] + [None] * 4
    image[...] = products(inverse[0], x[:size], 0, columns, back)
    store_all_at(masks_out, masks)
    store_all(outs, back)


def above_last(inverse, sq, x, blocks, masks, sums, own, cross, images):
    size = x.shape[0]
    back = [t[...] for t in sums]
    image = products(inverse, x[...], size // TILE, columns_of(blocks, read_rows(sq), masks), back)
    own[:size] = images[0] + back[0].T
    own[size:] = images[1] + back[1].T
    cross[:size] = back[2].T
    cross[size:] = back[3].T
    return image


def above_below_body(inverse, masks, below_sq, x, below, below_other, t0, t1, t2, t3, i0, i1, image, own, cross):
    image[...] = above_last(
        inverse[0], below_sq, x, (below, below_other), [masks[2], masks[3]], (t0, t1, t2, t3), own, cross, (i0[...], i1[...])
    )


def above_own_body(inverse, masks, sq, x, own_block, other, t0, t1, t2, t3, self_image, above_image, image, own, cross):
    size = x.shape[0]
    image[...] = above_image[...] + above_last(
        inverse[0], sq, x, (own_block, other), [masks[0], masks[1]], (t0, t1, t2, t3), own, cross,
        (self_image[:size], self_image[size:]),
    )


def gram_body(own, cross, below, above0, above1, image, gram):
    total = own[...] + cross[...] + below[...] + jnp.concatenate([above0[...], above1[...]], axis=0)
    image[...] = total
    gram[...] = contract(total, total, ((0,), (0,)), HIGHEST)


GROUP = 8


def full(value):
    return jnp.broadcast_to(value, (GROUP, value.shape[1] if value.shape[1] > 1 else TILE))


def factor(gram, block):
    size = gram.shape[0]
    groups = size // GROUP
    upper = [gram[GROUP * r : GROUP * (r + 1)] for r in range(groups)]
    row = lax.broadcasted_iota(jnp.int32, (GROUP, size), 0)
    col = lax.broadcasted_iota(jnp.int32, (GROUP, size), 1)
    inverse = [jnp.where(col == row + GROUP * r, 1.0, 0.0).astype(F32) for r in range(groups)]
    for b in range(0, groups, block):
        if b:
            done_upper, done_inverse = jnp.concatenate(upper[:b], axis=0), jnp.concatenate(inverse[:b], axis=0)
            coefficients = done_upper[:, GROUP * b : GROUP * (b + block)]
            less_upper = contract(coefficients, done_upper, ((0,), (0,)), HIGHEST)
            less_inverse = contract(coefficients, done_inverse, ((0,), (0,)), HIGHEST)
            for k in range(block):
                upper[b + k] = upper[b + k] - less_upper[GROUP * k : GROUP * (k + 1)]
                inverse[b + k] = inverse[b + k] - less_inverse[GROUP * k : GROUP * (k + 1)]
        for r in range(b, b + block):
            lane = GROUP * r
            columns = [full(upper[r][:, lane + k : lane + k + 1]) for k in range(GROUP)]
            diag = [[full(columns[j][i : i + 1]) for j in range(i + 1)] for i in range(GROUP)]
            lower = [[None] * GROUP for _ in range(GROUP)]
            scale = [None] * GROUP
            for i in range(GROUP):
                scale[i] = lax.rsqrt(diag[i][i])
                for k in range(i + 1, GROUP):
                    lower[k][i] = diag[k][i] * scale[i]
                for k in range(i + 1, GROUP):
                    for j in range(i + 1, k + 1):
                        diag[k][j] = diag[k][j] - lower[k][i] * lower[j][i]
            u = [full(upper[r][i : i + 1]) for i in range(GROUP)]
            v = [full(inverse[r][i : i + 1]) for i in range(GROUP)]
            for i in range(GROUP):
                u[i], v[i] = u[i] * scale[i], v[i] * scale[i]
                for k in range(i + 1, GROUP):
                    u[k], v[k] = u[k] - lower[k][i] * u[i], v[k] - lower[k][i] * v[i]
            upper[r], inverse[r] = u[0], v[0]
            for i in range(1, GROUP):
                upper[r] = jnp.where(row == i, u[i], upper[r])
                inverse[r] = jnp.where(row == i, v[i], inverse[r])
            for later in range(r + 1, b + block):
                left = [full(upper[later][:, lane + k : lane + k + 1]) for k in range(GROUP)]
                for i in range(GROUP):
                    left[i] = left[i] * scale[i]
                    for k in range(i + 1, GROUP):
                        left[k] = left[k] - lower[k][i] * left[i]
                    upper[later] = upper[later] - left[i] * u[i]
                    inverse[later] = inverse[later] - left[i] * v[i]
    at_row = lax.broadcasted_iota(jnp.int32, (size, size), 0)
    at_col = lax.broadcasted_iota(jnp.int32, (size, size), 1)
    return jnp.where(at_col >= at_row, jnp.concatenate(upper, axis=0), 0.0), jnp.concatenate(inverse, axis=0)


def basis_body(image, gram, basis, upper):
    upper[...], inverse = factor(gram[...], 4)
    basis[...] = contract(image[...], inverse, ((1,), (1,)), HIGHEST)


def per_device(embeddings, start_panel, tile_mask, inv_width):
    n_blk = lax.axis_size("blk")
    half, width = start_panel.shape
    tiles = half // TILE
    size = half // 2
    sub_move = lambda v: lax.ppermute(v, "sub", [(0, 1), (1, 0)])
    blk_route = lambda v, to: lax.ppermute(v, "blk", [(i, to(i) % n_blk) for i in range(n_blk)])
    blk_move = lambda v, by: blk_route(v, lambda i: i + by)

    mark = jnp.pad(tile_mask.astype(BF16), ((0, MARK - tiles), (0, embeddings.shape[1] + width - tile_mask.shape[1])))
    pack = lambda rows: jnp.concatenate([embeddings[rows], start_panel[rows]], axis=1)
    first, last = jnp.concatenate([pack(slice(0, size)), mark], axis=0), pack(slice(size, half))
    own = jnp.concatenate([first, last], axis=0)
    after = lambda v, *earlier: lax.optimization_barrier((v, *earlier))[0]
    sub = lax.axis_index("sub").astype(jnp.int32).reshape(1)
    relayed = n_blk == 8
    swapped = blk_route(last, lambda i: i ^ 1) if relayed else last
    above0 = blk_move(first, -2)
    other = sub_move(own)
    image = shape(size, width)
    turned = (shape(width, size),) * 4
    sq_rows = shape(4, size)
    mask_of = lambda count: shape(count, 2 * tiles, half)
    self_image, sq = vmem_call(self_body, (shape(half, width), sq_rows), inv_width, sub, own, other, scalars=2)
    below0 = blk_move(after(first, swapped, above0, self_image), 1)
    swapped = after(swapped, above0, self_image)
    below1 = blk_route(swapped, lambda i: i if i & 1 else i + 2) if relayed else blk_move(swapped, 1)
    below = jnp.concatenate([below0, below1], axis=0)
    below_other = sub_move(below)
    above1 = blk_move(after(last, below0, below1), -2)
    below_image0, masks, *back = vmem_call(
        below_first_body,
        (image, mask_of(2), *turned),
        inv_width,
        sub,
        sq,
        after(below0, below_other),
        own,
        other,
        scalars=2,
    )
    below_image1, *back = vmem_call(
        below_last_body, (image, *turned), inv_width, masks, sq, below1, own, other, *back, scalars=1
    )
    above_image0, below_sq, masks, *back = vmem_call(
        above_first_body,
        (image, sq_rows, mask_of(4), *turned, *turned),
        inv_width,
        sub,
        sq,
        above0,
        own,
        other,
        below,
        below_other,
        *back,
        scalars=2,
    )
    above_image0 = blk_move(above_image0, 2)
    above_image1, below_image, below_cross = vmem_call(
        above_below_body,
        (image, shape(half, width), shape(half, width)),
        inv_width,
        masks,
        below_sq,
        after(above1, above_image0),
        below,
        below_other,
        *back[4:],
        below_image0,
        below_image1,
        scalars=1,
    )
    below_image = blk_move(below_image + sub_move(below_cross), -1)
    above_image1, own_image, own_cross = vmem_call(
        above_own_body,
        (image, shape(half, width), shape(half, width)),
        inv_width,
        masks,
        sq,
        above1,
        own,
        other,
        *back[:4],
        self_image,
        above_image1,
        scalars=1,
    )
    above_image1 = blk_move(above_image1, 2)
    image, gram = vmem_call(
        gram_body,
        (shape(half, width), shape(width, width)),
        own_image,
        sub_move(own_cross),
        below_image,
        above_image0,
        above_image1,
    )
    if n_blk & (n_blk - 1):
        gram = lax.psum(gram, ("blk", "sub"))
    else:
        gram = gram + sub_move(gram)
        hop = 1
        while hop < n_blk:
            gram = gram + blk_route(gram, lambda i: i ^ hop)
            hop *= 2
    return vmem_call(basis_body, (shape(half, width), shape(width, width)), image, gram)


def solution(mesh):
    return jax.shard_map(
        per_device,
        mesh=mesh,
        in_specs=(
            P(("groups", "blk", "sub"), None),
            P(("groups", "blk", "sub"), None),
            P(("groups", "blk", "sub"), None),
            P(),
        ),
        out_specs=(P(("groups", "blk", "sub"), None), P("groups", None)),
        check_vma=False,
    )
```

```python
import jax
import jax.numpy as jnp
from jax import lax
from jax.experimental import pallas as pl
from jax.experimental.pallas import tpu as pltpu
from jax.sharding import PartitionSpec as P

TILE = 128
REACH = 3
F32 = jnp.float32
BF16 = jnp.bfloat16
HIGHEST = lax.Precision.HIGHEST


def vmem_call(body, out_shapes, *operands, scalars=0):
    in_vmem = pl.BlockSpec(memory_space=pltpu.VMEM)
    in_smem = pl.BlockSpec(memory_space=pltpu.SMEM)
    return pl.pallas_call(
        body,
        out_shape=out_shapes,
        in_specs=[in_smem] * scalars + [in_vmem] * (len(operands) - scalars),
        out_specs=jax.tree.map(lambda _: in_vmem, out_shapes),
        compiler_params=pltpu.CompilerParams(vmem_limit_bytes=48 << 20),
    )(*operands)


def shape(*dims):
    return jax.ShapeDtypeStruct(dims, F32)


def contract(a, b, dims, precision=None):
    return lax.dot_general(a, b, (dims, ((), ())), precision=precision, preferred_element_type=F32)


MARK = 8
OWN, BELOW, ABOVE = 0, 1, -2


def pair_mask(sub, rows, cols, offset, which):
    tiles = rows.shape[0]
    padded, lanes = rows.shape[1], tiles * TILE
    tile_of = lax.broadcasted_iota(jnp.int32, (padded, lanes), 1) // TILE
    first = (REACH + offset) * 2 * tiles + (sub if which == 0 else 1 - sub) * tiles
    chosen = (lax.broadcasted_iota(jnp.int32, (padded, lanes), 0) == first + tile_of).astype(F32)
    ahead = contract(rows, chosen, ((1,), (0,)))
    first = (REACH - offset) * 2 * tiles + sub * tiles
    row_at = lax.broadcasted_iota(jnp.int32, (tiles, padded), 0)
    chosen = (lax.broadcasted_iota(jnp.int32, (tiles, padded), 1) == first + row_at).astype(F32)
    spread = (lax.broadcasted_iota(jnp.int32, (tiles, lanes), 0) == tile_of[:tiles]).astype(F32)
    back = contract(contract(chosen, cols, ((1,), (1,))), spread, ((1,), (0,)))
    return jnp.concatenate([ahead, back], axis=0)


def marks(ref, size):
    return ref[size : size + MARK, :TILE].astype(F32)[: 2 * size // TILE]


def pieces(ref):
    size = (ref.shape[0] - MARK) // 2
    return [ref[:size], ref[size + MARK :]]


def squares(piece, features):
    wide = piece[:, :features].astype(F32)
    return jnp.sum(wide * wide, axis=1, keepdims=True)


def as_row(column):
    return jnp.broadcast_to(column, (column.shape[0], TILE)).T[:1]


def square_rows(blocks, out):
    rows = [as_row(squares(p, p.shape[1] - TILE)) for block in blocks for p in pieces(block)]
    for k, row in enumerate(rows):
        out[k : k + 1] = row
    return rows


def read_rows(ref):
    return [ref[k : k + 1] for k in range(ref.shape[0])]


def columns_of(blocks, sq_rows, masks):
    out = []
    for h, block in enumerate(blocks):
        for k, piece in enumerate(pieces(block)):
            size = piece.shape[0]
            out.append((piece, sq_rows[2 * h + k], masks[h][:, k * size : (k + 1) * size]))
    return out


def products(inverse, piece, tile, columns, back):
    size, width = piece.shape
    features = width - TILE
    row_sq = squares(piece, features)
    doubled = piece[:, :features] * 2
    panel_t = piece[:, features:].astype(F32).T.astype(BF16)
    image = None
    for k, (other, col_sq, mask) in enumerate(columns):
        tiles = mask.shape[0] // 2
        gram2 = contract(doubled, other[:, :features], ((1,), (1,)))
        kernel = jnp.exp(-inverse * jnp.maximum(row_sq + col_sq - gram2, 0.0))

        def masked(first):
            return jnp.concatenate(
                [kernel[i * TILE : (i + 1) * TILE] * mask[first + i : first + i + 1] for i in range(size // TILE)], axis=0
            ).astype(BF16)

        term = contract(masked(tile), other[:, features:], ((1,), (0,)))
        image = term if image is None else image + term
        if back is not None:
            term = contract(panel_t, masked(tiles + tile), ((1,), (0,)))
            back[k] = term if back[k] is None else back[k] + term
    return image


def store_all(outs, values):
    for out, value in zip(outs, values):
        out[...] = value


def pack_body(embeddings, panel, tile_mask, own, first, last):
    half, features = embeddings.shape
    size = half // 2
    tiles, window = tile_mask.shape
    at = lax.broadcasted_iota(jnp.int32, (window, TILE), 0) == lax.broadcasted_iota(jnp.int32, (window, TILE), 1)
    mask = contract(tile_mask[...].astype(F32), at.astype(F32), ((1,), (0,)))
    mask = jnp.concatenate([mask, jnp.zeros((MARK - tiles, TILE), F32)], axis=0).astype(BF16)
    for ref in (own, first):
        ref[:size, :features] = embeddings[:size]
        ref[:size, features:] = panel[:size]
        ref[size : size + MARK, :TILE] = mask
        ref[size : size + MARK, TILE:] = jnp.zeros((MARK, features), BF16)
    for ref, start in ((own, size + MARK), (last, 0)):
        ref[start : start + size, :features] = embeddings[size:]
        ref[start : start + size, features:] = panel[size:]


def masks_of(sub, ref, others, offset):
    size = (ref.shape[0] - MARK) // 2
    mine = marks(ref, size)
    return [pair_mask(sub, mine, marks(r, size), offset, h) for h, r in enumerate(others)]


def block_products(inverse, block, columns, back):
    out = []
    for piece in pieces(block):
        out.append(products(inverse, piece, len(out) * piece.shape[0] // TILE, columns, back))
    return out


def self_body(inverse, sub, own, other, image, sq):
    rows = square_rows((own, other), sq)
    columns = columns_of((own, other), rows, masks_of(sub[0], own, (own, other), OWN))
    image[...] = jnp.concatenate(block_products(inverse[0], own, columns, None), axis=0)


def above_own_body(inverse, sub, sq, above, own, other, image, *sums):
    columns = columns_of((own, other), read_rows(sq), masks_of(sub[0], above, (own, other), ABOVE))
    back = [None] * 4
    image[...] = jnp.concatenate(block_products(inverse[0], above, columns, back), axis=0)
    store_all(sums, back)


def split_back(back, own_rows, own, cross):
    size = back[0].shape[1]
    for k in range(2):
        own[k * size : (k + 1) * size] = own_rows[k] + back[k].T
        cross[k * size : (k + 1) * size] = back[2 + k].T


def below_own_body(inverse, sub, sq, below, own, other, self_image, t0, t1, t2, t3, image, own_image, cross):
    columns = columns_of((own, other), read_rows(sq), masks_of(sub[0], below, (own, other), BELOW))
    back = [t0[...], t1[...], t2[...], t3[...]]
    image[...] = jnp.concatenate(block_products(inverse[0], below, columns, back), axis=0)
    size = back[0].shape[1]
    split_back(back, (self_image[:size], self_image[size:]), own_image, cross)


def above_below_body(inverse, sub, above, below, other, above_image, below_image, image, below_out, cross):
    rows = [as_row(squares(p, p.shape[1] - TILE)) for block in (below, other) for p in pieces(block)]
    columns = columns_of((below, other), rows, masks_of(sub[0], above, (below, other), ABOVE - BELOW))
    back = [None] * 4
    image[...] = above_image[...] + jnp.concatenate(block_products(inverse[0], above, columns, back), axis=0)
    size = back[0].shape[1]
    split_back(back, (below_image[:size], below_image[size:]), below_out, cross)


def gram_body(own, cross, below, above, image, gram):
    total = own[...] + cross[...] + below[...] + above[...]
    image[...] = total
    gram[...] = contract(total, total, ((0,), (0,)), HIGHEST)


GROUP = 8


def full(value):
    return jnp.broadcast_to(value, (GROUP, value.shape[1] if value.shape[1] > 1 else TILE))


def factor(gram, block):
    size = gram.shape[0]
    groups = size // GROUP
    upper = [gram[GROUP * r : GROUP * (r + 1)] for r in range(groups)]
    row = lax.broadcasted_iota(jnp.int32, (GROUP, size), 0)
    col = lax.broadcasted_iota(jnp.int32, (GROUP, size), 1)
    inverse = [jnp.where(col == row + GROUP * r, 1.0, 0.0).astype(F32) for r in range(groups)]
    for b in range(0, groups, block):
        if b:
            done_upper, done_inverse = jnp.concatenate(upper[:b], axis=0), jnp.concatenate(inverse[:b], axis=0)
            coefficients = done_upper[:, GROUP * b : GROUP * (b + block)]
            less_upper = contract(coefficients, done_upper, ((0,), (0,)), HIGHEST)
            less_inverse = contract(coefficients, done_inverse, ((0,), (0,)), HIGHEST)
            for k in range(block):
                upper[b + k] = upper[b + k] - less_upper[GROUP * k : GROUP * (k + 1)]
                inverse[b + k] = inverse[b + k] - less_inverse[GROUP * k : GROUP * (k + 1)]
        for r in range(b, b + block):
            lane = GROUP * r
            columns = [full(upper[r][:, lane + k : lane + k + 1]) for k in range(GROUP)]
            diag = [[full(columns[j][i : i + 1]) for j in range(i + 1)] for i in range(GROUP)]
            lower = [[None] * GROUP for _ in range(GROUP)]
            scale = [None] * GROUP
            for i in range(GROUP):
                scale[i] = lax.rsqrt(diag[i][i])
                for k in range(i + 1, GROUP):
                    lower[k][i] = diag[k][i] * scale[i]
                for k in range(i + 1, GROUP):
                    for j in range(i + 1, k + 1):
                        diag[k][j] = diag[k][j] - lower[k][i] * lower[j][i]
            u = [full(upper[r][i : i + 1]) for i in range(GROUP)]
            v = [full(inverse[r][i : i + 1]) for i in range(GROUP)]
            for i in range(GROUP):
                u[i], v[i] = u[i] * scale[i], v[i] * scale[i]
                for k in range(i + 1, GROUP):
                    u[k], v[k] = u[k] - lower[k][i] * u[i], v[k] - lower[k][i] * v[i]
            upper[r], inverse[r] = u[0], v[0]
            for i in range(1, GROUP):
                upper[r] = jnp.where(row == i, u[i], upper[r])
                inverse[r] = jnp.where(row == i, v[i], inverse[r])
            for later in range(r + 1, b + block):
                left = [full(upper[later][:, lane + k : lane + k + 1]) for k in range(GROUP)]
                for i in range(GROUP):
                    left[i] = left[i] * scale[i]
                    for k in range(i + 1, GROUP):
                        left[k] = left[k] - lower[k][i] * left[i]
                    upper[later] = upper[later] - left[i] * u[i]
                    inverse[later] = inverse[later] - left[i] * v[i]
    at_row = lax.broadcasted_iota(jnp.int32, (size, size), 0)
    at_col = lax.broadcasted_iota(jnp.int32, (size, size), 1)
    return jnp.where(at_col >= at_row, jnp.concatenate(upper, axis=0), 0.0), jnp.concatenate(inverse, axis=0)


def basis_body(image, gram, basis, upper):
    upper[...], inverse = factor(gram[...], 4)
    basis[...] = contract(image[...], inverse, ((1,), (1,)), HIGHEST)


def per_device(embeddings, start_panel, tile_mask, inv_width):
    n_blk = lax.axis_size("blk")
    half, width = start_panel.shape
    size = half // 2
    sub_move = lambda v: lax.ppermute(v, "sub", [(0, 1), (1, 0)])
    blk_route = lambda v, to: lax.ppermute(v, "blk", [(i, to(i) % n_blk) for i in range(n_blk)])
    blk_move = lambda v, by: blk_route(v, lambda i: i + by)

    after = lambda v, *earlier: lax.optimization_barrier((v, *earlier))[0]
    sub = lax.axis_index("sub").astype(jnp.int32).reshape(1)
    wide = embeddings.shape[1] + width
    packed = lambda rows: jax.ShapeDtypeStruct((rows, wide), BF16)
    own, first, last = vmem_call(
        pack_body, (packed(half + MARK), packed(size + MARK), packed(size)), embeddings, start_panel, tile_mask
    )
    relayed = n_blk == 8
    swapped = blk_route(last, lambda i: i ^ 1) if relayed else last
    above = blk_move(own, -2)
    other = sub_move(own)
    image = shape(half, width)
    sq_rows = shape(4, size)
    self_image, sq = vmem_call(self_body, (image, sq_rows), inv_width, sub, own, other, scalars=2)
    first, swapped = after(first, swapped, above, self_image), after(swapped, above, self_image)
    below = [blk_move(first, 1), blk_route(swapped, lambda i: i if i & 1 else i + 2) if relayed else blk_move(swapped, 1)]
    above_image, *back = vmem_call(
        above_own_body, (image, *(shape(width, size),) * 4), inv_width, sub, sq, above, own, other, scalars=2
    )
    below = after(jnp.concatenate(below, axis=0), above_image)
    below_other = sub_move(below)
    below_image, own_image, own_cross = vmem_call(
        below_own_body, (image,) * 3, inv_width, sub, sq, below, own, other, self_image, *back, scalars=2
    )
    above_image, below_image, below_cross = vmem_call(
        above_below_body, (image,) * 3, inv_width, sub, above, below, below_other, above_image, below_image, scalars=2
    )
    above_image = blk_move(above_image, 2)
    below_image = blk_move(below_image + sub_move(below_cross), -1)
    image, gram = vmem_call(
        gram_body, (image, shape(width, width)), own_image, sub_move(own_cross), below_image, above_image
    )
    if n_blk & (n_blk - 1):
        gram = lax.psum(gram, ("blk", "sub"))
    else:
        gram = gram + sub_move(gram)
        hop = 1
        while hop < n_blk:
            gram = gram + blk_route(gram, lambda i: i ^ hop)
            hop *= 2
    return vmem_call(basis_body, (shape(half, width), shape(width, width)), image, gram)


def solution(mesh):
    return jax.shard_map(
        per_device,
        mesh=mesh,
        in_specs=(
            P(("groups", "blk", "sub"), None),
            P(("groups", "blk", "sub"), None),
            P(("groups", "blk", "sub"), None),
            P(),
        ),
        out_specs=(P(("groups", "blk", "sub"), None), P("groups", None)),
        check_vma=False,
    )
```

```python
import jax
import jax.numpy as jnp
from jax import lax
from jax.experimental import pallas as pl
from jax.experimental.pallas import tpu as pltpu
from jax.sharding import PartitionSpec as P

TILE = 128
REACH = 3
F32 = jnp.float32
BF16 = jnp.bfloat16
HIGHEST = lax.Precision.HIGHEST


def vmem_call(body, out_shapes, *operands, scalars=0, in_hbm=0, scratch=()):
    in_vmem = pl.BlockSpec(memory_space=pltpu.VMEM)
    lead = [pl.BlockSpec(memory_space=pltpu.SMEM)] * scalars + [pl.BlockSpec(memory_space=pltpu.HBM)] * in_hbm
    return pl.pallas_call(
        body,
        out_shape=out_shapes,
        in_specs=lead + [in_vmem] * (len(operands) - len(lead)),
        out_specs=jax.tree.map(lambda _: in_vmem, out_shapes),
        scratch_shapes=scratch,
        compiler_params=pltpu.CompilerParams(vmem_limit_bytes=48 << 20),
        cost_estimate=pl.CostEstimate(flops=10**11, transcendentals=0, bytes_accessed=0),
    )(*operands)


def shape(*dims):
    return jax.ShapeDtypeStruct(dims, F32)


def contract(a, b, dims, precision=None):
    return lax.dot_general(a, b, (dims, ((), ())), precision=precision, preferred_element_type=F32)


MARK = 8
OWN, BELOW, ABOVE = 0, 1, -2


def pair_mask(sub, rows, cols, offset, which):
    tiles = rows.shape[0]
    padded, lanes = rows.shape[1], tiles * TILE
    tile_of = lax.broadcasted_iota(jnp.int32, (padded, lanes), 1) // TILE
    first = (REACH + offset) * 2 * tiles + (sub if which == 0 else 1 - sub) * tiles
    chosen = (lax.broadcasted_iota(jnp.int32, (padded, lanes), 0) == first + tile_of).astype(F32)
    ahead = contract(rows, chosen, ((1,), (0,)))
    first = (REACH - offset) * 2 * tiles + sub * tiles
    row_at = lax.broadcasted_iota(jnp.int32, (tiles, padded), 0)
    chosen = (lax.broadcasted_iota(jnp.int32, (tiles, padded), 1) == first + row_at).astype(F32)
    spread = (lax.broadcasted_iota(jnp.int32, (tiles, lanes), 0) == tile_of[:tiles]).astype(F32)
    back = contract(contract(chosen, cols, ((1,), (1,))), spread, ((1,), (0,)))
    return jnp.concatenate([ahead, back], axis=0)


def marks(ref, at, half):
    return ref[at : at + MARK, :TILE].astype(F32)[: half // TILE]


def pieces(*refs, count, size):
    out = []
    for k in range(count):
        rows = slice(k * size, (k + 1) * size)
        if len(refs) == 2:
            out.append((refs[0][rows], refs[1][rows]))
        else:
            features = refs[0].shape[1] - TILE
            out.append((refs[0][rows, :features], refs[0][rows, features:]))
    return out


def squares(features):
    wide = features.astype(F32)
    return jnp.sum(wide * wide, axis=1, keepdims=True)


def as_row(column):
    return jnp.broadcast_to(column, (column.shape[0], TILE)).T[:1]


def read_rows(ref):
    return [ref[k : k + 1] for k in range(ref.shape[0])]


def columns_of(all_pieces, sq_rows, masks, first=0):
    count = len(all_pieces) // 2
    out = []
    for k, (features, panel) in enumerate(all_pieces):
        size = features.shape[0]
        at = (first + k % count) * size
        out.append((features, panel, sq_rows[k], masks[k // count][:, at : at + size]))
    return out


def products(inverse, piece, tile, columns, back):
    features, panel = piece
    size = features.shape[0]
    row_sq = squares(features)
    doubled = features * 2
    panel_t = panel.astype(F32).T.astype(BF16)
    image = None
    for k, (other, other_panel, col_sq, mask) in enumerate(columns):
        tiles = mask.shape[0] // 2
        gram2 = contract(doubled, other, ((1,), (1,)))
        kernel = jnp.exp(-inverse * jnp.maximum(row_sq + col_sq - gram2, 0.0))

        def masked(first):
            return jnp.concatenate(
                [kernel[i * TILE : (i + 1) * TILE] * mask[first + i : first + i + 1] for i in range(size // TILE)], axis=0
            ).astype(BF16)

        term = contract(masked(tile), other_panel, ((1,), (0,)))
        image = term if image is None else image + term
        if back is not None:
            term = contract(panel_t, masked(tiles + tile), ((1,), (0,)))
            back[k] = term if back[k] is None else back[k] + term
    return image


def piece_images(inverse, rows, columns, back):
    images = [products(inverse, piece, k * piece[0].shape[0] // TILE, columns, back) for k, piece in enumerate(rows)]
    return jnp.concatenate(images, axis=0)


def store_all(outs, values):
    for out, value in zip(outs, values):
        out[...] = value


def pack_body(embeddings, panel, tile_mask, own, first, last, panel_mark, mask_here, done):
    half, features = embeddings.shape
    size = half // 2
    tiles, window = tile_mask.shape
    moves = [(tile_mask, mask_here), (panel, panel_mark.at[:half])]
    for ref, start, stop in ((own, 0, half), (first, 0, size), (last, size, half)):
        rows = ref.at[: stop - start]
        moves.append((embeddings.at[start:stop], rows.at[:, :features]))
        moves.append((panel.at[start:stop], rows.at[:, features:]))
    copies = [pltpu.make_async_copy(a, b, done.at[k]) for k, (a, b) in enumerate(moves)]
    for copy in copies:
        copy.start()
    for copy in copies:
        copy.wait()
    at = lax.broadcasted_iota(jnp.int32, (window, TILE), 0) == lax.broadcasted_iota(jnp.int32, (window, TILE), 1)
    mask = contract(mask_here[...].astype(F32), at.astype(F32), ((1,), (0,)))
    mask = jnp.concatenate([mask, jnp.zeros((MARK - tiles, TILE), F32)], axis=0).astype(BF16)
    for ref in (own, first):
        ref[ref.shape[0] - MARK :, :TILE] = mask
        ref[ref.shape[0] - MARK :, TILE:] = jnp.zeros((MARK, features), BF16)
    panel_mark[half:] = mask


def masks_of(sub, rows, others, offset):
    return [pair_mask(sub, rows, r, offset, h) for h, r in enumerate(others)]


def own_pieces(own, other):
    size = own.shape[0] // 2 - MARK // 2
    return [p for ref in (own, other) for p in pieces(ref, count=2, size=size)]


def own_marks(own, other):
    half = own.shape[0] - MARK
    return [marks(ref, half, half) for ref in (own, other)]


def self_body(inverse, sub, own, other, image, sq):
    blocks = own_pieces(own, other)
    rows = [as_row(squares(features)) for features, _ in blocks]
    for k, row in enumerate(rows):
        sq[k : k + 1] = row
    both = own_marks(own, other)
    columns = columns_of(blocks, rows, masks_of(sub[0], both[0], both, OWN))
    image[...] = piece_images(inverse[0], blocks[:2], columns, None)


def above_own_body(inverse, sub, sq, above, above_panel, own, other, image, *sums):
    half = above.shape[0]
    masks = masks_of(sub[0], marks(above_panel, half, half), own_marks(own, other), ABOVE)
    back = [None] * 4
    columns = columns_of(own_pieces(own, other), read_rows(sq), masks)
    image[...] = piece_images(inverse[0], pieces(above, above_panel, count=2, size=half // 2), columns, back)
    store_all(sums, back)


def below_first_body(inverse, sub, sq, below, own, other, t0, t1, t2, t3, image, *sums):
    size = below.shape[0] - MARK
    masks = masks_of(sub[0], marks(below, size, 2 * size), own_marks(own, other), BELOW)
    back = [t0[...], t1[...], t2[...], t3[...]]
    columns = columns_of(own_pieces(own, other), read_rows(sq), masks)
    image[...] = products(inverse[0], pieces(below, count=1, size=size)[0], 0, columns, back)
    store_all(sums, back)


def below_last_body(inverse, sub, sq, marked, below, own, other, self_image, t0, t1, t2, t3, image, own_image, cross):
    size = below.shape[0]
    masks = masks_of(sub[0], marks(marked, 0, 2 * size), own_marks(own, other), BELOW)
    back = [t0[...], t1[...], t2[...], t3[...]]
    columns = columns_of(own_pieces(own, other), read_rows(sq), masks)
    image[...] = products(inverse[0], pieces(below, count=1, size=size)[0], size // TILE, columns, back)
    for k in range(2):
        rows = slice(k * size, (k + 1) * size)
        own_image[rows] = self_image[rows] + back[k].T
        cross[rows] = back[2 + k].T


def above_below(part, inverse, sub, above, above_panel, pair, pair_marks, above_image, image):
    half = above.shape[0]
    size = half // 2
    masks = masks_of(sub[0], marks(above_panel, half, half), pair_marks, ABOVE - BELOW)
    back = [None] * 2
    rows = [as_row(squares(features)) for features, _ in pair]
    columns = columns_of(pair, rows, masks, part)
    image[...] = above_image[...] + piece_images(inverse[0], pieces(above, above_panel, count=2, size=size), columns, back)
    return back[0].T, back[1].T


def above_below_first_body(inverse, sub, above, above_panel, below, other, above_image, below_image, image, below_out, cross, marked):
    size = above.shape[0] // 2
    pair = [pieces(r, count=1, size=size)[0] for r in (below, other)]
    both = [marks(r, size, 2 * size) for r in (below, other)]
    mine, cross[...] = above_below(0, inverse, sub, above, above_panel, pair, both, above_image, image)
    below_out[...] = below_image[...] + mine
    marked[:MARK] = below[size:, :TILE]
    marked[MARK:] = other[size:, :TILE]


def above_below_last_body(inverse, sub, above, above_panel, below, other, marked, above_image, image, below_out, cross):
    size = above.shape[0] // 2
    pair = [pieces(r, count=1, size=size)[0] for r in (below, other)]
    both = [marks(marked, at, 2 * size) for at in (0, MARK)]
    below_out[...], cross[...] = above_below(1, inverse, sub, above, above_panel, pair, both, above_image, image)


def gram_body(own, cross, below0, below1, above, image, gram):
    below = jnp.concatenate([below0[...], below1[...]], axis=0)
    total = own[...] + cross[...] + below + above[...]
    image[...] = total
    gram[...] = contract(total, total, ((0,), (0,)), HIGHEST)


GROUP = 8


def full(value):
    return jnp.broadcast_to(value, (GROUP, value.shape[1] if value.shape[1] > 1 else TILE))


def factor(gram, block):
    size = gram.shape[0]
    groups = size // GROUP
    upper = [gram[GROUP * r : GROUP * (r + 1)] for r in range(groups)]
    row = lax.broadcasted_iota(jnp.int32, (GROUP, size), 0)
    col = lax.broadcasted_iota(jnp.int32, (GROUP, size), 1)
    inverse = [jnp.where(col == row + GROUP * r, 1.0, 0.0).astype(F32) for r in range(groups)]
    for b in range(0, groups, block):
        if b:
            done_upper, done_inverse = jnp.concatenate(upper[:b], axis=0), jnp.concatenate(inverse[:b], axis=0)
            coefficients = done_upper[:, GROUP * b : GROUP * (b + block)]
            less_upper = contract(coefficients, done_upper, ((0,), (0,)), HIGHEST)
            less_inverse = contract(coefficients, done_inverse, ((0,), (0,)), HIGHEST)
            for k in range(block):
                upper[b + k] = upper[b + k] - less_upper[GROUP * k : GROUP * (k + 1)]
                inverse[b + k] = inverse[b + k] - less_inverse[GROUP * k : GROUP * (k + 1)]
        for r in range(b, b + block):
            lane = GROUP * r
            columns = [full(upper[r][:, lane + k : lane + k + 1]) for k in range(GROUP)]
            diag = [[full(columns[j][i : i + 1]) for j in range(i + 1)] for i in range(GROUP)]
            lower = [[None] * GROUP for _ in range(GROUP)]
            scale = [None] * GROUP
            for i in range(GROUP):
                scale[i] = lax.rsqrt(diag[i][i])
                for k in range(i + 1, GROUP):
                    lower[k][i] = diag[k][i] * scale[i]
                for k in range(i + 1, GROUP):
                    for j in range(i + 1, k + 1):
                        diag[k][j] = diag[k][j] - lower[k][i] * lower[j][i]
            u = [full(upper[r][i : i + 1]) for i in range(GROUP)]
            v = [full(inverse[r][i : i + 1]) for i in range(GROUP)]
            for i in range(GROUP):
                u[i], v[i] = u[i] * scale[i], v[i] * scale[i]
                for k in range(i + 1, GROUP):
                    u[k], v[k] = u[k] - lower[k][i] * u[i], v[k] - lower[k][i] * v[i]
            upper[r], inverse[r] = u[0], v[0]
            for i in range(1, GROUP):
                upper[r] = jnp.where(row == i, u[i], upper[r])
                inverse[r] = jnp.where(row == i, v[i], inverse[r])
            for later in range(r + 1, b + block):
                left = [full(upper[later][:, lane + k : lane + k + 1]) for k in range(GROUP)]
                for i in range(GROUP):
                    left[i] = left[i] * scale[i]
                    for k in range(i + 1, GROUP):
                        left[k] = left[k] - lower[k][i] * left[i]
                    upper[later] = upper[later] - left[i] * u[i]
                    inverse[later] = inverse[later] - left[i] * v[i]
    at_row = lax.broadcasted_iota(jnp.int32, (size, size), 0)
    at_col = lax.broadcasted_iota(jnp.int32, (size, size), 1)
    return jnp.where(at_col >= at_row, jnp.concatenate(upper, axis=0), 0.0), jnp.concatenate(inverse, axis=0)


def basis_body(image, gram, basis, upper):
    upper[...], inverse = factor(gram[...], 4)
    basis[...] = contract(image[...], inverse, ((1,), (1,)), HIGHEST)


def per_device(embeddings, start_panel, tile_mask, inv_width):
    n_blk = lax.axis_size("blk")
    half, width = start_panel.shape
    size = half // 2
    sub_move = lambda v: lax.ppermute(v, "sub", [(0, 1), (1, 0)])
    blk_route = lambda v, to: lax.ppermute(v, "blk", [(i, to(i) % n_blk) for i in range(n_blk)])
    blk_move = lambda v, by: blk_route(v, lambda i: i + by)

    after = lambda v, *earlier: lax.optimization_barrier((v, *earlier))[0]
    sub = lax.axis_index("sub").astype(jnp.int32).reshape(1)
    wide = embeddings.shape[1] + width
    packed = lambda rows, lanes: jax.ShapeDtypeStruct((rows, lanes), BF16)
    above = blk_move(embeddings, -2)
    own, first, last, panel_mark = vmem_call(
        pack_body,
        (packed(half + MARK, wide), packed(size + MARK, wide), packed(size, wide), packed(half + MARK, width)),
        embeddings,
        start_panel,
        tile_mask,
        in_hbm=3,
        scratch=[pltpu.VMEM(tile_mask.shape, tile_mask.dtype), pltpu.SemaphoreType.DMA((8,))],
    )
    relayed = n_blk == 8
    swapped = blk_route(last, lambda i: i ^ 1) if relayed else last
    above_panel = blk_move(panel_mark, -2)
    other = sub_move(own)
    image, piece_image = shape(half, width), shape(size, width)
    turned = (shape(width, size),) * 4
    self_image, sq = vmem_call(self_body, (image, shape(4, size)), inv_width, sub, own, other, scalars=2)
    first = after(first, swapped, above, above_panel, self_image)
    swapped = after(swapped, above, above_panel, self_image)
    below0 = blk_move(first, 1)
    below1 = blk_route(swapped, lambda i: i if i & 1 else i + 2) if relayed else blk_move(swapped, 1)
    above_image, *back = vmem_call(
        above_own_body, (image, *turned), inv_width, sub, sq, above, above_panel, own, other, scalars=2
    )
    below_other0 = sub_move(after(below0, above_image))
    below_image0, *back = vmem_call(
        below_first_body, (piece_image, *turned), inv_width, sub, sq, below0, own, other, *back, scalars=2
    )
    above_image, below_image0, below_cross0, marked = vmem_call(
        above_below_first_body,
        (image, piece_image, piece_image, packed(2 * MARK, TILE)),
        inv_width,
        sub,
        above,
        above_panel,
        below0,
        below_other0,
        above_image,
        below_image0,
        scalars=2,
    )
    below1 = after(below1, above_image)
    below_other1 = sub_move(below1)
    above_image, below_sum1, below_cross1 = vmem_call(
        above_below_last_body,
        (image, piece_image, piece_image),
        inv_width,
        sub,
        above,
        above_panel,
        below1,
        below_other1,
        marked,
        above_image,
        scalars=2,
    )
    below_image1, own_image, own_cross = vmem_call(
        below_last_body, (piece_image, image, image), inv_width, sub, sq, marked, below1, own, other, self_image, *back, scalars=2
    )
    above_image = blk_move(above_image, 2)
    below_image0 = blk_move(below_image0 + sub_move(below_cross0), -1)
    below_image1 = blk_move(below_image1 + below_sum1 + sub_move(below_cross1), -1)
    image, gram = vmem_call(
        gram_body, (image, shape(width, width)), own_image, sub_move(own_cross), below_image0, below_image1, above_image
    )
    if n_blk & (n_blk - 1):
        gram = lax.psum(gram, ("blk", "sub"))
    else:
        gram = gram + sub_move(gram)
        hop = 1
        while hop < n_blk:
            gram = gram + blk_route(gram, lambda i: i ^ hop)
            hop *= 2
    return vmem_call(basis_body, (shape(half, width), shape(width, width)), image, gram)


def solution(mesh):
    return jax.shard_map(
        per_device,
        mesh=mesh,
        in_specs=(
            P(("groups", "blk", "sub"), None),
            P(("groups", "blk", "sub"), None),
            P(("groups", "blk", "sub"), None),
            P(),
        ),
        out_specs=(P(("groups", "blk", "sub"), None), P("groups", None)),
        check_vma=False,
    )
```

```python
import jax
import jax.numpy as jnp
from jax import lax
from jax.experimental import pallas as pl
from jax.experimental.pallas import tpu as pltpu
from jax.sharding import PartitionSpec as P

TILE = 128
REACH = 3
F32 = jnp.float32
BF16 = jnp.bfloat16
HIGHEST = lax.Precision.HIGHEST


def vmem_call(body, out_shapes, *operands, scalars=0):
    in_vmem = pl.BlockSpec(memory_space=pltpu.VMEM)
    in_smem = pl.BlockSpec(memory_space=pltpu.SMEM)
    return pl.pallas_call(
        body,
        out_shape=out_shapes,
        in_specs=[in_smem] * scalars + [in_vmem] * (len(operands) - scalars),
        out_specs=jax.tree.map(lambda _: in_vmem, out_shapes),
        compiler_params=pltpu.CompilerParams(vmem_limit_bytes=48 << 20),
        cost_estimate=pl.CostEstimate(flops=10**11, transcendentals=0, bytes_accessed=0),
    )(*operands)


def shape(*dims):
    return jax.ShapeDtypeStruct(dims, F32)


def contract(a, b, dims, precision=None):
    return lax.dot_general(a, b, (dims, ((), ())), precision=precision, preferred_element_type=F32)


MARK = 8
OWN, BELOW, ABOVE = 0, 1, -2


def pair_mask(sub, rows, cols, offset, which):
    tiles = rows.shape[0]
    padded, lanes = rows.shape[1], tiles * TILE
    tile_of = lax.broadcasted_iota(jnp.int32, (padded, lanes), 1) // TILE
    first = (REACH + offset) * 2 * tiles + (sub if which == 0 else 1 - sub) * tiles
    chosen = (lax.broadcasted_iota(jnp.int32, (padded, lanes), 0) == first + tile_of).astype(F32)
    ahead = contract(rows, chosen, ((1,), (0,)))
    first = (REACH - offset) * 2 * tiles + sub * tiles
    row_at = lax.broadcasted_iota(jnp.int32, (tiles, padded), 0)
    chosen = (lax.broadcasted_iota(jnp.int32, (tiles, padded), 1) == first + row_at).astype(F32)
    spread = (lax.broadcasted_iota(jnp.int32, (tiles, lanes), 0) == tile_of[:tiles]).astype(F32)
    back = contract(contract(chosen, cols, ((1,), (1,))), spread, ((1,), (0,)))
    return jnp.concatenate([ahead, back], axis=0)


def marks(ref, size):
    return ref[size : size + MARK, :TILE].astype(F32)[: 2 * size // TILE]


def pieces(ref):
    size = (ref.shape[0] - MARK) // 2
    return [ref[:size], ref[size + MARK :]]


def squares(piece, features):
    wide = piece[:, :features].astype(F32)
    return jnp.sum(wide * wide, axis=1, keepdims=True)


def as_row(column):
    return jnp.broadcast_to(column, (column.shape[0], TILE)).T[:1]


def square_rows(blocks, out):
    rows = [as_row(squares(p, p.shape[1] - TILE)) for block in blocks for p in pieces(block)]
    for k, row in enumerate(rows):
        out[k : k + 1] = row
    return rows


def read_rows(ref):
    return [ref[k : k + 1] for k in range(ref.shape[0])]


def columns_of(blocks, sq_rows, masks):
    out = []
    for h, block in enumerate(blocks):
        for k, piece in enumerate(pieces(block)):
            size = piece.shape[0]
            out.append((piece, sq_rows[2 * h + k], masks[h][:, k * size : (k + 1) * size]))
    return out


def products(inverse, piece, tile, columns, back):
    size, width = piece.shape
    features = width - TILE
    row_sq = squares(piece, features)
    doubled = piece[:, :features] * 2
    panel_t = piece[:, features:].astype(F32).T.astype(BF16)
    image = None
    for k, (other, col_sq, mask) in enumerate(columns):
        tiles = mask.shape[0] // 2
        gram2 = contract(doubled, other[:, :features], ((1,), (1,)))
        kernel = jnp.exp(-inverse * jnp.maximum(row_sq + col_sq - gram2, 0.0))

        def masked(first):
            return jnp.concatenate(
                [kernel[i * TILE : (i + 1) * TILE] * mask[first + i : first + i + 1] for i in range(size // TILE)], axis=0
            ).astype(BF16)

        term = contract(masked(tile), other[:, features:], ((1,), (0,)))
        image = term if image is None else image + term
        if back is not None:
            term = contract(panel_t, masked(tiles + tile), ((1,), (0,)))
            back[k] = term if back[k] is None else back[k] + term
    return image


def store_all(outs, values):
    for out, value in zip(outs, values):
        out[...] = value


def pack_body(embeddings, panel, tile_mask, own, first, last):
    half, features = embeddings.shape
    size = half // 2
    tiles, window = tile_mask.shape
    at = lax.broadcasted_iota(jnp.int32, (window, TILE), 0) == lax.broadcasted_iota(jnp.int32, (window, TILE), 1)
    mask = contract(tile_mask[...].astype(F32), at.astype(F32), ((1,), (0,)))
    mask = jnp.concatenate([mask, jnp.zeros((MARK - tiles, TILE), F32)], axis=0).astype(BF16)
    for ref in (own, first):
        ref[:size, :features] = embeddings[:size]
        ref[:size, features:] = panel[:size]
        ref[size : size + MARK, :TILE] = mask
        ref[size : size + MARK, TILE:] = jnp.zeros((MARK, features), BF16)
    for ref, start in ((own, size + MARK), (last, 0)):
        ref[start : start + size, :features] = embeddings[size:]
        ref[start : start + size, features:] = panel[size:]


def masks_of(sub, ref, others, offset):
    size = (ref.shape[0] - MARK) // 2
    mine = marks(ref, size)
    return [pair_mask(sub, mine, marks(r, size), offset, h) for h, r in enumerate(others)]


def block_products(inverse, block, columns, back):
    out = []
    for piece in pieces(block):
        out.append(products(inverse, piece, len(out) * piece.shape[0] // TILE, columns, back))
    return out


def self_body(inverse, sub, own, other, image, sq):
    rows = square_rows((own, other), sq)
    columns = columns_of((own, other), rows, masks_of(sub[0], own, (own, other), OWN))
    image[...] = jnp.concatenate(block_products(inverse[0], own, columns, None), axis=0)


def above_own_body(inverse, sub, sq, above, own, other, image, *sums):
    columns = columns_of((own, other), read_rows(sq), masks_of(sub[0], above, (own, other), ABOVE))
    back = [None] * 4
    image[...] = jnp.concatenate(block_products(inverse[0], above, columns, back), axis=0)
    store_all(sums, back)


def split_back(back, own_rows, own, cross):
    size = back[0].shape[1]
    for k in range(2):
        own[k * size : (k + 1) * size] = own_rows[k] + back[k].T
        cross[k * size : (k + 1) * size] = back[2 + k].T


def below_own_body(inverse, sub, sq, below, own, other, self_image, t0, t1, t2, t3, image, own_image, cross):
    columns = columns_of((own, other), read_rows(sq), masks_of(sub[0], below, (own, other), BELOW))
    back = [t0[...], t1[...], t2[...], t3[...]]
    image[...] = jnp.concatenate(block_products(inverse[0], below, columns, back), axis=0)
    size = back[0].shape[1]
    split_back(back, (self_image[:size], self_image[size:]), own_image, cross)


def above_below_body(inverse, sub, above, below, other, above_image, below_image, image, below_out, cross):
    rows = [as_row(squares(p, p.shape[1] - TILE)) for block in (below, other) for p in pieces(block)]
    columns = columns_of((below, other), rows, masks_of(sub[0], above, (below, other), ABOVE - BELOW))
    back = [None] * 4
    image[...] = above_image[...] + jnp.concatenate(block_products(inverse[0], above, columns, back), axis=0)
    size = back[0].shape[1]
    split_back(back, (below_image[:size], below_image[size:]), below_out, cross)


def gram_body(own, cross, below, above, image, gram):
    total = own[...] + cross[...] + below[...] + above[...]
    image[...] = total
    gram[...] = contract(total, total, ((0,), (0,)), HIGHEST)


GROUP = 8


def full(value):
    return jnp.broadcast_to(value, (GROUP, value.shape[1] if value.shape[1] > 1 else TILE))


def factor(gram, block):
    size = gram.shape[0]
    groups = size // GROUP
    upper = [gram[GROUP * r : GROUP * (r + 1)] for r in range(groups)]
    row = lax.broadcasted_iota(jnp.int32, (GROUP, size), 0)
    col = lax.broadcasted_iota(jnp.int32, (GROUP, size), 1)
    inverse = [jnp.where(col == row + GROUP * r, 1.0, 0.0).astype(F32) for r in range(groups)]
    for b in range(0, groups, block):
        if b:
            done_upper, done_inverse = jnp.concatenate(upper[:b], axis=0), jnp.concatenate(inverse[:b], axis=0)
            coefficients = done_upper[:, GROUP * b : GROUP * (b + block)]
            less_upper = contract(coefficients, done_upper, ((0,), (0,)), HIGHEST)
            less_inverse = contract(coefficients, done_inverse, ((0,), (0,)), HIGHEST)
            for k in range(block):
                upper[b + k] = upper[b + k] - less_upper[GROUP * k : GROUP * (k + 1)]
                inverse[b + k] = inverse[b + k] - less_inverse[GROUP * k : GROUP * (k + 1)]
        for r in range(b, b + block):
            lane = GROUP * r
            columns = [full(upper[r][:, lane + k : lane + k + 1]) for k in range(GROUP)]
            diag = [[full(columns[j][i : i + 1]) for j in range(i + 1)] for i in range(GROUP)]
            lower = [[None] * GROUP for _ in range(GROUP)]
            scale = [None] * GROUP
            for i in range(GROUP):
                scale[i] = lax.rsqrt(diag[i][i])
                for k in range(i + 1, GROUP):
                    lower[k][i] = diag[k][i] * scale[i]
                for k in range(i + 1, GROUP):
                    for j in range(i + 1, k + 1):
                        diag[k][j] = diag[k][j] - lower[k][i] * lower[j][i]
            u = [full(upper[r][i : i + 1]) for i in range(GROUP)]
            v = [full(inverse[r][i : i + 1]) for i in range(GROUP)]
            for i in range(GROUP):
                u[i], v[i] = u[i] * scale[i], v[i] * scale[i]
                for k in range(i + 1, GROUP):
                    u[k], v[k] = u[k] - lower[k][i] * u[i], v[k] - lower[k][i] * v[i]
            upper[r], inverse[r] = u[0], v[0]
            for i in range(1, GROUP):
                upper[r] = jnp.where(row == i, u[i], upper[r])
                inverse[r] = jnp.where(row == i, v[i], inverse[r])
            for later in range(r + 1, b + block):
                left = [full(upper[later][:, lane + k : lane + k + 1]) for k in range(GROUP)]
                for i in range(GROUP):
                    left[i] = left[i] * scale[i]
                    for k in range(i + 1, GROUP):
                        left[k] = left[k] - lower[k][i] * left[i]
                    upper[later] = upper[later] - left[i] * u[i]
                    inverse[later] = inverse[later] - left[i] * v[i]
    at_row = lax.broadcasted_iota(jnp.int32, (size, size), 0)
    at_col = lax.broadcasted_iota(jnp.int32, (size, size), 1)
    return jnp.where(at_col >= at_row, jnp.concatenate(upper, axis=0), 0.0), jnp.concatenate(inverse, axis=0)


def basis_body(image, gram, basis, upper):
    upper[...], inverse = factor(gram[...], 4)
    basis[...] = contract(image[...], inverse, ((1,), (1,)), HIGHEST)


def per_device(embeddings, start_panel, tile_mask, inv_width):
    n_blk = lax.axis_size("blk")
    half, width = start_panel.shape
    size = half // 2
    sub_move = lambda v: lax.ppermute(v, "sub", [(0, 1), (1, 0)])
    blk_route = lambda v, to: lax.ppermute(v, "blk", [(i, to(i) % n_blk) for i in range(n_blk)])
    blk_move = lambda v, by: blk_route(v, lambda i: i + by)

    after = lambda v, *earlier: lax.optimization_barrier((v, *earlier))[0]
    sub = lax.axis_index("sub").astype(jnp.int32).reshape(1)
    wide = embeddings.shape[1] + width
    packed = lambda rows: jax.ShapeDtypeStruct((rows, wide), BF16)
    own, first, last = vmem_call(
        pack_body, (packed(half + MARK), packed(size + MARK), packed(size)), embeddings, start_panel, tile_mask
    )
    relayed = n_blk == 8
    swapped = blk_route(last, lambda i: i ^ 1) if relayed else last
    above = blk_move(own, -2)
    other = sub_move(own)
    image = shape(half, width)
    sq_rows = shape(4, size)
    self_image, sq = vmem_call(self_body, (image, sq_rows), inv_width, sub, own, other, scalars=2)
    first, swapped = after(first, swapped, self_image), after(swapped, self_image)
    below = [blk_move(first, 1), blk_route(swapped, lambda i: i if i & 1 else i + 2) if relayed else blk_move(swapped, 1)]
    above_image, *back = vmem_call(
        above_own_body, (image, *(shape(width, size),) * 4), inv_width, sub, sq, above, own, other, scalars=2
    )
    below = after(jnp.concatenate(below, axis=0), above_image)
    below_other = sub_move(below)
    below_image, own_image, own_cross = vmem_call(
        below_own_body, (image,) * 3, inv_width, sub, sq, below, own, other, self_image, *back, scalars=2
    )
    above_image, below_image, below_cross = vmem_call(
        above_below_body, (image,) * 3, inv_width, sub, above, below, below_other, above_image, below_image, scalars=2
    )
    above_image = blk_move(above_image, 2)
    below_image = blk_move(below_image + sub_move(below_cross), -1)
    image, gram = vmem_call(
        gram_body, (image, shape(width, width)), own_image, sub_move(own_cross), below_image, above_image
    )
    if n_blk & (n_blk - 1):
        gram = lax.psum(gram, ("blk", "sub"))
    else:
        gram = gram + sub_move(gram)
        hop = 1
        while hop < n_blk:
            gram = gram + blk_route(gram, lambda i: i ^ hop)
            hop *= 2
    return vmem_call(basis_body, (shape(half, width), shape(width, width)), image, gram)


def solution(mesh):
    return jax.shard_map(
        per_device,
        mesh=mesh,
        in_specs=(
            P(("groups", "blk", "sub"), None),
            P(("groups", "blk", "sub"), None),
            P(("groups", "blk", "sub"), None),
            P(),
        ),
        out_specs=(P(("groups", "blk", "sub"), None), P("groups", None)),
        check_vma=False,
    )
```

```python
import jax
import jax.numpy as jnp
from jax import lax
from jax.experimental import pallas as pl
from jax.experimental.pallas import tpu as pltpu
from jax.sharding import PartitionSpec as P

TILE = 128
REACH = 3
F32 = jnp.float32
BF16 = jnp.bfloat16
HIGHEST = lax.Precision.HIGHEST


def vmem_call(body, out_shapes, *operands, scalars=0):
    in_vmem = pl.BlockSpec(memory_space=pltpu.VMEM)
    in_smem = pl.BlockSpec(memory_space=pltpu.SMEM)
    return pl.pallas_call(
        body,
        out_shape=out_shapes,
        in_specs=[in_smem] * scalars + [in_vmem] * (len(operands) - scalars),
        out_specs=jax.tree.map(lambda _: in_vmem, out_shapes),
        compiler_params=pltpu.CompilerParams(vmem_limit_bytes=24 << 20),
        cost_estimate=pl.CostEstimate(flops=10**11, transcendentals=0, bytes_accessed=0),
    )(*operands)


def shape(*dims):
    return jax.ShapeDtypeStruct(dims, F32)


def contract(a, b, dims, precision=None):
    return lax.dot_general(a, b, (dims, ((), ())), precision=precision, preferred_element_type=F32)


MARK = 8
OWN, BELOW, ABOVE = 0, 1, -2


def pair_mask(sub, rows, cols, offset, which):
    tiles = rows.shape[0]
    padded, lanes = rows.shape[1], tiles * TILE
    tile_of = lax.broadcasted_iota(jnp.int32, (padded, lanes), 1) // TILE
    first = (REACH + offset) * 2 * tiles + (sub if which == 0 else 1 - sub) * tiles
    chosen = (lax.broadcasted_iota(jnp.int32, (padded, lanes), 0) == first + tile_of).astype(F32)
    ahead = contract(rows, chosen, ((1,), (0,)))
    first = (REACH - offset) * 2 * tiles + sub * tiles
    row_at = lax.broadcasted_iota(jnp.int32, (tiles, padded), 0)
    chosen = (lax.broadcasted_iota(jnp.int32, (tiles, padded), 1) == first + row_at).astype(F32)
    spread = (lax.broadcasted_iota(jnp.int32, (tiles, lanes), 0) == tile_of[:tiles]).astype(F32)
    back = contract(contract(chosen, cols, ((1,), (1,))), spread, ((1,), (0,)))
    return jnp.concatenate([ahead, back], axis=0)


def marks(ref, half):
    return ref[ref.shape[0] - MARK :, ref.shape[1] - TILE :].astype(F32)[: half // TILE]


def pieces(*refs):
    size = min(r.shape[0] for r in refs)
    return [(r[:size, : r.shape[1] - TILE], r[:size, r.shape[1] - TILE :]) for r in refs]


def apart(features, panel):
    size = features.shape[0] // 2
    return [(features[rows], panel[rows]) for rows in (slice(0, size), slice(size, 2 * size))]


def squares(features):
    wide = features.astype(F32)
    return jnp.sum(wide * wide, axis=1, keepdims=True)


def as_row(column):
    return jnp.broadcast_to(column, (column.shape[0], TILE)).T[:1]


def read_rows(ref):
    return [ref[k : k + 1] for k in range(ref.shape[0])]


def columns_of(own, other, sq_rows, masks):
    out = []
    for half, mask in zip((own, other), masks):
        for k, (features, panel) in enumerate(half):
            size = features.shape[0]
            out.append((features, panel, sq_rows[len(out)], mask[:, k * size : (k + 1) * size]))
    return out


def products(inverse, rows, columns, back):
    panels = jnp.concatenate([panel for _, panel, _, _ in columns], axis=0)
    images = []
    for r, (features, panel) in enumerate(rows):
        size = features.shape[0]
        row_sq = squares(features)
        doubled = features * 2
        tile = r * size // TILE
        ahead, behind = [], []
        for other, _, col_sq, mask in columns:
            tiles = mask.shape[0] // 2
            gram2 = contract(doubled, other, ((1,), (1,)))
            kernel = jnp.exp(-inverse * jnp.maximum(row_sq + col_sq - gram2, 0.0))

            def masked(first):
                parts = [kernel[i * TILE : (i + 1) * TILE] * mask[first + i : first + i + 1] for i in range(size // TILE)]
                return jnp.concatenate(parts, axis=0).astype(BF16)

            ahead.append(masked(tile))
            if back is not None:
                behind.append(masked(tiles + tile))
        images.append(contract(jnp.concatenate(ahead, axis=1), panels, ((1,), (0,))))
        if back is not None:
            panel_t = panel.astype(F32).T.astype(BF16)
            back = back + contract(panel_t, jnp.concatenate(behind, axis=1), ((1,), (0,)))
    return jnp.concatenate(images, axis=0), back


def pack_body(embeddings, panel, tile_mask, first, last, panel_mark):
    half, features = embeddings.shape
    size = half // 2
    tiles, window = tile_mask.shape
    at = lax.broadcasted_iota(jnp.int32, (window, TILE), 0) == lax.broadcasted_iota(jnp.int32, (window, TILE), 1)
    mask = contract(tile_mask[...].astype(F32), at.astype(F32), ((1,), (0,)))
    mask = jnp.concatenate([mask, jnp.zeros((MARK - tiles, TILE), F32)], axis=0).astype(BF16)
    for ref, start in ((first, 0), (last, size)):
        ref[:size, :features] = embeddings[start : start + size]
        ref[:size, features:] = panel[start : start + size]
    first[size:, : features] = jnp.zeros((MARK, features), BF16)
    first[size:, features:] = mask
    panel_mark[:half] = panel[...]
    panel_mark[half:] = mask


def masks_of(sub, rows, others, offset):
    return [pair_mask(sub, rows, r, offset, h) for h, r in enumerate(others)]


def self_body(inverse, sub, first, last, other_first, other_last, image, sq):
    half = 2 * last.shape[0]
    own, other = pieces(first, last), pieces(other_first, other_last)
    rows = [as_row(squares(features)) for features, _ in own + other]
    for k, row in enumerate(rows):
        sq[k : k + 1] = row
    both = [marks(r, half) for r in (first, other_first)]
    image[...], _ = products(inverse[0], own, columns_of(own, other, rows, masks_of(sub[0], both[0], both, OWN)), None)


def above_own_body(inverse, sub, sq, above, panel, first, last, other_first, other_last, image, back):
    half = above.shape[0]
    masks = masks_of(sub[0], marks(panel, half), [marks(r, half) for r in (first, other_first)], ABOVE)
    columns = columns_of(pieces(first, last), pieces(other_first, other_last), read_rows(sq), masks)
    image[...], back[...] = products(inverse[0], apart(above, panel), columns, jnp.zeros(back.shape, F32))


def below_own_body(inverse, sub, sq, below0, below1, first, last, other_first, other_last, self_image, back, image, own_image, cross):
    half = image.shape[0]
    masks = masks_of(sub[0], marks(below0, half), [marks(r, half) for r in (first, other_first)], BELOW)
    columns = columns_of(pieces(first, last), pieces(other_first, other_last), read_rows(sq), masks)
    image[...], total = products(inverse[0], pieces(below0, below1), columns, back[...])
    own_image[...] = self_image[...] + total[:, :half].T
    cross[...] = total[:, half:].T


def above_below_body(
    inverse, sub, above, panel, below0, below1, other0, other1, above_image, below_image, image, below_out, cross
):
    half = image.shape[0]
    masks = masks_of(sub[0], marks(panel, half), [marks(r, half) for r in (below0, other0)], ABOVE - BELOW)
    own, other = pieces(below0, below1), pieces(other0, other1)
    columns = columns_of(own, other, [as_row(squares(features)) for features, _ in own + other], masks)
    products_image, total = products(inverse[0], apart(above, panel), columns, jnp.zeros((TILE, 2 * half), F32))
    image[...] = above_image[...] + products_image
    below_out[...] = below_image[...] + total[:, :half].T
    cross[...] = total[:, half:].T


def gram_body(own, cross, below, above, image, gram):
    total = own[...] + cross[...] + below[...] + above[...]
    image[...] = total
    gram[...] = contract(total, total, ((0,), (0,)), HIGHEST)


GROUP = 8


def full(value):
    return jnp.broadcast_to(value, (GROUP, value.shape[1] if value.shape[1] > 1 else TILE))


def factor(gram, block):
    size = gram.shape[0]
    groups = size // GROUP
    upper = [gram[GROUP * r : GROUP * (r + 1)] for r in range(groups)]
    row = lax.broadcasted_iota(jnp.int32, (GROUP, size), 0)
    col = lax.broadcasted_iota(jnp.int32, (GROUP, size), 1)
    inverse = [jnp.where(col == row + GROUP * r, 1.0, 0.0).astype(F32) for r in range(groups)]
    for b in range(0, groups, block):
        if b:
            done_upper, done_inverse = jnp.concatenate(upper[:b], axis=0), jnp.concatenate(inverse[:b], axis=0)
            coefficients = done_upper[:, GROUP * b : GROUP * (b + block)]
            less_upper = contract(coefficients, done_upper, ((0,), (0,)), HIGHEST)
            less_inverse = contract(coefficients, done_inverse, ((0,), (0,)), HIGHEST)
            for k in range(block):
                upper[b + k] = upper[b + k] - less_upper[GROUP * k : GROUP * (k + 1)]
                inverse[b + k] = inverse[b + k] - less_inverse[GROUP * k : GROUP * (k + 1)]
        for r in range(b, b + block):
            lane = GROUP * r
            columns = [full(upper[r][:, lane + k : lane + k + 1]) for k in range(GROUP)]
            diag = [[full(columns[j][i : i + 1]) for j in range(i + 1)] for i in range(GROUP)]
            lower = [[None] * GROUP for _ in range(GROUP)]
            scale = [None] * GROUP
            for i in range(GROUP):
                scale[i] = lax.rsqrt(diag[i][i])
                for k in range(i + 1, GROUP):
                    lower[k][i] = diag[k][i] * scale[i]
                for k in range(i + 1, GROUP):
                    for j in range(i + 1, k + 1):
                        diag[k][j] = diag[k][j] - lower[k][i] * lower[j][i]
            u = [full(upper[r][i : i + 1]) for i in range(GROUP)]
            v = [full(inverse[r][i : i + 1]) for i in range(GROUP)]
            for i in range(GROUP):
                u[i], v[i] = u[i] * scale[i], v[i] * scale[i]
                for k in range(i + 1, GROUP):
                    u[k], v[k] = u[k] - lower[k][i] * u[i], v[k] - lower[k][i] * v[i]
            upper[r], inverse[r] = u[0], v[0]
            for i in range(1, GROUP):
                upper[r] = jnp.where(row == i, u[i], upper[r])
                inverse[r] = jnp.where(row == i, v[i], inverse[r])
            for later in range(r + 1, b + block):
                left = [full(upper[later][:, lane + k : lane + k + 1]) for k in range(GROUP)]
                for i in range(GROUP):
                    left[i] = left[i] * scale[i]
                    for k in range(i + 1, GROUP):
                        left[k] = left[k] - lower[k][i] * left[i]
                    upper[later] = upper[later] - left[i] * u[i]
                    inverse[later] = inverse[later] - left[i] * v[i]
    at_row = lax.broadcasted_iota(jnp.int32, (size, size), 0)
    at_col = lax.broadcasted_iota(jnp.int32, (size, size), 1)
    return jnp.where(at_col >= at_row, jnp.concatenate(upper, axis=0), 0.0), jnp.concatenate(inverse, axis=0)


def basis_body(image, gram, basis, upper):
    upper[...], inverse = factor(gram[...], 4)
    basis[...] = contract(image[...], inverse, ((1,), (1,)), HIGHEST)


def per_device(embeddings, start_panel, tile_mask, inv_width):
    n_blk = lax.axis_size("blk")
    half, width = start_panel.shape
    size = half // 2
    sub_move = lambda v: lax.ppermute(v, "sub", [(0, 1), (1, 0)])
    blk_route = lambda v, to: lax.ppermute(v, "blk", [(i, to(i) % n_blk) for i in range(n_blk)])
    blk_move = lambda v, by: blk_route(v, lambda i: i + by)

    after = lambda v, *earlier: lax.optimization_barrier((v, *earlier))[0]
    sub = lax.axis_index("sub").astype(jnp.int32).reshape(1)
    wide = embeddings.shape[1] + width
    packed = lambda rows, lanes: jax.ShapeDtypeStruct((rows, lanes), BF16)
    above = blk_move(embeddings, -2)
    first, last, panel_mark = vmem_call(
        pack_body,
        (packed(size + MARK, wide), packed(size, wide), packed(half + MARK, width)),
        embeddings,
        start_panel,
        tile_mask,
    )
    relayed = n_blk == 8
    swapped = blk_route(last, lambda i: i ^ 1) if relayed else last
    above_panel = blk_move(panel_mark, -2)
    own = (first, last, sub_move(first), sub_move(last))
    image, turned = shape(half, width), shape(width, 2 * half)
    self_image, sq = vmem_call(self_body, (image, shape(4, size)), inv_width, sub, *own, scalars=2)
    below0 = blk_move(after(first, swapped, self_image), 1)
    swapped = after(swapped, self_image)
    below1 = blk_route(swapped, lambda i: i if i & 1 else i + 2) if relayed else blk_move(swapped, 1)
    above_image, back = vmem_call(above_own_body, (image, turned), inv_width, sub, sq, above, above_panel, *own, scalars=2)
    below0, below1 = after(below0, above_image, below1), after(below1, above_image, below0)
    below_other = (sub_move(below0), sub_move(below1))
    below_image, own_image, own_cross = vmem_call(
        below_own_body, (image,) * 3, inv_width, sub, sq, below0, below1, *own, self_image, back, scalars=2
    )
    above_image, below_image, below_cross = vmem_call(
        above_below_body,
        (image,) * 3,
        inv_width,
        sub,
        above,
        above_panel,
        below0,
        below1,
        *below_other,
        above_image,
        below_image,
        scalars=2,
    )
    above_image = blk_move(above_image, 2)
    below_image = blk_move(below_image + sub_move(below_cross), -1)
    image, gram = vmem_call(
        gram_body, (image, shape(width, width)), own_image, sub_move(own_cross), below_image, above_image
    )
    if n_blk & (n_blk - 1):
        gram = lax.psum(gram, ("blk", "sub"))
    else:
        gram = gram + sub_move(gram)
        hop = 1
        while hop < n_blk:
            gram = gram + blk_route(gram, lambda i: i ^ hop)
            hop *= 2
    return vmem_call(basis_body, (shape(half, width), shape(width, width)), image, gram)


def solution(mesh):
    return jax.shard_map(
        per_device,
        mesh=mesh,
        in_specs=(
            P(("groups", "blk", "sub"), None),
            P(("groups", "blk", "sub"), None),
            P(("groups", "blk", "sub"), None),
            P(),
        ),
        out_specs=(P(("groups", "blk", "sub"), None), P("groups", None)),
        check_vma=False,
    )
```

```python
import jax
import jax.numpy as jnp
from jax import lax
from jax.experimental import pallas as pl
from jax.experimental.pallas import tpu as pltpu
from jax.sharding import PartitionSpec as P

TILE = 128
REACH = 3
F32 = jnp.float32
BF16 = jnp.bfloat16
HIGHEST = lax.Precision.HIGHEST


def vmem_call(body, out_shapes, *operands, scalars=0, long=True):
    in_vmem = pl.BlockSpec(memory_space=pltpu.VMEM)
    in_smem = pl.BlockSpec(memory_space=pltpu.SMEM)
    return pl.pallas_call(
        body,
        out_shape=out_shapes,
        in_specs=[in_smem] * scalars + [in_vmem] * (len(operands) - scalars),
        out_specs=jax.tree.map(lambda _: in_vmem, out_shapes),
        compiler_params=pltpu.CompilerParams(vmem_limit_bytes=24 << 20),
        cost_estimate=pl.CostEstimate(flops=10**11 if long else 1, transcendentals=0, bytes_accessed=1),
    )(*operands)


def shape(*dims):
    return jax.ShapeDtypeStruct(dims, F32)


def contract(a, b, dims, precision=None):
    return lax.dot_general(a, b, (dims, ((), ())), precision=precision, preferred_element_type=F32)


MARK = 8
OWN, BELOW, ABOVE = 0, 1, -2


def pair_mask(sub, rows, cols, offset, which):
    tiles = rows.shape[0]
    padded, lanes = rows.shape[1], tiles * TILE
    tile_of = lax.broadcasted_iota(jnp.int32, (padded, lanes), 1) // TILE
    first = (REACH + offset) * 2 * tiles + (sub if which == 0 else 1 - sub) * tiles
    chosen = (lax.broadcasted_iota(jnp.int32, (padded, lanes), 0) == first + tile_of).astype(F32)
    ahead = contract(rows, chosen, ((1,), (0,)))
    first = (REACH - offset) * 2 * tiles + sub * tiles
    row_at = lax.broadcasted_iota(jnp.int32, (tiles, padded), 0)
    chosen = (lax.broadcasted_iota(jnp.int32, (tiles, padded), 1) == first + row_at).astype(F32)
    spread = (lax.broadcasted_iota(jnp.int32, (tiles, lanes), 0) == tile_of[:tiles]).astype(F32)
    back = contract(contract(chosen, cols, ((1,), (1,))), spread, ((1,), (0,)))
    return jnp.concatenate([ahead, back], axis=0)


def marks(ref, half):
    return ref[ref.shape[0] - MARK :, ref.shape[1] - TILE :].astype(F32)[: half // TILE]


def pieces(*refs):
    size = min(r.shape[0] for r in refs)
    return [(r[:size, : r.shape[1] - TILE], r[:size, r.shape[1] - TILE :]) for r in refs]


def apart(features, panel):
    size = features.shape[0] // 2
    return [(features[rows], panel[rows]) for rows in (slice(0, size), slice(size, 2 * size))]


def squares(features):
    wide = features.astype(F32)
    return jnp.sum(wide * wide, axis=1, keepdims=True)


def as_row(column):
    return jnp.broadcast_to(column, (column.shape[0], TILE)).T[:1]


def read_rows(ref):
    return [ref[k : k + 1] for k in range(ref.shape[0])]


def columns_of(own, other, sq_rows, masks):
    out = []
    for half, mask in zip((own, other), masks):
        for k, (features, panel) in enumerate(half):
            size = features.shape[0]
            out.append((features, panel, sq_rows[len(out)], mask[:, k * size : (k + 1) * size]))
    return out


def products(inverse, rows, columns, back):
    panels = jnp.concatenate([panel for _, panel, _, _ in columns], axis=0)
    images = []
    for r, (features, panel) in enumerate(rows):
        size = features.shape[0]
        row_sq = squares(features)
        doubled = features * 2
        tile = r * size // TILE
        ahead, behind = [], []
        for other, _, col_sq, mask in columns:
            tiles = mask.shape[0] // 2
            gram2 = contract(doubled, other, ((1,), (1,)))
            kernel = jnp.exp(-inverse * jnp.maximum(row_sq + col_sq - gram2, 0.0))

            def masked(first):
                parts = [kernel[i * TILE : (i + 1) * TILE] * mask[first + i : first + i + 1] for i in range(size // TILE)]
                return jnp.concatenate(parts, axis=0).astype(BF16)

            ahead.append(masked(tile))
            if back is not None:
                behind.append(masked(tiles + tile))
        images.append(contract(jnp.concatenate(ahead, axis=1), panels, ((1,), (0,))))
        if back is not None:
            panel_t = panel.astype(F32).T.astype(BF16)
            back = back + contract(panel_t, jnp.concatenate(behind, axis=1), ((1,), (0,)))
    return jnp.concatenate(images, axis=0), back


def pack_body(embeddings, panel, tile_mask, first, last, panel_mark):
    half, features = embeddings.shape
    size = half // 2
    tiles, window = tile_mask.shape
    at = lax.broadcasted_iota(jnp.int32, (window, TILE), 0) == lax.broadcasted_iota(jnp.int32, (window, TILE), 1)
    mask = contract(tile_mask[...].astype(F32), at.astype(F32), ((1,), (0,)))
    mask = jnp.concatenate([mask, jnp.zeros((MARK - tiles, TILE), F32)], axis=0).astype(BF16)
    for ref, start in ((first, 0), (last, size)):
        ref[:size, :features] = embeddings[start : start + size]
        ref[:size, features:] = panel[start : start + size]
    first[size:, : features] = jnp.zeros((MARK, features), BF16)
    first[size:, features:] = mask
    panel_mark[:half] = panel[...]
    panel_mark[half:] = mask


def masks_of(sub, rows, others, offset):
    return [pair_mask(sub, rows, r, offset, h) for h, r in enumerate(others)]


def self_body(inverse, sub, first, last, other_first, other_last, image, sq):
    half = 2 * last.shape[0]
    own, other = pieces(first, last), pieces(other_first, other_last)
    rows = [as_row(squares(features)) for features, _ in own + other]
    for k, row in enumerate(rows):
        sq[k : k + 1] = row
    both = [marks(r, half) for r in (first, other_first)]
    image[...], _ = products(inverse[0], own, columns_of(own, other, rows, masks_of(sub[0], both[0], both, OWN)), None)


def above_own_body(inverse, sub, sq, above, panel, first, last, other_first, other_last, image, back):
    half = above.shape[0]
    masks = masks_of(sub[0], marks(panel, half), [marks(r, half) for r in (first, other_first)], ABOVE)
    columns = columns_of(pieces(first, last), pieces(other_first, other_last), read_rows(sq), masks)
    image[...], back[...] = products(inverse[0], apart(above, panel), columns, jnp.zeros(back.shape, F32))


def below_own_body(inverse, sub, sq, below0, below1, first, last, other_first, other_last, self_image, back, image, own_image, cross):
    half = image.shape[0]
    masks = masks_of(sub[0], marks(below0, half), [marks(r, half) for r in (first, other_first)], BELOW)
    columns = columns_of(pieces(first, last), pieces(other_first, other_last), read_rows(sq), masks)
    image[...], total = products(inverse[0], pieces(below0, below1), columns, back[...])
    own_image[...] = self_image[...] + total[:, :half].T
    cross[...] = total[:, half:].T


def above_below_body(
    inverse, sub, above, panel, below0, below1, other0, other1, above_image, below_image, image, below_out, cross
):
    half = image.shape[0]
    masks = masks_of(sub[0], marks(panel, half), [marks(r, half) for r in (below0, other0)], ABOVE - BELOW)
    own, other = pieces(below0, below1), pieces(other0, other1)
    columns = columns_of(own, other, [as_row(squares(features)) for features, _ in own + other], masks)
    products_image, total = products(inverse[0], apart(above, panel), columns, jnp.zeros((TILE, 2 * half), F32))
    image[...] = above_image[...] + products_image
    below_out[...] = below_image[...] + total[:, :half].T
    cross[...] = total[:, half:].T


def gram_body(own, cross, below, above, image, gram):
    total = own[...] + cross[...] + below[...] + above[...]
    image[...] = total
    gram[...] = contract(total, total, ((0,), (0,)), HIGHEST)


GROUP = 8


def full(value):
    return jnp.broadcast_to(value, (GROUP, value.shape[1] if value.shape[1] > 1 else TILE))


def factor(gram, block):
    size = gram.shape[0]
    groups = size // GROUP
    upper = [gram[GROUP * r : GROUP * (r + 1)] for r in range(groups)]
    row = lax.broadcasted_iota(jnp.int32, (GROUP, size), 0)
    col = lax.broadcasted_iota(jnp.int32, (GROUP, size), 1)
    inverse = [jnp.where(col == row + GROUP * r, 1.0, 0.0).astype(F32) for r in range(groups)]
    for b in range(0, groups, block):
        if b:
            done_upper, done_inverse = jnp.concatenate(upper[:b], axis=0), jnp.concatenate(inverse[:b], axis=0)
            coefficients = done_upper[:, GROUP * b : GROUP * (b + block)]
            less_upper = contract(coefficients, done_upper, ((0,), (0,)), HIGHEST)
            less_inverse = contract(coefficients, done_inverse, ((0,), (0,)), HIGHEST)
            for k in range(block):
                upper[b + k] = upper[b + k] - less_upper[GROUP * k : GROUP * (k + 1)]
                inverse[b + k] = inverse[b + k] - less_inverse[GROUP * k : GROUP * (k + 1)]
        for r in range(b, b + block):
            lane = GROUP * r
            columns = [full(upper[r][:, lane + k : lane + k + 1]) for k in range(GROUP)]
            diag = [[full(columns[j][i : i + 1]) for j in range(i + 1)] for i in range(GROUP)]
            lower = [[None] * GROUP for _ in range(GROUP)]
            scale = [None] * GROUP
            for i in range(GROUP):
                scale[i] = lax.rsqrt(diag[i][i])
                for k in range(i + 1, GROUP):
                    lower[k][i] = diag[k][i] * scale[i]
                for k in range(i + 1, GROUP):
                    for j in range(i + 1, k + 1):
                        diag[k][j] = diag[k][j] - lower[k][i] * lower[j][i]
            u = [full(upper[r][i : i + 1]) for i in range(GROUP)]
            v = [full(inverse[r][i : i + 1]) for i in range(GROUP)]
            for i in range(GROUP):
                u[i], v[i] = u[i] * scale[i], v[i] * scale[i]
                for k in range(i + 1, GROUP):
                    u[k], v[k] = u[k] - lower[k][i] * u[i], v[k] - lower[k][i] * v[i]
            upper[r], inverse[r] = u[0], v[0]
            for i in range(1, GROUP):
                upper[r] = jnp.where(row == i, u[i], upper[r])
                inverse[r] = jnp.where(row == i, v[i], inverse[r])
            for later in range(r + 1, b + block):
                left = [full(upper[later][:, lane + k : lane + k + 1]) for k in range(GROUP)]
                for i in range(GROUP):
                    left[i] = left[i] * scale[i]
                    for k in range(i + 1, GROUP):
                        left[k] = left[k] - lower[k][i] * left[i]
                    upper[later] = upper[later] - left[i] * u[i]
                    inverse[later] = inverse[later] - left[i] * v[i]
    at_row = lax.broadcasted_iota(jnp.int32, (size, size), 0)
    at_col = lax.broadcasted_iota(jnp.int32, (size, size), 1)
    return jnp.where(at_col >= at_row, jnp.concatenate(upper, axis=0), 0.0), jnp.concatenate(inverse, axis=0)


def basis_body(image, gram, basis, upper):
    upper[...], inverse = factor(gram[...], 4)
    basis[...] = contract(image[...], inverse, ((1,), (1,)), HIGHEST)


def per_device(embeddings, start_panel, tile_mask, inv_width):
    n_blk = lax.axis_size("blk")
    half, width = start_panel.shape
    size = half // 2
    sub_move = lambda v: lax.ppermute(v, "sub", [(0, 1), (1, 0)])
    blk_route = lambda v, to: lax.ppermute(v, "blk", [(i, to(i) % n_blk) for i in range(n_blk)])
    blk_move = lambda v, by: blk_route(v, lambda i: i + by)

    after = lambda v, *earlier: lax.optimization_barrier((v, *earlier))[0]
    sub = lax.axis_index("sub").astype(jnp.int32).reshape(1)
    wide = embeddings.shape[1] + width
    packed = lambda rows, lanes: jax.ShapeDtypeStruct((rows, lanes), BF16)
    above = blk_move(embeddings, -2)
    first, last, panel_mark = vmem_call(
        pack_body,
        (packed(size + MARK, wide), packed(size, wide), packed(half + MARK, width)),
        embeddings,
        start_panel,
        tile_mask,
        long=False,
    )
    relayed = n_blk == 8
    swapped = blk_route(last, lambda i: i ^ 1) if relayed else last
    above_panel = blk_move(panel_mark, -2)
    own = (first, last, sub_move(first), sub_move(last))
    image, turned = shape(half, width), shape(width, 2 * half)
    self_image, sq = vmem_call(self_body, (image, shape(4, size)), inv_width, sub, *own, scalars=2, long=False)
    below0 = blk_move(after(first, swapped, self_image), 1)
    swapped = after(swapped, self_image)
    below1 = blk_route(swapped, lambda i: i if i & 1 else i + 2) if relayed else blk_move(swapped, 1)
    above_image, back = vmem_call(above_own_body, (image, turned), inv_width, sub, sq, above, above_panel, *own, scalars=2)
    below0, below1 = after(below0, above_image, below1), after(below1, above_image, below0)
    below_other = (sub_move(below0), sub_move(below1))
    below_image, own_image, own_cross = vmem_call(
        below_own_body, (image,) * 3, inv_width, sub, sq, below0, below1, *own, self_image, back, scalars=2
    )
    above_image, below_image, below_cross = vmem_call(
        above_below_body,
        (image,) * 3,
        inv_width,
        sub,
        above,
        above_panel,
        below0,
        below1,
        *below_other,
        above_image,
        below_image,
        scalars=2,
    )
    above_image = blk_move(above_image, 2)
    below_image = blk_move(below_image + sub_move(below_cross), -1)
    image, gram = vmem_call(
        gram_body, (image, shape(width, width)), own_image, sub_move(own_cross), below_image, above_image
    )
    if n_blk & (n_blk - 1):
        gram = lax.psum(gram, ("blk", "sub"))
    else:
        gram = gram + sub_move(gram)
        hop = 1
        while hop < n_blk:
            gram = gram + blk_route(gram, lambda i: i ^ hop)
            hop *= 2
    return vmem_call(basis_body, (shape(half, width), shape(width, width)), image, gram)


def solution(mesh):
    return jax.shard_map(
        per_device,
        mesh=mesh,
        in_specs=(
            P(("groups", "blk", "sub"), None),
            P(("groups", "blk", "sub"), None),
            P(("groups", "blk", "sub"), None),
            P(),
        ),
        out_specs=(P(("groups", "blk", "sub"), None), P("groups", None)),
        check_vma=False,
    )
```

```python
import jax
import jax.numpy as jnp
from jax import lax
from jax.experimental import pallas as pl
from jax.experimental.pallas import tpu as pltpu
from jax.sharding import PartitionSpec as P

TILE = 128
REACH = 3
F32 = jnp.float32
BF16 = jnp.bfloat16
HIGHEST = lax.Precision.HIGHEST


def vmem_call(body, out_shapes, *operands, scalars=0, long=True):
    in_vmem = pl.BlockSpec(memory_space=pltpu.VMEM)
    in_smem = pl.BlockSpec(memory_space=pltpu.SMEM)
    return pl.pallas_call(
        body,
        out_shape=out_shapes,
        in_specs=[in_smem] * scalars + [in_vmem] * (len(operands) - scalars),
        out_specs=jax.tree.map(lambda _: in_vmem, out_shapes),
        compiler_params=pltpu.CompilerParams(vmem_limit_bytes=24 << 20),
        cost_estimate=pl.CostEstimate(flops=10**11 if long else 1, transcendentals=0, bytes_accessed=1),
    )(*operands)


def shape(*dims):
    return jax.ShapeDtypeStruct(dims, F32)


def contract(a, b, dims, precision=None):
    return lax.dot_general(a, b, (dims, ((), ())), precision=precision, preferred_element_type=F32)


MARK = 8
OWN, BELOW, ABOVE = 0, 1, -2


def pair_mask(sub, rows, cols, offset, which):
    tiles = rows.shape[0]
    padded, lanes = rows.shape[1], tiles * TILE
    tile_of = lax.broadcasted_iota(jnp.int32, (padded, lanes), 1) // TILE
    first = (REACH + offset) * 2 * tiles + (sub if which == 0 else 1 - sub) * tiles
    chosen = (lax.broadcasted_iota(jnp.int32, (padded, lanes), 0) == first + tile_of).astype(F32)
    ahead = contract(rows, chosen, ((1,), (0,)))
    first = (REACH - offset) * 2 * tiles + sub * tiles
    row_at = lax.broadcasted_iota(jnp.int32, (tiles, padded), 0)
    chosen = (lax.broadcasted_iota(jnp.int32, (tiles, padded), 1) == first + row_at).astype(F32)
    spread = (lax.broadcasted_iota(jnp.int32, (tiles, lanes), 0) == tile_of[:tiles]).astype(F32)
    back = contract(contract(chosen, cols, ((1,), (1,))), spread, ((1,), (0,)))
    return jnp.concatenate([ahead, back], axis=0)


def marks(ref, half):
    return ref[ref.shape[0] - MARK :, ref.shape[1] - TILE :].astype(F32)[: half // TILE]


def pieces(*refs):
    size = min(r.shape[0] for r in refs)
    return [(r[:size, : r.shape[1] - TILE], r[:size, r.shape[1] - TILE :]) for r in refs]


def apart(features, panel):
    size = features.shape[0] // 2
    return [(features[rows], panel[rows]) for rows in (slice(0, size), slice(size, 2 * size))]


def squares(features):
    wide = features.astype(F32)
    return jnp.sum(wide * wide, axis=1, keepdims=True)


def as_row(column):
    return jnp.broadcast_to(column, (column.shape[0], TILE)).T[:1]


def as_column(row):
    return jnp.broadcast_to(row, (TILE, row.shape[1])).T[:, :1]


SPLIT = 3


def square_rows(ref):
    size = ref.shape[0] - MARK
    parts = ref[size:, : 2 * size].astype(F32)
    row = (parts[0:1] + parts[1:2]) + parts[2:3]
    return [row[:, :size], row[:, size:]]


def columns_of(own, other, sq_rows, masks):
    out = []
    for half, mask in zip((own, other), masks):
        for k, (features, panel) in enumerate(half):
            size = features.shape[0]
            out.append((features, panel, sq_rows[len(out)], mask[:, k * size : (k + 1) * size]))
    return out


def products(inverse, rows, squares_of, columns, back):
    panels = jnp.concatenate([panel for _, panel, _, _ in columns], axis=0)
    images = []
    for r, (features, panel) in enumerate(rows):
        size = features.shape[0]
        row_sq = squares_of[r]
        doubled = features * 2
        tile = r * size // TILE
        ahead, behind = [], []
        for other, _, col_sq, mask in columns:
            tiles = mask.shape[0] // 2
            gram2 = contract(doubled, other, ((1,), (1,)))
            kernel = jnp.exp(-inverse * jnp.maximum(row_sq + col_sq - gram2, 0.0))

            def masked(first):
                parts = [kernel[i * TILE : (i + 1) * TILE] * mask[first + i : first + i + 1] for i in range(size // TILE)]
                return jnp.concatenate(parts, axis=0).astype(BF16)

            ahead.append(masked(tile))
            if back is not None:
                behind.append(masked(tiles + tile))
        images.append(contract(jnp.concatenate(ahead, axis=1), panels, ((1,), (0,))))
        if back is not None:
            panel_t = panel.astype(F32).T.astype(BF16)
            back = back + contract(panel_t, jnp.concatenate(behind, axis=1), ((1,), (0,)))
    return jnp.concatenate(images, axis=0), back


def pack_body(embeddings, panel, tile_mask, first, last, panel_mark):
    half, features = embeddings.shape
    size = half // 2
    tiles, window = tile_mask.shape
    at = lax.broadcasted_iota(jnp.int32, (window, TILE), 0) == lax.broadcasted_iota(jnp.int32, (window, TILE), 1)
    mask = contract(tile_mask[...].astype(F32), at.astype(F32), ((1,), (0,)))
    mask = jnp.concatenate([mask, jnp.zeros((MARK - tiles, TILE), F32)], axis=0).astype(BF16)
    for ref, start in ((first, 0), (last, size)):
        ref[:size, :features] = embeddings[start : start + size]
        ref[:size, features:] = panel[start : start + size]
    row = as_row(jnp.concatenate([squares(r[:size, :features]) for r in (first, last)], axis=0))
    carried = []
    for _ in range(SPLIT):
        carried.append(row.astype(BF16).astype(F32))
        row = row - carried[-1]
    carried = jnp.concatenate(carried + [jnp.zeros((MARK - SPLIT, half), F32)], axis=0).astype(BF16)
    first[size:, :features] = jnp.concatenate([carried, jnp.zeros((MARK, features - half), BF16)], axis=1)
    first[size:, features:] = mask
    panel_mark[:half] = panel[...]
    panel_mark[half:] = mask


def masks_of(sub, rows, others, offset):
    return [pair_mask(sub, rows, r, offset, h) for h, r in enumerate(others)]


def self_body(inverse, sub, first, last, other_first, other_last, image):
    half = 2 * last.shape[0]
    own, other = pieces(first, last), pieces(other_first, other_last)
    rows = square_rows(first)
    both = [marks(r, half) for r in (first, other_first)]
    columns = columns_of(own, other, rows + square_rows(other_first), masks_of(sub[0], both[0], both, OWN))
    image[...], _ = products(inverse[0], own, [as_column(r) for r in rows], columns, None)


def own_columns(sub, mark, first, last, other_first, other_last, offset):
    half = 2 * last.shape[0]
    masks = masks_of(sub, mark, [marks(r, half) for r in (first, other_first)], offset)
    rows = square_rows(first) + square_rows(other_first)
    return columns_of(pieces(first, last), pieces(other_first, other_last), rows, masks)


def above_own_body(inverse, sub, above, panel, first, last, other_first, other_last, image, back, above_sq):
    half = above.shape[0]
    size = half // 2
    columns = own_columns(sub[0], marks(panel, half), first, last, other_first, other_last, ABOVE)
    rows = apart(above, panel)
    columns_sq = [squares(features) for features, _ in rows]
    for k, column in enumerate(columns_sq):
        above_sq[k * size : (k + 1) * size] = jnp.broadcast_to(column, (size, TILE))
    image[...], back[...] = products(inverse[0], rows, columns_sq, columns, jnp.zeros(back.shape, F32))


def below_own_body(inverse, sub, below0, below1, first, last, other_first, other_last, self_image, back, image, own_image, cross):
    half = image.shape[0]
    columns = own_columns(sub[0], marks(below0, half), first, last, other_first, other_last, BELOW)
    rows_sq = [as_column(r) for r in square_rows(below0)]
    image[...], total = products(inverse[0], pieces(below0, below1), rows_sq, columns, back[...])
    own_image[...] = self_image[...] + total[:, :half].T
    cross[...] = total[:, half:].T


def above_below_body(
    inverse, sub, above, panel, above_sq, below0, below1, other0, other1, above_image, below_image, image, below_out, cross
):
    half = image.shape[0]
    size = half // 2
    columns = own_columns(sub[0], marks(panel, half), below0, below1, other0, other1, ABOVE - BELOW)
    rows_sq = [above_sq[k * size : (k + 1) * size, :1] for k in range(2)]
    products_image, total = products(inverse[0], apart(above, panel), rows_sq, columns, jnp.zeros((TILE, 2 * half), F32))
    image[...] = above_image[...] + products_image
    below_out[...] = below_image[...] + total[:, :half].T
    cross[...] = total[:, half:].T


def gram_body(own, cross, below, above, image, gram):
    total = own[...] + cross[...] + below[...] + above[...]
    image[...] = total
    gram[...] = contract(total, total, ((0,), (0,)), HIGHEST)


GROUP = 8


def full(value):
    return jnp.broadcast_to(value, (GROUP, value.shape[1] if value.shape[1] > 1 else TILE))


def factor(gram, block):
    size = gram.shape[0]
    groups = size // GROUP
    upper = [gram[GROUP * r : GROUP * (r + 1)] for r in range(groups)]
    row = lax.broadcasted_iota(jnp.int32, (GROUP, size), 0)
    col = lax.broadcasted_iota(jnp.int32, (GROUP, size), 1)
    inverse = [jnp.where(col == row + GROUP * r, 1.0, 0.0).astype(F32) for r in range(groups)]
    for b in range(0, groups, block):
        if b:
            done_upper, done_inverse = jnp.concatenate(upper[:b], axis=0), jnp.concatenate(inverse[:b], axis=0)
            coefficients = done_upper[:, GROUP * b : GROUP * (b + block)]
            less_upper = contract(coefficients, done_upper, ((0,), (0,)), HIGHEST)
            less_inverse = contract(coefficients, done_inverse, ((0,), (0,)), HIGHEST)
            for k in range(block):
                upper[b + k] = upper[b + k] - less_upper[GROUP * k : GROUP * (k + 1)]
                inverse[b + k] = inverse[b + k] - less_inverse[GROUP * k : GROUP * (k + 1)]
        for r in range(b, b + block):
            lane = GROUP * r
            columns = [full(upper[r][:, lane + k : lane + k + 1]) for k in range(GROUP)]
            diag = [[full(columns[j][i : i + 1]) for j in range(i + 1)] for i in range(GROUP)]
            lower = [[None] * GROUP for _ in range(GROUP)]
            scale = [None] * GROUP
            for i in range(GROUP):
                scale[i] = lax.rsqrt(diag[i][i])
                for k in range(i + 1, GROUP):
                    lower[k][i] = diag[k][i] * scale[i]
                for k in range(i + 1, GROUP):
                    for j in range(i + 1, k + 1):
                        diag[k][j] = diag[k][j] - lower[k][i] * lower[j][i]
            u = [full(upper[r][i : i + 1]) for i in range(GROUP)]
            v = [full(inverse[r][i : i + 1]) for i in range(GROUP)]
            for i in range(GROUP):
                u[i], v[i] = u[i] * scale[i], v[i] * scale[i]
                for k in range(i + 1, GROUP):
                    u[k], v[k] = u[k] - lower[k][i] * u[i], v[k] - lower[k][i] * v[i]
            upper[r], inverse[r] = u[0], v[0]
            for i in range(1, GROUP):
                upper[r] = jnp.where(row == i, u[i], upper[r])
                inverse[r] = jnp.where(row == i, v[i], inverse[r])
            for later in range(r + 1, b + block):
                left = [full(upper[later][:, lane + k : lane + k + 1]) for k in range(GROUP)]
                for i in range(GROUP):
                    left[i] = left[i] * scale[i]
                    for k in range(i + 1, GROUP):
                        left[k] = left[k] - lower[k][i] * left[i]
                    upper[later] = upper[later] - left[i] * u[i]
                    inverse[later] = inverse[later] - left[i] * v[i]
    at_row = lax.broadcasted_iota(jnp.int32, (size, size), 0)
    at_col = lax.broadcasted_iota(jnp.int32, (size, size), 1)
    return jnp.where(at_col >= at_row, jnp.concatenate(upper, axis=0), 0.0), jnp.concatenate(inverse, axis=0)


def basis_body(image, *refs):
    *grams, basis, upper = refs
    upper[...], inverse = factor(jnp.concatenate([g[...] for g in grams], axis=0), 4)
    basis[...] = contract(image[...], inverse, ((1,), (1,)), HIGHEST)


def per_device(embeddings, start_panel, tile_mask, inv_width):
    n_blk = lax.axis_size("blk")
    half, width = start_panel.shape
    size = half // 2
    sub_move = lambda v: lax.ppermute(v, "sub", [(0, 1), (1, 0)])
    blk_route = lambda v, to: lax.ppermute(v, "blk", [(i, to(i) % n_blk) for i in range(n_blk)])
    blk_move = lambda v, by: blk_route(v, lambda i: i + by)

    after = lambda v, *earlier: lax.optimization_barrier((v, *earlier))[0]
    sub = lax.axis_index("sub").astype(jnp.int32).reshape(1)
    wide = embeddings.shape[1] + width
    packed = lambda rows, lanes: jax.ShapeDtypeStruct((rows, lanes), BF16)
    above = blk_move(embeddings, -2)
    first, last, panel_mark = vmem_call(
        pack_body,
        (packed(size + MARK, wide), packed(size, wide), packed(half + MARK, width)),
        embeddings,
        start_panel,
        tile_mask,
        long=False,
    )
    relayed = n_blk == 8
    swapped = blk_route(last, lambda i: i ^ 1) if relayed else last
    above_panel = blk_move(panel_mark, -2)
    own = (first, last, sub_move(first), sub_move(last))
    image, turned = shape(half, width), shape(width, 2 * half)
    self_image = vmem_call(self_body, image, inv_width, sub, *own, scalars=2, long=False)
    below0 = blk_move(after(first, swapped, self_image), 1)
    swapped = after(swapped, self_image)
    below1 = blk_route(swapped, lambda i: i if i & 1 else i + 2) if relayed else blk_move(swapped, 1)
    above_image, back, above_sq = vmem_call(
        above_own_body, (image, turned, image), inv_width, sub, above, above_panel, *own, scalars=2
    )
    below0, below1 = after(below0, above_image, below1), after(below1, above_image, below0)
    below_other = (sub_move(below0), sub_move(below1))
    below_image, own_image, own_cross = vmem_call(
        below_own_body, (image,) * 3, inv_width, sub, below0, below1, *own, self_image, back, scalars=2
    )
    above_image, below_image, below_cross = vmem_call(
        above_below_body,
        (image,) * 3,
        inv_width,
        sub,
        above,
        above_panel,
        above_sq,
        below0,
        below1,
        *below_other,
        above_image,
        below_image,
        scalars=2,
    )
    above_image = blk_move(above_image, 2)
    below_image = blk_move(below_image + sub_move(below_cross), -1)
    image_rows, gram = vmem_call(
        gram_body, (image, shape(width, width)), own_image, sub_move(own_cross), below_image, above_image
    )
    if n_blk & (n_blk - 1):
        gram_parts = [lax.psum(gram, ("blk", "sub"))]
    else:
        rows = width // 2
        top, bottom = gram[:rows], gram[rows:]
        mine = lax.axis_index("sub") == 0
        part = jnp.where(mine, top, bottom) + sub_move(jnp.where(mine, bottom, top))
        hops = [1 << k for k in range(n_blk.bit_length() - 1)]
        part = part + blk_route(part, lambda i: i ^ hops[0])
        for k in range(1, len(hops), 2):
            a, *b = hops[k : k + 2]
            near = part + blk_route(part, lambda i: i ^ a)
            if b:
                near = near + (blk_route(part, lambda i: i ^ b[0]) + blk_route(part, lambda i: i ^ a ^ b[0]))
            part = near
        moved = sub_move(part)
        gram_parts = [jnp.where(mine, part, moved), jnp.where(mine, moved, part)]
    return vmem_call(basis_body, (image, shape(width, width)), image_rows, *gram_parts)


def solution(mesh):
    return jax.shard_map(
        per_device,
        mesh=mesh,
        in_specs=(
            P(("groups", "blk", "sub"), None),
            P(("groups", "blk", "sub"), None),
            P(("groups", "blk", "sub"), None),
            P(),
        ),
        out_specs=(P(("groups", "blk", "sub"), None), P("groups", None)),
        check_vma=False,
    )
```

```python
import jax
import jax.numpy as jnp
from jax import lax
from jax.experimental import pallas as pl
from jax.experimental.pallas import tpu as pltpu
from jax.sharding import PartitionSpec as P

TILE = 128
REACH = 3
F32 = jnp.float32
BF16 = jnp.bfloat16
HIGHEST = lax.Precision.HIGHEST


def vmem_call(body, out_shapes, *operands, scalars=0, long=True):
    in_vmem = pl.BlockSpec(memory_space=pltpu.VMEM)
    in_smem = pl.BlockSpec(memory_space=pltpu.SMEM)
    return pl.pallas_call(
        body,
        out_shape=out_shapes,
        in_specs=[in_smem] * scalars + [in_vmem] * (len(operands) - scalars),
        out_specs=jax.tree.map(lambda _: in_vmem, out_shapes),
        compiler_params=pltpu.CompilerParams(vmem_limit_bytes=24 << 20),
        cost_estimate=pl.CostEstimate(flops=10**11 if long else 1, transcendentals=0, bytes_accessed=1),
    )(*operands)


def shape(*dims):
    return jax.ShapeDtypeStruct(dims, F32)


def contract(a, b, dims, precision=None):
    return lax.dot_general(a, b, (dims, ((), ())), precision=precision, preferred_element_type=F32)


MARK = 8
OWN, BELOW, ABOVE = 0, 1, -2


def pair_mask(sub, rows, cols, offset, which):
    tiles = rows.shape[0]
    padded, lanes = rows.shape[1], tiles * TILE
    tile_of = lax.broadcasted_iota(jnp.int32, (padded, lanes), 1) // TILE
    first = (REACH + offset) * 2 * tiles + (sub if which == 0 else 1 - sub) * tiles
    chosen = (lax.broadcasted_iota(jnp.int32, (padded, lanes), 0) == first + tile_of).astype(F32)
    ahead = contract(rows, chosen, ((1,), (0,)))
    first = (REACH - offset) * 2 * tiles + sub * tiles
    row_at = lax.broadcasted_iota(jnp.int32, (tiles, padded), 0)
    chosen = (lax.broadcasted_iota(jnp.int32, (tiles, padded), 1) == first + row_at).astype(F32)
    spread = (lax.broadcasted_iota(jnp.int32, (tiles, lanes), 0) == tile_of[:tiles]).astype(F32)
    back = contract(contract(chosen, cols, ((1,), (1,))), spread, ((1,), (0,)))
    return jnp.concatenate([ahead, back], axis=0)


def marks(ref, half):
    return ref[ref.shape[0] - MARK :, ref.shape[1] - TILE :].astype(F32)[: half // TILE]


def pieces(*refs):
    size = min(r.shape[0] for r in refs)
    return [(r[:size, : r.shape[1] - TILE], r[:size, r.shape[1] - TILE :]) for r in refs]


def apart(features, panel):
    size = features.shape[0] // 2
    return [(features[rows], panel[rows]) for rows in (slice(0, size), slice(size, 2 * size))]


def squares(features):
    wide = features.astype(F32)
    return jnp.sum(wide * wide, axis=1, keepdims=True)


def as_row(column):
    return jnp.broadcast_to(column, (column.shape[0], TILE)).T[:1]


def as_column(row):
    return jnp.broadcast_to(row, (TILE, row.shape[1])).T[:, :1]


SPLIT = 3


def square_rows(ref):
    size = ref.shape[0] - MARK
    parts = ref[size:, : 2 * size].astype(F32)
    row = (parts[0:1] + parts[1:2]) + parts[2:3]
    return [row[:, :size], row[:, size:]]


def columns_of(own, other, sq_rows, masks):
    out = []
    for half, mask in zip((own, other), masks):
        for k, (features, panel) in enumerate(half):
            size = features.shape[0]
            out.append((features, panel, sq_rows[len(out)], mask[:, k * size : (k + 1) * size]))
    return out


def products(inverse, rows, squares_of, columns, back):
    panels = jnp.concatenate([panel for _, panel, _, _ in columns], axis=0)
    images = []
    for r, (features, panel) in enumerate(rows):
        size = features.shape[0]
        row_sq = squares_of[r]
        doubled = features * 2
        tile = r * size // TILE
        ahead, behind = [], []
        for other, _, col_sq, mask in columns:
            tiles = mask.shape[0] // 2
            gram2 = contract(doubled, other, ((1,), (1,)))
            kernel = jnp.exp(-inverse * jnp.maximum(row_sq + col_sq - gram2, 0.0))

            def masked(first):
                parts = [kernel[i * TILE : (i + 1) * TILE] * mask[first + i : first + i + 1] for i in range(size // TILE)]
                return jnp.concatenate(parts, axis=0).astype(BF16)

            ahead.append(masked(tile))
            if back is not None:
                behind.append(masked(tiles + tile))
        images.append(contract(jnp.concatenate(ahead, axis=1), panels, ((1,), (0,))))
        if back is not None:
            panel_t = panel.astype(F32).T.astype(BF16)
            back = back + contract(panel_t, jnp.concatenate(behind, axis=1), ((1,), (0,)))
    return jnp.concatenate(images, axis=0), back


def pack_body(embeddings, panel, tile_mask, first, last, panel_mark):
    half, features = embeddings.shape
    size = half // 2
    tiles, window = tile_mask.shape
    at = lax.broadcasted_iota(jnp.int32, (window, TILE), 0) == lax.broadcasted_iota(jnp.int32, (window, TILE), 1)
    mask = contract(tile_mask[...].astype(F32), at.astype(F32), ((1,), (0,)))
    mask = jnp.concatenate([mask, jnp.zeros((MARK - tiles, TILE), F32)], axis=0).astype(BF16)
    for ref, start in ((first, 0), (last, size)):
        ref[:size, :features] = embeddings[start : start + size]
        ref[:size, features:] = panel[start : start + size]
    row = as_row(jnp.concatenate([squares(r[:size, :features]) for r in (first, last)], axis=0))
    carried = []
    for _ in range(SPLIT):
        carried.append(row.astype(BF16).astype(F32))
        row = row - carried[-1]
    carried = jnp.concatenate(carried + [jnp.zeros((MARK - SPLIT, half), F32)], axis=0).astype(BF16)
    first[size:, :features] = jnp.concatenate([carried, jnp.zeros((MARK, features - half), BF16)], axis=1)
    first[size:, features:] = mask
    panel_mark[:half] = panel[...]
    panel_mark[half:] = mask


def masks_of(sub, rows, others, offset):
    return [pair_mask(sub, rows, r, offset, h) for h, r in enumerate(others)]


def self_body(inverse, sub, first, last, other_first, other_last, image):
    half = 2 * last.shape[0]
    own, other = pieces(first, last), pieces(other_first, other_last)
    rows = square_rows(first)
    both = [marks(r, half) for r in (first, other_first)]
    columns = columns_of(own, other, rows + square_rows(other_first), masks_of(sub[0], both[0], both, OWN))
    image[...], _ = products(inverse[0], own, [as_column(r) for r in rows], columns, None)


def own_columns(sub, mark, first, last, other_first, other_last, offset):
    half = 2 * last.shape[0]
    masks = masks_of(sub, mark, [marks(r, half) for r in (first, other_first)], offset)
    rows = square_rows(first) + square_rows(other_first)
    return columns_of(pieces(first, last), pieces(other_first, other_last), rows, masks)


def above_own_body(inverse, sub, above, panel, first, last, other_first, other_last, image, back, above_sq):
    half = above.shape[0]
    size = half // 2
    columns = own_columns(sub[0], marks(panel, half), first, last, other_first, other_last, ABOVE)
    rows = apart(above, panel)
    columns_sq = [squares(features) for features, _ in rows]
    for k, column in enumerate(columns_sq):
        above_sq[k * size : (k + 1) * size] = jnp.broadcast_to(column, (size, TILE))
    image[...], back[...] = products(inverse[0], rows, columns_sq, columns, jnp.zeros(back.shape, F32))


def below_own_body(inverse, sub, below0, below1, first, last, other_first, other_last, back, image, total):
    half = image.shape[0]
    columns = own_columns(sub[0], marks(below0, half), first, last, other_first, other_last, BELOW)
    rows_sq = [as_column(r) for r in square_rows(below0)]
    image[...], total[...] = products(inverse[0], pieces(below0, below1), rows_sq, columns, back[...])


def above_below_body(
    inverse,
    sub,
    above,
    panel,
    above_sq,
    below0,
    below1,
    other0,
    other1,
    above_image,
    below_image,
    self_image,
    back,
    image,
    below_out,
    below_cross,
    own_out,
    own_cross,
):
    half = image.shape[0]
    size = half // 2
    columns = own_columns(sub[0], marks(panel, half), below0, below1, other0, other1, ABOVE - BELOW)
    rows_sq = [above_sq[k * size : (k + 1) * size, :1] for k in range(2)]
    products_image, total = products(inverse[0], apart(above, panel), rows_sq, columns, jnp.zeros((TILE, 2 * half), F32))
    image[...] = above_image[...] + products_image
    below_out[...] = below_image[...] + total[:, :half].T
    below_cross[...] = total[:, half:].T
    own_out[...] = self_image[...] + back[:, :half].T
    own_cross[...] = back[:, half:].T


def gram_body(own, cross, below, above, image, gram):
    total = own[...] + cross[...] + below[...] + above[...]
    image[...] = total
    gram[...] = contract(total, total, ((0,), (0,)), HIGHEST)


GROUP = 8


def full(value):
    return jnp.broadcast_to(value, (GROUP, value.shape[1] if value.shape[1] > 1 else TILE))


def factor(gram, block):
    size = gram.shape[0]
    groups = size // GROUP
    upper = [gram[GROUP * r : GROUP * (r + 1)] for r in range(groups)]
    row = lax.broadcasted_iota(jnp.int32, (GROUP, size), 0)
    col = lax.broadcasted_iota(jnp.int32, (GROUP, size), 1)
    inverse = [jnp.where(col == row + GROUP * r, 1.0, 0.0).astype(F32) for r in range(groups)]
    for b in range(0, groups, block):
        if b:
            done_upper, done_inverse = jnp.concatenate(upper[:b], axis=0), jnp.concatenate(inverse[:b], axis=0)
            coefficients = done_upper[:, GROUP * b : GROUP * (b + block)]
            less_upper = contract(coefficients, done_upper, ((0,), (0,)), HIGHEST)
            less_inverse = contract(coefficients, done_inverse, ((0,), (0,)), HIGHEST)
            for k in range(block):
                upper[b + k] = upper[b + k] - less_upper[GROUP * k : GROUP * (k + 1)]
                inverse[b + k] = inverse[b + k] - less_inverse[GROUP * k : GROUP * (k + 1)]
        for r in range(b, b + block):
            lane = GROUP * r
            columns = [full(upper[r][:, lane + k : lane + k + 1]) for k in range(GROUP)]
            diag = [[full(columns[j][i : i + 1]) for j in range(i + 1)] for i in range(GROUP)]
            lower = [[None] * GROUP for _ in range(GROUP)]
            scale = [None] * GROUP
            for i in range(GROUP):
                scale[i] = lax.rsqrt(diag[i][i])
                for k in range(i + 1, GROUP):
                    lower[k][i] = diag[k][i] * scale[i]
                for k in range(i + 1, GROUP):
                    for j in range(i + 1, k + 1):
                        diag[k][j] = diag[k][j] - lower[k][i] * lower[j][i]
            u = [full(upper[r][i : i + 1]) for i in range(GROUP)]
            v = [full(inverse[r][i : i + 1]) for i in range(GROUP)]
            for i in range(GROUP):
                u[i], v[i] = u[i] * scale[i], v[i] * scale[i]
                for k in range(i + 1, GROUP):
                    u[k], v[k] = u[k] - lower[k][i] * u[i], v[k] - lower[k][i] * v[i]
            upper[r], inverse[r] = u[0], v[0]
            for i in range(1, GROUP):
                upper[r] = jnp.where(row == i, u[i], upper[r])
                inverse[r] = jnp.where(row == i, v[i], inverse[r])
            for later in range(r + 1, b + block):
                left = [full(upper[later][:, lane + k : lane + k + 1]) for k in range(GROUP)]
                for i in range(GROUP):
                    left[i] = left[i] * scale[i]
                    for k in range(i + 1, GROUP):
                        left[k] = left[k] - lower[k][i] * left[i]
                    upper[later] = upper[later] - left[i] * u[i]
                    inverse[later] = inverse[later] - left[i] * v[i]
    at_row = lax.broadcasted_iota(jnp.int32, (size, size), 0)
    at_col = lax.broadcasted_iota(jnp.int32, (size, size), 1)
    return jnp.where(at_col >= at_row, jnp.concatenate(upper, axis=0), 0.0), jnp.concatenate(inverse, axis=0)


def basis_body(image, gram, basis, upper):
    upper[...], inverse = factor(gram[...], 4)
    basis[...] = contract(image[...], inverse, ((1,), (1,)), HIGHEST)


def per_device(embeddings, start_panel, tile_mask, inv_width):
    n_blk = lax.axis_size("blk")
    half, width = start_panel.shape
    size = half // 2
    sub_move = lambda v: lax.ppermute(v, "sub", [(0, 1), (1, 0)])
    blk_route = lambda v, to: lax.ppermute(v, "blk", [(i, to(i) % n_blk) for i in range(n_blk)])
    blk_move = lambda v, by: blk_route(v, lambda i: i + by)

    after = lambda v, *earlier: lax.optimization_barrier((v, *earlier))[0]
    sub = lax.axis_index("sub").astype(jnp.int32).reshape(1)
    wide = embeddings.shape[1] + width
    packed = lambda rows, lanes: jax.ShapeDtypeStruct((rows, lanes), BF16)
    above = blk_move(embeddings, -2)
    first, last, panel_mark = vmem_call(
        pack_body,
        (packed(size + MARK, wide), packed(size, wide), packed(half + MARK, width)),
        embeddings,
        start_panel,
        tile_mask,
        long=False,
    )
    relayed = n_blk == 8
    swapped = blk_route(last, lambda i: i ^ 1) if relayed else last
    above_panel = blk_move(panel_mark, -2)
    own = (first, last, sub_move(first), sub_move(last))
    image, turned = shape(half, width), shape(width, 2 * half)
    self_image = vmem_call(self_body, image, inv_width, sub, *own, scalars=2, long=False)
    below0 = blk_move(after(first, swapped, self_image), 1)
    swapped = after(swapped, self_image)
    below1 = blk_route(swapped, lambda i: i if i & 1 else i + 2) if relayed else blk_move(swapped, 1)
    above_image, back, above_sq = vmem_call(
        above_own_body, (image, turned, image), inv_width, sub, above, above_panel, *own, scalars=2
    )
    below0, below1 = after(below0, above_image, below1), after(below1, above_image, below0)
    below_other = (sub_move(below0), sub_move(below1))
    below_image, back = vmem_call(
        below_own_body, (image, turned), inv_width, sub, below0, below1, *own, back, scalars=2
    )
    above_image, below_image, below_cross, own_image, own_cross = vmem_call(
        above_below_body,
        (image,) * 5,
        inv_width,
        sub,
        above,
        above_panel,
        above_sq,
        below0,
        below1,
        *below_other,
        above_image,
        below_image,
        self_image,
        back,
        scalars=2,
    )
    above_image = blk_move(above_image, 2)
    below_image = blk_move(below_image + sub_move(below_cross), -1)
    image_rows, gram = vmem_call(
        gram_body, (image, shape(width, width)), own_image, sub_move(own_cross), below_image, above_image
    )
    if n_blk & (n_blk - 1):
        gram = lax.psum(gram, ("blk", "sub"))
    else:
        gram = gram + sub_move(gram)
        hop = 1
        while hop < n_blk:
            gram = gram + blk_route(gram, lambda i: i ^ hop)
            hop *= 2
    return vmem_call(basis_body, (image, shape(width, width)), image_rows, gram)


def solution(mesh):
    return jax.shard_map(
        per_device,
        mesh=mesh,
        in_specs=(
            P(("groups", "blk", "sub"), None),
            P(("groups", "blk", "sub"), None),
            P(("groups", "blk", "sub"), None),
            P(),
        ),
        out_specs=(P(("groups", "blk", "sub"), None), P("groups", None)),
        check_vma=False,
    )
```

```python
import jax
import jax.numpy as jnp
from jax import lax
from jax.experimental import pallas as pl
from jax.experimental.pallas import tpu as pltpu
from jax.sharding import PartitionSpec as P

TILE = 128
REACH = 3
F32 = jnp.float32
BF16 = jnp.bfloat16
HIGHEST = lax.Precision.HIGHEST


def vmem_call(body, out_shapes, *operands, scalars=0, long=True):
    in_vmem = pl.BlockSpec(memory_space=pltpu.VMEM)
    in_smem = pl.BlockSpec(memory_space=pltpu.SMEM)
    return pl.pallas_call(
        body,
        out_shape=out_shapes,
        in_specs=[in_smem] * scalars + [in_vmem] * (len(operands) - scalars),
        out_specs=jax.tree.map(lambda _: in_vmem, out_shapes),
        compiler_params=pltpu.CompilerParams(vmem_limit_bytes=24 << 20),
        cost_estimate=pl.CostEstimate(flops=10**11 if long else 1, transcendentals=0, bytes_accessed=1),
    )(*operands)


def shape(*dims):
    return jax.ShapeDtypeStruct(dims, F32)


def contract(a, b, dims, precision=None):
    return lax.dot_general(a, b, (dims, ((), ())), precision=precision, preferred_element_type=F32)


MARK = 8
OWN, BELOW, ABOVE = 0, 1, -2


def pair_mask(sub, rows, cols, offset, which):
    tiles = rows.shape[0]
    padded, lanes = rows.shape[1], tiles * TILE
    tile_of = lax.broadcasted_iota(jnp.int32, (padded, lanes), 1) // TILE
    first = (REACH + offset) * 2 * tiles + (sub if which == 0 else 1 - sub) * tiles
    chosen = (lax.broadcasted_iota(jnp.int32, (padded, lanes), 0) == first + tile_of).astype(F32)
    ahead = contract(rows, chosen, ((1,), (0,)))
    first = (REACH - offset) * 2 * tiles + sub * tiles
    row_at = lax.broadcasted_iota(jnp.int32, (tiles, padded), 0)
    chosen = (lax.broadcasted_iota(jnp.int32, (tiles, padded), 1) == first + row_at).astype(F32)
    spread = (lax.broadcasted_iota(jnp.int32, (tiles, lanes), 0) == tile_of[:tiles]).astype(F32)
    back = contract(contract(chosen, cols, ((1,), (1,))), spread, ((1,), (0,)))
    return jnp.concatenate([ahead, back], axis=0)


def marks(ref, half):
    return ref[ref.shape[0] - MARK :, ref.shape[1] - TILE :].astype(F32)[: half // TILE]


def pieces(*refs):
    size = min(r.shape[0] for r in refs)
    return [(r[:size, : r.shape[1] - TILE], r[:size, r.shape[1] - TILE :]) for r in refs]


def apart(features, panel):
    size = features.shape[0] // 2
    return [(features[rows], panel[rows]) for rows in (slice(0, size), slice(size, 2 * size))]


def squares(features):
    wide = features.astype(F32)
    return jnp.sum(wide * wide, axis=1, keepdims=True)


def as_row(column):
    return jnp.broadcast_to(column, (column.shape[0], TILE)).T[:1]


def as_column(row):
    return jnp.broadcast_to(row, (TILE, row.shape[1])).T[:, :1]


SPLIT = 3


def square_rows(ref):
    size = ref.shape[0] - MARK
    parts = ref[size:, : 2 * size].astype(F32)
    row = (parts[0:1] + parts[1:2]) + parts[2:3]
    return [row[:, :size], row[:, size:]]


def columns_of(own, other, sq_rows, masks):
    out = []
    for half, mask in zip((own, other), masks):
        for k, (features, panel) in enumerate(half):
            size = features.shape[0]
            out.append((features, panel, sq_rows[len(out)], mask[:, k * size : (k + 1) * size]))
    return out


def products(inverse, rows, squares_of, columns, back, first=0):
    panels = jnp.concatenate([panel for _, panel, _, _ in columns], axis=0)
    images = []
    for r, (features, panel) in enumerate(rows):
        size = features.shape[0]
        row_sq = squares_of[r]
        doubled = features * 2
        tile = (first + r) * size // TILE
        ahead, behind = [], []
        for other, _, col_sq, mask in columns:
            tiles = mask.shape[0] // 2
            gram2 = contract(doubled, other, ((1,), (1,)))
            kernel = jnp.exp(-inverse * jnp.maximum(row_sq + col_sq - gram2, 0.0))

            def masked(first):
                parts = [kernel[i * TILE : (i + 1) * TILE] * mask[first + i : first + i + 1] for i in range(size // TILE)]
                return jnp.concatenate(parts, axis=0).astype(BF16)

            ahead.append(masked(tile))
            if back is not None:
                behind.append(masked(tiles + tile))
        images.append(contract(jnp.concatenate(ahead, axis=1), panels, ((1,), (0,))))
        if back is not None:
            panel_t = panel.astype(F32).T.astype(BF16)
            back = back + contract(panel_t, jnp.concatenate(behind, axis=1), ((1,), (0,)))
    return jnp.concatenate(images, axis=0), back


def pack_body(embeddings, panel, tile_mask, first, last, panel_mark):
    half, features = embeddings.shape
    size = half // 2
    tiles, window = tile_mask.shape
    at = lax.broadcasted_iota(jnp.int32, (window, TILE), 0) == lax.broadcasted_iota(jnp.int32, (window, TILE), 1)
    mask = contract(tile_mask[...].astype(F32), at.astype(F32), ((1,), (0,)))
    mask = jnp.concatenate([mask, jnp.zeros((MARK - tiles, TILE), F32)], axis=0).astype(BF16)
    for ref, start in ((first, 0), (last, size)):
        ref[:size, :features] = embeddings[start : start + size]
        ref[:size, features:] = panel[start : start + size]
    row = as_row(jnp.concatenate([squares(r[:size, :features]) for r in (first, last)], axis=0))
    carried = []
    for _ in range(SPLIT):
        carried.append(row.astype(BF16).astype(F32))
        row = row - carried[-1]
    carried = jnp.concatenate(carried + [jnp.zeros((MARK - SPLIT, half), F32)], axis=0).astype(BF16)
    first[size:, :features] = jnp.concatenate([carried, jnp.zeros((MARK, features - half), BF16)], axis=1)
    first[size:, features:] = mask
    panel_mark[:half] = panel[...]
    panel_mark[half:] = mask


def masks_of(sub, rows, others, offset):
    return [pair_mask(sub, rows, r, offset, h) for h, r in enumerate(others)]


def self_body(inverse, sub, first, last, other_first, other_last, image):
    half = 2 * last.shape[0]
    own, other = pieces(first, last), pieces(other_first, other_last)
    rows = square_rows(first)
    both = [marks(r, half) for r in (first, other_first)]
    columns = columns_of(own, other, rows + square_rows(other_first), masks_of(sub[0], both[0], both, OWN))
    image[...], _ = products(inverse[0], own, [as_column(r) for r in rows], columns, None)


def own_columns(sub, mark, first, last, other_first, other_last, offset):
    half = 2 * last.shape[0]
    masks = masks_of(sub, mark, [marks(r, half) for r in (first, other_first)], offset)
    rows = square_rows(first) + square_rows(other_first)
    return columns_of(pieces(first, last), pieces(other_first, other_last), rows, masks)


def above_own_body(inverse, sub, above, panel, first, last, other_first, other_last, image, back, above_sq):
    half = above.shape[0]
    size = half // 2
    columns = own_columns(sub[0], marks(panel, half), first, last, other_first, other_last, ABOVE)
    rows = apart(above, panel)
    columns_sq = [squares(features) for features, _ in rows]
    for k, column in enumerate(columns_sq):
        above_sq[k * size : (k + 1) * size] = jnp.broadcast_to(column, (size, TILE))
    image[...], back[...] = products(inverse[0], rows, columns_sq, columns, jnp.zeros(back.shape, F32))


def below_first_body(inverse, sub, below, first, last, other_first, other_last, back, image, total):
    half = 2 * last.shape[0]
    columns = own_columns(sub[0], marks(below, half), first, last, other_first, other_last, BELOW)
    rows_sq = [as_column(square_rows(below)[0])]
    image[...], total[...] = products(inverse[0], [pieces(below, last)[0]], rows_sq, columns, back[...])


def below_last_body(
    inverse, sub, marked, below, first, last, other_first, other_last, self_image, back, image, own_image, own_cross
):
    half = 2 * last.shape[0]
    columns = own_columns(sub[0], marks(marked, half), first, last, other_first, other_last, BELOW)
    rows_sq = [as_column(square_rows(marked)[1])]
    image[...], total = products(inverse[0], pieces(below), rows_sq, columns, back[...], 1)
    own_image[...] = self_image[...] + total[:, :half].T
    own_cross[...] = total[:, half:].T


def above_below_body(inverse, sub, above, panel, above_sq, below0, below1, other0, other1, above_image, image, below_image, cross):
    half = image.shape[0]
    size = half // 2
    columns = own_columns(sub[0], marks(panel, half), below0, below1, other0, other1, ABOVE - BELOW)
    rows_sq = [above_sq[k * size : (k + 1) * size, :1] for k in range(2)]
    products_image, total = products(inverse[0], apart(above, panel), rows_sq, columns, jnp.zeros((TILE, 2 * half), F32))
    image[...] = above_image[...] + products_image
    below_image[...] = total[:, :half].T
    cross[...] = total[:, half:].T


def gram_body(own, cross, below, above, image, gram):
    total = own[...] + cross[...] + below[...] + above[...]
    image[...] = total
    gram[...] = contract(total, total, ((0,), (0,)), HIGHEST)


GROUP = 8


def full(value):
    return jnp.broadcast_to(value, (GROUP, value.shape[1] if value.shape[1] > 1 else TILE))


def factor(gram, block):
    size = gram.shape[0]
    groups = size // GROUP
    upper = [gram[GROUP * r : GROUP * (r + 1)] for r in range(groups)]
    row = lax.broadcasted_iota(jnp.int32, (GROUP, size), 0)
    col = lax.broadcasted_iota(jnp.int32, (GROUP, size), 1)
    inverse = [jnp.where(col == row + GROUP * r, 1.0, 0.0).astype(F32) for r in range(groups)]
    for b in range(0, groups, block):
        if b:
            done_upper, done_inverse = jnp.concatenate(upper[:b], axis=0), jnp.concatenate(inverse[:b], axis=0)
            coefficients = done_upper[:, GROUP * b : GROUP * (b + block)]
            less_upper = contract(coefficients, done_upper, ((0,), (0,)), HIGHEST)
            less_inverse = contract(coefficients, done_inverse, ((0,), (0,)), HIGHEST)
            for k in range(block):
                upper[b + k] = upper[b + k] - less_upper[GROUP * k : GROUP * (k + 1)]
                inverse[b + k] = inverse[b + k] - less_inverse[GROUP * k : GROUP * (k + 1)]
        for r in range(b, b + block):
            lane = GROUP * r
            columns = [full(upper[r][:, lane + k : lane + k + 1]) for k in range(GROUP)]
            diag = [[full(columns[j][i : i + 1]) for j in range(i + 1)] for i in range(GROUP)]
            lower = [[None] * GROUP for _ in range(GROUP)]
            scale = [None] * GROUP
            for i in range(GROUP):
                scale[i] = lax.rsqrt(diag[i][i])
                for k in range(i + 1, GROUP):
                    lower[k][i] = diag[k][i] * scale[i]
                for k in range(i + 1, GROUP):
                    for j in range(i + 1, k + 1):
                        diag[k][j] = diag[k][j] - lower[k][i] * lower[j][i]
            u = [full(upper[r][i : i + 1]) for i in range(GROUP)]
            v = [full(inverse[r][i : i + 1]) for i in range(GROUP)]
            for i in range(GROUP):
                u[i], v[i] = u[i] * scale[i], v[i] * scale[i]
                for k in range(i + 1, GROUP):
                    u[k], v[k] = u[k] - lower[k][i] * u[i], v[k] - lower[k][i] * v[i]
            upper[r], inverse[r] = u[0], v[0]
            for i in range(1, GROUP):
                upper[r] = jnp.where(row == i, u[i], upper[r])
                inverse[r] = jnp.where(row == i, v[i], inverse[r])
            for later in range(r + 1, b + block):
                left = [full(upper[later][:, lane + k : lane + k + 1]) for k in range(GROUP)]
                for i in range(GROUP):
                    left[i] = left[i] * scale[i]
                    for k in range(i + 1, GROUP):
                        left[k] = left[k] - lower[k][i] * left[i]
                    upper[later] = upper[later] - left[i] * u[i]
                    inverse[later] = inverse[later] - left[i] * v[i]
    at_row = lax.broadcasted_iota(jnp.int32, (size, size), 0)
    at_col = lax.broadcasted_iota(jnp.int32, (size, size), 1)
    return jnp.where(at_col >= at_row, jnp.concatenate(upper, axis=0), 0.0), jnp.concatenate(inverse, axis=0)


def basis_body(image, gram, basis, upper):
    upper[...], inverse = factor(gram[...], 4)
    basis[...] = contract(image[...], inverse, ((1,), (1,)), HIGHEST)


def per_device(embeddings, start_panel, tile_mask, inv_width):
    n_blk = lax.axis_size("blk")
    half, width = start_panel.shape
    size = half // 2
    sub_move = lambda v: lax.ppermute(v, "sub", [(0, 1), (1, 0)])
    blk_route = lambda v, to: lax.ppermute(v, "blk", [(i, to(i) % n_blk) for i in range(n_blk)])
    blk_move = lambda v, by: blk_route(v, lambda i: i + by)

    after = lambda v, *earlier: lax.optimization_barrier((v, *earlier))[0]
    sub = lax.axis_index("sub").astype(jnp.int32).reshape(1)
    wide = embeddings.shape[1] + width
    packed = lambda rows, lanes: jax.ShapeDtypeStruct((rows, lanes), BF16)
    above = blk_move(embeddings, -2)
    first, last, panel_mark = vmem_call(
        pack_body,
        (packed(size + MARK, wide), packed(size, wide), packed(half + MARK, width)),
        embeddings,
        start_panel,
        tile_mask,
        long=False,
    )
    relayed = n_blk == 8
    swapped = blk_route(last, lambda i: i ^ 1) if relayed else last
    above_panel = blk_move(panel_mark, -2)
    own = (first, last, sub_move(first), sub_move(last))
    image, turned = shape(half, width), shape(width, 2 * half)
    self_image = vmem_call(self_body, image, inv_width, sub, *own, scalars=2, long=False)
    below0 = blk_move(after(first, swapped, self_image), 1)
    swapped = after(swapped, self_image)
    below1 = blk_route(swapped, lambda i: i if i & 1 else i + 2) if relayed else blk_move(swapped, 1)
    above_image, back, above_sq = vmem_call(
        above_own_body, (image, turned, image), inv_width, sub, above, above_panel, *own, scalars=2
    )
    below0, below1 = after(below0, above_image, below1), after(below1, above_image, below0)
    below_other = (sub_move(below0), sub_move(below1))
    below_image0, back = vmem_call(
        below_first_body, (shape(size, width), turned), inv_width, sub, below0, *own, back, scalars=2
    )
    above_image, below_sum, below_cross = vmem_call(
        above_below_body,
        (image,) * 3,
        inv_width,
        sub,
        above,
        above_panel,
        above_sq,
        below0,
        below1,
        *below_other,
        after(above_image, below_image0),
        scalars=2,
    )
    below_image1, own_image, own_cross = vmem_call(
        below_last_body,
        (shape(size, width), image, image),
        inv_width,
        sub,
        below0,
        below1,
        *own,
        self_image,
        after(back, above_image),
        scalars=2,
    )
    above_image = blk_move(above_image, 2)
    below_image = jnp.concatenate([below_image0, below_image1], axis=0)
    below_image = blk_move(below_sum + sub_move(below_cross) + below_image, -1)
    image_rows, gram = vmem_call(
        gram_body, (image, shape(width, width)), own_image, sub_move(own_cross), below_image, above_image
    )
    if n_blk & (n_blk - 1):
        gram = lax.psum(gram, ("blk", "sub"))
    else:
        gram = gram + sub_move(gram)
        hop = 1
        while hop < n_blk:
            gram = gram + blk_route(gram, lambda i: i ^ hop)
            hop *= 2
    return vmem_call(basis_body, (image, shape(width, width)), image_rows, gram)


def solution(mesh):
    return jax.shard_map(
        per_device,
        mesh=mesh,
        in_specs=(
            P(("groups", "blk", "sub"), None),
            P(("groups", "blk", "sub"), None),
            P(("groups", "blk", "sub"), None),
            P(),
        ),
        out_specs=(P(("groups", "blk", "sub"), None), P("groups", None)),
        check_vma=False,
    )
```

```python
import jax
import jax.numpy as jnp
from jax import lax
from jax.experimental import pallas as pl
from jax.experimental.pallas import tpu as pltpu
from jax.sharding import PartitionSpec as P

TILE = 128
REACH = 3
F32 = jnp.float32
BF16 = jnp.bfloat16
HIGHEST = lax.Precision.HIGHEST


def vmem_call(body, out_shapes, *operands, scalars=0, long=True):
    in_vmem = pl.BlockSpec(memory_space=pltpu.VMEM)
    in_smem = pl.BlockSpec(memory_space=pltpu.SMEM)
    return pl.pallas_call(
        body,
        out_shape=out_shapes,
        in_specs=[in_smem] * scalars + [in_vmem] * (len(operands) - scalars),
        out_specs=jax.tree.map(lambda _: in_vmem, out_shapes),
        compiler_params=pltpu.CompilerParams(vmem_limit_bytes=24 << 20),
        cost_estimate=pl.CostEstimate(flops=10**11 if long else 1, transcendentals=0, bytes_accessed=1),
    )(*operands)


def shape(*dims):
    return jax.ShapeDtypeStruct(dims, F32)


def contract(a, b, dims, precision=None):
    return lax.dot_general(a, b, (dims, ((), ())), precision=precision, preferred_element_type=F32)


MARK = 8
OWN, BELOW, ABOVE = 0, 1, -2


def pair_mask(sub, rows, cols, offset, which):
    tiles = rows.shape[0]
    padded, lanes = rows.shape[1], tiles * TILE
    tile_of = lax.broadcasted_iota(jnp.int32, (padded, lanes), 1) // TILE
    first = (REACH + offset) * 2 * tiles + (sub if which == 0 else 1 - sub) * tiles
    chosen = (lax.broadcasted_iota(jnp.int32, (padded, lanes), 0) == first + tile_of).astype(F32)
    ahead = contract(rows, chosen, ((1,), (0,)))
    first = (REACH - offset) * 2 * tiles + sub * tiles
    row_at = lax.broadcasted_iota(jnp.int32, (tiles, padded), 0)
    chosen = (lax.broadcasted_iota(jnp.int32, (tiles, padded), 1) == first + row_at).astype(F32)
    spread = (lax.broadcasted_iota(jnp.int32, (tiles, lanes), 0) == tile_of[:tiles]).astype(F32)
    back = contract(contract(chosen, cols, ((1,), (1,))), spread, ((1,), (0,)))
    return jnp.concatenate([ahead, back], axis=0)


def marks(ref, half):
    return ref[ref.shape[0] - MARK :, ref.shape[1] - TILE :].astype(F32)[: half // TILE]


def pieces(*refs):
    size = min(r.shape[0] for r in refs)
    return [(r[:size, : r.shape[1] - TILE], r[:size, r.shape[1] - TILE :]) for r in refs]


def apart(features, panel):
    size = features.shape[0] // 2
    return [(features[rows], panel[rows]) for rows in (slice(0, size), slice(size, 2 * size))]


def squares(features):
    wide = features.astype(F32)
    return jnp.sum(wide * wide, axis=1, keepdims=True)


def as_row(column):
    return jnp.broadcast_to(column, (column.shape[0], TILE)).T[:1]


def as_column(row):
    return jnp.broadcast_to(row, (TILE, row.shape[1])).T[:, :1]


SPLIT = 3


def square_rows(ref):
    size = ref.shape[0] - MARK
    parts = ref[size:, : 2 * size].astype(F32)
    row = (parts[0:1] + parts[1:2]) + parts[2:3]
    return [row[:, :size], row[:, size:]]


def columns_of(own, other, sq_rows, masks):
    out = []
    for half, mask in zip((own, other), masks):
        for k, (features, panel) in enumerate(half):
            size = features.shape[0]
            out.append((features, panel, sq_rows[len(out)], mask[:, k * size : (k + 1) * size]))
    return out


def products(inverse, rows, squares_of, columns, back, first=0):
    panels = jnp.concatenate([panel for _, panel, _, _ in columns], axis=0)
    images = []
    for r, (features, panel) in enumerate(rows):
        size = features.shape[0]
        row_sq = squares_of[r]
        doubled = features * 2
        tile = (first + r) * size // TILE
        ahead, behind = [], []
        for other, _, col_sq, mask in columns:
            tiles = mask.shape[0] // 2
            gram2 = contract(doubled, other, ((1,), (1,)))
            kernel = jnp.exp(-inverse * jnp.maximum(row_sq + col_sq - gram2, 0.0))

            def masked(first):
                parts = [kernel[i * TILE : (i + 1) * TILE] * mask[first + i : first + i + 1] for i in range(size // TILE)]
                return jnp.concatenate(parts, axis=0).astype(BF16)

            ahead.append(masked(tile))
            if back is not None:
                behind.append(masked(tiles + tile))
        images.append(contract(jnp.concatenate(ahead, axis=1), panels, ((1,), (0,))))
        if back is not None:
            panel_t = panel.astype(F32).T.astype(BF16)
            back = back + contract(panel_t, jnp.concatenate(behind, axis=1), ((1,), (0,)))
    return jnp.concatenate(images, axis=0), back


def pack_body(embeddings, panel, tile_mask, first, last, panel_mark):
    half, features = embeddings.shape
    size = half // 2
    tiles, window = tile_mask.shape
    at = lax.broadcasted_iota(jnp.int32, (window, TILE), 0) == lax.broadcasted_iota(jnp.int32, (window, TILE), 1)
    mask = contract(tile_mask[...].astype(F32), at.astype(F32), ((1,), (0,)))
    mask = jnp.concatenate([mask, jnp.zeros((MARK - tiles, TILE), F32)], axis=0).astype(BF16)
    for ref, start in ((first, 0), (last, size)):
        ref[:size, :features] = embeddings[start : start + size]
        ref[:size, features:] = panel[start : start + size]
    row = as_row(jnp.concatenate([squares(r[:size, :features]) for r in (first, last)], axis=0))
    carried = []
    for _ in range(SPLIT):
        carried.append(row.astype(BF16).astype(F32))
        row = row - carried[-1]
    carried = jnp.concatenate(carried + [jnp.zeros((MARK - SPLIT, half), F32)], axis=0).astype(BF16)
    first[size:, :features] = jnp.concatenate([carried, jnp.zeros((MARK, features - half), BF16)], axis=1)
    first[size:, features:] = mask
    panel_mark[:half] = panel[...]
    panel_mark[half:] = mask


def place(numbers):
    return jnp.where(numbers[1] > 0.5, 1, 0)


def masks_of(sub, rows, others, offset):
    return [pair_mask(sub, rows, r, offset, h) for h, r in enumerate(others)]


def self_body(numbers, first, last, other_first, other_last, image):
    half = 2 * last.shape[0]
    own, other = pieces(first, last), pieces(other_first, other_last)
    rows = square_rows(first)
    both = [marks(r, half) for r in (first, other_first)]
    columns = columns_of(own, other, rows + square_rows(other_first), masks_of(place(numbers), both[0], both, OWN))
    image[...], _ = products(numbers[0], own, [as_column(r) for r in rows], columns, None)


def own_columns(sub, mark, first, last, other_first, other_last, offset):
    half = 2 * last.shape[0]
    masks = masks_of(sub, mark, [marks(r, half) for r in (first, other_first)], offset)
    rows = square_rows(first) + square_rows(other_first)
    return columns_of(pieces(first, last), pieces(other_first, other_last), rows, masks)


def above_own_body(numbers, above, panel, first, last, other_first, other_last, image, back, above_sq, kept_panel):
    half = above.shape[0]
    size = half // 2
    columns = own_columns(place(numbers), marks(panel, half), first, last, other_first, other_last, ABOVE)
    kept_panel[...] = panel[...]
    rows = apart(above, panel)
    columns_sq = [squares(features) for features, _ in rows]
    for k, column in enumerate(columns_sq):
        above_sq[k * size : (k + 1) * size] = jnp.broadcast_to(column, (size, TILE))
    image[...], back[...] = products(numbers[0], rows, columns_sq, columns, jnp.zeros(back.shape, F32))


def below_first_body(numbers, below, first, last, other_first, other_last, back, image, total):
    half = 2 * last.shape[0]
    columns = own_columns(place(numbers), marks(below, half), first, last, other_first, other_last, BELOW)
    rows_sq = [as_column(square_rows(below)[0])]
    image[...], total[...] = products(numbers[0], [pieces(below, last)[0]], rows_sq, columns, back[...])


def below_last_body(
    numbers, marked, below, first, last, other_first, other_last, self_image, back, image, own_image, own_cross
):
    half = 2 * last.shape[0]
    columns = own_columns(place(numbers), marks(marked, half), first, last, other_first, other_last, BELOW)
    rows_sq = [as_column(square_rows(marked)[1])]
    image[...], total = products(numbers[0], pieces(below), rows_sq, columns, back[...], 1)
    own_image[...] = self_image[...] + total[:, :half].T
    own_cross[...] = total[:, half:].T


def above_below_body(numbers, above, panel, above_sq, below0, below1, other0, other1, above_image, image, below_image, cross):
    half = image.shape[0]
    size = half // 2
    columns = own_columns(place(numbers), marks(panel, half), below0, below1, other0, other1, ABOVE - BELOW)
    rows_sq = [above_sq[k * size : (k + 1) * size, :1] for k in range(2)]
    products_image, total = products(numbers[0], apart(above, panel), rows_sq, columns, jnp.zeros((TILE, 2 * half), F32))
    image[...] = above_image[...] + products_image
    below_image[...] = total[:, :half].T
    cross[...] = total[:, half:].T


def gram_body(own, cross, below, above, image, gram):
    total = own[...] + cross[...] + below[...] + above[...]
    image[...] = total
    gram[...] = contract(total, total, ((0,), (0,)), HIGHEST)


GROUP = 8


def full(value):
    return jnp.broadcast_to(value, (GROUP, value.shape[1] if value.shape[1] > 1 else TILE))


def factor(gram, block):
    size = gram.shape[0]
    groups = size // GROUP
    upper = [gram[GROUP * r : GROUP * (r + 1)] for r in range(groups)]
    row = lax.broadcasted_iota(jnp.int32, (GROUP, size), 0)
    col = lax.broadcasted_iota(jnp.int32, (GROUP, size), 1)
    inverse = [jnp.where(col == row + GROUP * r, 1.0, 0.0).astype(F32) for r in range(groups)]
    for b in range(0, groups, block):
        if b:
            done_upper, done_inverse = jnp.concatenate(upper[:b], axis=0), jnp.concatenate(inverse[:b], axis=0)
            coefficients = done_upper[:, GROUP * b : GROUP * (b + block)]
            less_upper = contract(coefficients, done_upper, ((0,), (0,)), HIGHEST)
            less_inverse = contract(coefficients, done_inverse, ((0,), (0,)), HIGHEST)
            for k in range(block):
                upper[b + k] = upper[b + k] - less_upper[GROUP * k : GROUP * (k + 1)]
                inverse[b + k] = inverse[b + k] - less_inverse[GROUP * k : GROUP * (k + 1)]
        for r in range(b, b + block):
            lane = GROUP * r
            columns = [full(upper[r][:, lane + k : lane + k + 1]) for k in range(GROUP)]
            diag = [[full(columns[j][i : i + 1]) for j in range(i + 1)] for i in range(GROUP)]
            lower = [[None] * GROUP for _ in range(GROUP)]
            scale = [None] * GROUP
            for i in range(GROUP):
                scale[i] = lax.rsqrt(diag[i][i])
                for k in range(i + 1, GROUP):
                    lower[k][i] = diag[k][i] * scale[i]
                for k in range(i + 1, GROUP):
                    for j in range(i + 1, k + 1):
                        diag[k][j] = diag[k][j] - lower[k][i] * lower[j][i]
            u = [full(upper[r][i : i + 1]) for i in range(GROUP)]
            v = [full(inverse[r][i : i + 1]) for i in range(GROUP)]
            for i in range(GROUP):
                u[i], v[i] = u[i] * scale[i], v[i] * scale[i]
                for k in range(i + 1, GROUP):
                    u[k], v[k] = u[k] - lower[k][i] * u[i], v[k] - lower[k][i] * v[i]
            upper[r], inverse[r] = u[0], v[0]
            for i in range(1, GROUP):
                upper[r] = jnp.where(row == i, u[i], upper[r])
                inverse[r] = jnp.where(row == i, v[i], inverse[r])
            for later in range(r + 1, b + block):
                left = [full(upper[later][:, lane + k : lane + k + 1]) for k in range(GROUP)]
                for i in range(GROUP):
                    left[i] = left[i] * scale[i]
                    for k in range(i + 1, GROUP):
                        left[k] = left[k] - lower[k][i] * left[i]
                    upper[later] = upper[later] - left[i] * u[i]
                    inverse[later] = inverse[later] - left[i] * v[i]
    at_row = lax.broadcasted_iota(jnp.int32, (size, size), 0)
    at_col = lax.broadcasted_iota(jnp.int32, (size, size), 1)
    return jnp.where(at_col >= at_row, jnp.concatenate(upper, axis=0), 0.0), jnp.concatenate(inverse, axis=0)


def basis_body(image, gram, basis, upper):
    upper[...], inverse = factor(gram[...], 4)
    basis[...] = contract(image[...], inverse, ((1,), (1,)), HIGHEST)


def per_device(embeddings, start_panel, tile_mask, inv_width):
    n_blk = lax.axis_size("blk")
    half, width = start_panel.shape
    size = half // 2
    sub_move = lambda v: lax.ppermute(v, "sub", [(0, 1), (1, 0)])
    blk_route = lambda v, to: lax.ppermute(v, "blk", [(i, to(i) % n_blk) for i in range(n_blk)])
    blk_move = lambda v, by: blk_route(v, lambda i: i + by)

    after = lambda v, *earlier: lax.optimization_barrier((v, *earlier))[0]
    numbers = jnp.concatenate([inv_width, lax.axis_index("sub").astype(F32).reshape(1)])
    wide = embeddings.shape[1] + width
    packed = lambda rows, lanes: jax.ShapeDtypeStruct((rows, lanes), BF16)
    above = blk_move(embeddings, -2)
    first, last, panel_mark = vmem_call(
        pack_body,
        (packed(size + MARK, wide), packed(size, wide), packed(half + MARK, width)),
        embeddings,
        start_panel,
        tile_mask,
        long=False,
    )
    relayed = n_blk == 8
    swapped = blk_route(last, lambda i: i ^ 1) if relayed else last
    above_panel = blk_move(panel_mark, -2)
    own = (first, last, sub_move(first), sub_move(last))
    image, turned = shape(half, width), shape(width, 2 * half)
    self_image = vmem_call(self_body, image, numbers, *own, scalars=1, long=False)
    below0 = blk_move(after(first, swapped, self_image), 1)
    swapped = after(swapped, self_image)
    below1 = blk_route(swapped, lambda i: i if i & 1 else i + 2) if relayed else blk_move(swapped, 1)
    above_image, back, above_sq, above_panel = vmem_call(
        above_own_body,
        (image, turned, image, packed(half + MARK, width)),
        numbers,
        above,
        above_panel,
        *own,
        scalars=1,
    )
    below0, below1 = after(below0, above_image, below1), after(below1, above_image, below0)
    below_other = (sub_move(below0), sub_move(below1))
    below_image0, back = vmem_call(
        below_first_body, (shape(size, width), turned), numbers, below0, *own, back, scalars=1
    )
    above_image, below_sum, below_cross = vmem_call(
        above_below_body,
        (image,) * 3,
        numbers,
        above,
        above_panel,
        above_sq,
        below0,
        below1,
        *below_other,
        after(above_image, below_image0),
        scalars=1,
    )
    below_image1, own_image, own_cross = vmem_call(
        below_last_body,
        (shape(size, width), image, image),
        numbers,
        below0,
        below1,
        *own,
        self_image,
        after(back, above_image),
        scalars=1,
    )
    above_image = blk_move(above_image, 2)
    below_image = jnp.concatenate([below_image0, below_image1], axis=0)
    below_image = blk_move(below_sum + sub_move(below_cross) + below_image, -1)
    image_rows, gram = vmem_call(
        gram_body, (image, shape(width, width)), own_image, sub_move(own_cross), below_image, above_image
    )
    if n_blk & (n_blk - 1):
        gram = lax.psum(gram, ("blk", "sub"))
    else:
        gram = gram + sub_move(gram)
        hop = 1
        while hop < n_blk:
            gram = gram + blk_route(gram, lambda i: i ^ hop)
            hop *= 2
    return vmem_call(basis_body, (image, shape(width, width)), image_rows, gram)


def solution(mesh):
    return jax.shard_map(
        per_device,
        mesh=mesh,
        in_specs=(
            P(("groups", "blk", "sub"), None),
            P(("groups", "blk", "sub"), None),
            P(("groups", "blk", "sub"), None),
            P(),
        ),
        out_specs=(P(("groups", "blk", "sub"), None), P("groups", None)),
        check_vma=False,
    )
```

```python
import jax
import jax.numpy as jnp
from jax import lax
from jax.experimental import pallas as pl
from jax.experimental.pallas import tpu as pltpu
from jax.sharding import PartitionSpec as P

TILE = 128
REACH = 3
F32 = jnp.float32
BF16 = jnp.bfloat16
HIGHEST = lax.Precision.HIGHEST


def vmem_call(body, out_shapes, *operands, long=True):
    in_vmem = pl.BlockSpec(memory_space=pltpu.VMEM)
    return pl.pallas_call(
        body,
        out_shape=out_shapes,
        in_specs=[in_vmem] * len(operands),
        out_specs=jax.tree.map(lambda _: in_vmem, out_shapes),
        compiler_params=pltpu.CompilerParams(vmem_limit_bytes=24 << 20),
        cost_estimate=pl.CostEstimate(flops=10**11 if long else 1, transcendentals=0, bytes_accessed=1),
    )(*operands)


def shape(*dims):
    return jax.ShapeDtypeStruct(dims, F32)


def contract(a, b, dims, precision=None):
    return lax.dot_general(a, b, (dims, ((), ())), precision=precision, preferred_element_type=F32)


MARK = 8
OWN, BELOW, ABOVE = 0, 1, -2


def pair_mask(sub, rows, cols, offset, which):
    tiles = rows.shape[0]
    padded, lanes = rows.shape[1], tiles * TILE
    tile_of = lax.broadcasted_iota(jnp.int32, (padded, lanes), 1) // TILE
    first = (REACH + offset) * 2 * tiles + (sub if which == 0 else 1 - sub) * tiles
    chosen = (lax.broadcasted_iota(jnp.int32, (padded, lanes), 0) == first + tile_of).astype(F32)
    ahead = contract(rows, chosen, ((1,), (0,)))
    first = (REACH - offset) * 2 * tiles + sub * tiles
    row_at = lax.broadcasted_iota(jnp.int32, (tiles, padded), 0)
    chosen = (lax.broadcasted_iota(jnp.int32, (tiles, padded), 1) == first + row_at).astype(F32)
    spread = (lax.broadcasted_iota(jnp.int32, (tiles, lanes), 0) == tile_of[:tiles]).astype(F32)
    back = contract(contract(chosen, cols, ((1,), (1,))), spread, ((1,), (0,)))
    return jnp.concatenate([ahead, back], axis=0)


def marks(ref, half):
    return ref[ref.shape[0] - MARK :, ref.shape[1] - TILE :].astype(F32)[: half // TILE]


def pieces(*refs):
    size = min(r.shape[0] for r in refs)
    return [(r[:size, : r.shape[1] - TILE], r[:size, r.shape[1] - TILE :]) for r in refs]


def apart(features, panel):
    size = features.shape[0] // 2
    return [(features[rows], panel[rows]) for rows in (slice(0, size), slice(size, 2 * size))]


def squares(features):
    wide = features.astype(F32)
    return jnp.sum(wide * wide, axis=1, keepdims=True)


def as_row(column):
    return jnp.broadcast_to(column, (column.shape[0], TILE)).T[:1]


def as_column(row):
    return jnp.broadcast_to(row, (TILE, row.shape[1])).T[:, :1]


SPLIT = 3


def square_rows(ref):
    size = ref.shape[0] - MARK
    parts = ref[size:, : 2 * size].astype(F32)
    row = (parts[0:1] + parts[1:2]) + parts[2:3]
    return [row[:, :size], row[:, size:]]


def columns_of(own, other, sq_rows, masks):
    out = []
    for half, mask in zip((own, other), masks):
        for k, (features, panel) in enumerate(half):
            size = features.shape[0]
            out.append((features, panel, sq_rows[len(out)], mask[:, k * size : (k + 1) * size]))
    return out


def products(inverse, rows, squares_of, columns, back, first=0):
    panels = jnp.concatenate([panel for _, panel, _, _ in columns], axis=0)
    images = []
    for r, (features, panel) in enumerate(rows):
        size = features.shape[0]
        row_sq = squares_of[r]
        doubled = features * 2
        tile = (first + r) * size // TILE
        ahead, behind = [], []
        for other, _, col_sq, mask in columns:
            tiles = mask.shape[0] // 2
            gram2 = contract(doubled, other, ((1,), (1,)))
            kernel = jnp.exp(-inverse * jnp.maximum(row_sq + col_sq - gram2, 0.0))

            def masked(first):
                parts = [kernel[i * TILE : (i + 1) * TILE] * mask[first + i : first + i + 1] for i in range(size // TILE)]
                return jnp.concatenate(parts, axis=0).astype(BF16)

            ahead.append(masked(tile))
            if back is not None:
                behind.append(masked(tiles + tile))
        images.append(contract(jnp.concatenate(ahead, axis=1), panels, ((1,), (0,))))
        if back is not None:
            panel_t = panel.astype(F32).T.astype(BF16)
            back = back + contract(panel_t, jnp.concatenate(behind, axis=1), ((1,), (0,)))
    return jnp.concatenate(images, axis=0), back


def pack_body(embeddings, panel, tile_mask, first, last, panel_mark):
    half, features = embeddings.shape
    size = half // 2
    tiles, window = tile_mask.shape
    at = lax.broadcasted_iota(jnp.int32, (window, TILE), 0) == lax.broadcasted_iota(jnp.int32, (window, TILE), 1)
    mask = contract(tile_mask[...].astype(F32), at.astype(F32), ((1,), (0,)))
    mask = jnp.concatenate([mask, jnp.zeros((MARK - tiles, TILE), F32)], axis=0).astype(BF16)
    for ref, start in ((first, 0), (last, size)):
        ref[:size, :features] = embeddings[start : start + size]
        ref[:size, features:] = panel[start : start + size]
    row = as_row(jnp.concatenate([squares(r[:size, :features]) for r in (first, last)], axis=0))
    carried = []
    for _ in range(SPLIT):
        carried.append(row.astype(BF16).astype(F32))
        row = row - carried[-1]
    carried = jnp.concatenate(carried + [jnp.zeros((MARK - SPLIT, half), F32)], axis=0).astype(BF16)
    first[size:, :features] = jnp.concatenate([carried, jnp.zeros((MARK, features - half), BF16)], axis=1)
    first[size:, features:] = mask
    panel_mark[:half] = panel[...]
    panel_mark[half:] = mask


def width_of(numbers):
    return numbers[0:1, 0:1]


def place(numbers):
    return jnp.where(numbers[1:2, 0:1] > 0.5, 1, 0)


def masks_of(sub, rows, others, offset):
    return [pair_mask(sub, rows, r, offset, h) for h, r in enumerate(others)]


def self_body(numbers, first, last, other_first, other_last, image):
    half = 2 * last.shape[0]
    own, other = pieces(first, last), pieces(other_first, other_last)
    rows = square_rows(first)
    both = [marks(r, half) for r in (first, other_first)]
    columns = columns_of(own, other, rows + square_rows(other_first), masks_of(place(numbers), both[0], both, OWN))
    image[...], _ = products(width_of(numbers), own, [as_column(r) for r in rows], columns, None)


def own_columns(sub, mark, first, last, other_first, other_last, offset):
    half = 2 * last.shape[0]
    masks = masks_of(sub, mark, [marks(r, half) for r in (first, other_first)], offset)
    rows = square_rows(first) + square_rows(other_first)
    return columns_of(pieces(first, last), pieces(other_first, other_last), rows, masks)


def above_own_body(numbers, above, panel, first, last, other_first, other_last, image, back, above_sq, kept_panel):
    half = above.shape[0]
    size = half // 2
    columns = own_columns(place(numbers), marks(panel, half), first, last, other_first, other_last, ABOVE)
    kept_panel[...] = panel[...]
    rows = apart(above, panel)
    columns_sq = [squares(features) for features, _ in rows]
    for k, column in enumerate(columns_sq):
        above_sq[k * size : (k + 1) * size] = jnp.broadcast_to(column, (size, TILE))
    image[...], back[...] = products(width_of(numbers), rows, columns_sq, columns, jnp.zeros(back.shape, F32))


def below_first_body(numbers, below, first, last, other_first, other_last, back, image, total):
    half = 2 * last.shape[0]
    columns = own_columns(place(numbers), marks(below, half), first, last, other_first, other_last, BELOW)
    rows_sq = [as_column(square_rows(below)[0])]
    image[...], total[...] = products(width_of(numbers), [pieces(below, last)[0]], rows_sq, columns, back[...])


def below_last_body(
    numbers, marked, below, first, last, other_first, other_last, self_image, back, image, own_image, own_cross
):
    half = 2 * last.shape[0]
    columns = own_columns(place(numbers), marks(marked, half), first, last, other_first, other_last, BELOW)
    rows_sq = [as_column(square_rows(marked)[1])]
    image[...], total = products(width_of(numbers), pieces(below), rows_sq, columns, back[...], 1)
    own_image[...] = self_image[...] + total[:, :half].T
    own_cross[...] = total[:, half:].T


def above_below_body(numbers, above, panel, above_sq, below0, below1, other0, other1, above_image, image, below_image, cross):
    half = image.shape[0]
    size = half // 2
    columns = own_columns(place(numbers), marks(panel, half), below0, below1, other0, other1, ABOVE - BELOW)
    rows_sq = [above_sq[k * size : (k + 1) * size, :1] for k in range(2)]
    products_image, total = products(width_of(numbers), apart(above, panel), rows_sq, columns, jnp.zeros((TILE, 2 * half), F32))
    image[...] = above_image[...] + products_image
    below_image[...] = total[:, :half].T
    cross[...] = total[:, half:].T


def gram_body(own, cross, below, above, image, gram):
    total = own[...] + cross[...] + below[...] + above[...]
    image[...] = total
    gram[...] = contract(total, total, ((0,), (0,)), HIGHEST)


GROUP = 8


def full(value):
    return jnp.broadcast_to(value, (GROUP, value.shape[1] if value.shape[1] > 1 else TILE))


def factor(gram, block):
    size = gram.shape[0]
    groups = size // GROUP
    upper = [gram[GROUP * r : GROUP * (r + 1)] for r in range(groups)]
    row = lax.broadcasted_iota(jnp.int32, (GROUP, size), 0)
    col = lax.broadcasted_iota(jnp.int32, (GROUP, size), 1)
    inverse = [jnp.where(col == row + GROUP * r, 1.0, 0.0).astype(F32) for r in range(groups)]
    for b in range(0, groups, block):
        if b:
            done_upper, done_inverse = jnp.concatenate(upper[:b], axis=0), jnp.concatenate(inverse[:b], axis=0)
            coefficients = done_upper[:, GROUP * b : GROUP * (b + block)]
            less_upper = contract(coefficients, done_upper, ((0,), (0,)), HIGHEST)
            less_inverse = contract(coefficients, done_inverse, ((0,), (0,)), HIGHEST)
            for k in range(block):
                upper[b + k] = upper[b + k] - less_upper[GROUP * k : GROUP * (k + 1)]
                inverse[b + k] = inverse[b + k] - less_inverse[GROUP * k : GROUP * (k + 1)]
        for r in range(b, b + block):
            lane = GROUP * r
            columns = [full(upper[r][:, lane + k : lane + k + 1]) for k in range(GROUP)]
            diag = [[full(columns[j][i : i + 1]) for j in range(i + 1)] for i in range(GROUP)]
            lower = [[None] * GROUP for _ in range(GROUP)]
            scale = [None] * GROUP
            for i in range(GROUP):
                scale[i] = lax.rsqrt(diag[i][i])
                for k in range(i + 1, GROUP):
                    lower[k][i] = diag[k][i] * scale[i]
                for k in range(i + 1, GROUP):
                    for j in range(i + 1, k + 1):
                        diag[k][j] = diag[k][j] - lower[k][i] * lower[j][i]
            u = [full(upper[r][i : i + 1]) for i in range(GROUP)]
            v = [full(inverse[r][i : i + 1]) for i in range(GROUP)]
            for i in range(GROUP):
                u[i], v[i] = u[i] * scale[i], v[i] * scale[i]
                for k in range(i + 1, GROUP):
                    u[k], v[k] = u[k] - lower[k][i] * u[i], v[k] - lower[k][i] * v[i]
            upper[r], inverse[r] = u[0], v[0]
            for i in range(1, GROUP):
                upper[r] = jnp.where(row == i, u[i], upper[r])
                inverse[r] = jnp.where(row == i, v[i], inverse[r])
            for later in range(r + 1, b + block):
                left = [full(upper[later][:, lane + k : lane + k + 1]) for k in range(GROUP)]
                for i in range(GROUP):
                    left[i] = left[i] * scale[i]
                    for k in range(i + 1, GROUP):
                        left[k] = left[k] - lower[k][i] * left[i]
                    upper[later] = upper[later] - left[i] * u[i]
                    inverse[later] = inverse[later] - left[i] * v[i]
    at_row = lax.broadcasted_iota(jnp.int32, (size, size), 0)
    at_col = lax.broadcasted_iota(jnp.int32, (size, size), 1)
    return jnp.where(at_col >= at_row, jnp.concatenate(upper, axis=0), 0.0), jnp.concatenate(inverse, axis=0)


def basis_body(image, gram, basis, upper):
    upper[...], inverse = factor(gram[...], 4)
    basis[...] = contract(image[...], inverse, ((1,), (1,)), HIGHEST)


def per_device(embeddings, start_panel, tile_mask, inv_width):
    n_blk = lax.axis_size("blk")
    half, width = start_panel.shape
    size = half // 2
    sub_move = lambda v: lax.ppermute(v, "sub", [(0, 1), (1, 0)])
    blk_route = lambda v, to: lax.ppermute(v, "blk", [(i, to(i) % n_blk) for i in range(n_blk)])
    blk_move = lambda v, by: blk_route(v, lambda i: i + by)

    after = lambda v, *earlier: lax.optimization_barrier((v, *earlier))[0]
    numbers = jnp.concatenate([inv_width, lax.axis_index("sub").astype(F32).reshape(1)])
    numbers = jnp.broadcast_to(numbers[:, None], (2, TILE))
    wide = embeddings.shape[1] + width
    packed = lambda rows, lanes: jax.ShapeDtypeStruct((rows, lanes), BF16)
    above = blk_move(embeddings, -2)
    first, last, panel_mark = vmem_call(
        pack_body,
        (packed(size + MARK, wide), packed(size, wide), packed(half + MARK, width)),
        embeddings,
        start_panel,
        tile_mask,
        long=False,
    )
    relayed = n_blk == 8
    swapped = blk_route(last, lambda i: i ^ 1) if relayed else last
    above_panel = blk_move(panel_mark, -2)
    own = (first, last, sub_move(first), sub_move(last))
    image, turned = shape(half, width), shape(width, 2 * half)
    self_image = vmem_call(self_body, image, numbers, *own, long=False)
    below0 = blk_move(after(first, swapped, self_image), 1)
    swapped = after(swapped, self_image)
    below1 = blk_route(swapped, lambda i: i if i & 1 else i + 2) if relayed else blk_move(swapped, 1)
    above_image, back, above_sq, above_panel = vmem_call(
        above_own_body,
        (image, turned, image, packed(half + MARK, width)),
        numbers,
        above,
        above_panel,
        *own,
    )
    below0, below1 = after(below0, above_image, below1), after(below1, above_image, below0)
    below_other = (sub_move(below0), sub_move(below1))
    below_image0, back = vmem_call(
        below_first_body, (shape(size, width), turned), numbers, below0, *own, back
    )
    above_image, below_sum, below_cross = vmem_call(
        above_below_body,
        (image,) * 3,
        numbers,
        above,
        above_panel,
        above_sq,
        below0,
        below1,
        *below_other,
        after(above_image, below_image0),
    )
    below_image1, own_image, own_cross = vmem_call(
        below_last_body,
        (shape(size, width), image, image),
        numbers,
        below0,
        below1,
        *own,
        self_image,
        after(back, above_image),
    )
    above_image = blk_move(above_image, 2)
    below_image = jnp.concatenate([below_image0, below_image1], axis=0)
    below_image = blk_move(below_sum + sub_move(below_cross) + below_image, -1)
    image_rows, gram = vmem_call(
        gram_body, (image, shape(width, width)), own_image, sub_move(own_cross), below_image, above_image
    )
    if n_blk & (n_blk - 1):
        gram = lax.psum(gram, ("blk", "sub"))
    else:
        gram = gram + sub_move(gram)
        hop = 1
        while hop < n_blk:
            gram = gram + blk_route(gram, lambda i: i ^ hop)
            hop *= 2
    return vmem_call(basis_body, (image, shape(width, width)), image_rows, gram)


def solution(mesh):
    return jax.shard_map(
        per_device,
        mesh=mesh,
        in_specs=(
            P(("groups", "blk", "sub"), None),
            P(("groups", "blk", "sub"), None),
            P(("groups", "blk", "sub"), None),
            P(),
        ),
        out_specs=(P(("groups", "blk", "sub"), None), P("groups", None)),
        check_vma=False,
    )
```

```python
import jax
import jax.numpy as jnp
from jax import lax
from jax.experimental import pallas as pl
from jax.experimental.pallas import tpu as pltpu
from jax.sharding import PartitionSpec as P

TILE = 128
REACH = 3
F32 = jnp.float32
BF16 = jnp.bfloat16
HIGHEST = lax.Precision.HIGHEST


def vmem_call(body, out_shapes, *operands, long=True):
    in_vmem = pl.BlockSpec(memory_space=pltpu.VMEM)
    return pl.pallas_call(
        body,
        out_shape=out_shapes,
        in_specs=[in_vmem] * len(operands),
        out_specs=jax.tree.map(lambda _: in_vmem, out_shapes),
        compiler_params=pltpu.CompilerParams(vmem_limit_bytes=24 << 20),
        cost_estimate=pl.CostEstimate(flops=10**11 if long else 1, transcendentals=0, bytes_accessed=1),
    )(*operands)


def shape(*dims):
    return jax.ShapeDtypeStruct(dims, F32)


def contract(a, b, dims, precision=None):
    return lax.dot_general(a, b, (dims, ((), ())), precision=precision, preferred_element_type=F32)


MARK = 8
OWN, BELOW, ABOVE = 0, 1, -2


def pair_mask(sub, rows, cols, offset, which):
    tiles = rows.shape[0]
    padded, lanes = rows.shape[1], tiles * TILE
    tile_of = lax.broadcasted_iota(jnp.int32, (padded, lanes), 1) // TILE
    first = (REACH + offset) * 2 * tiles + (sub if which == 0 else 1 - sub) * tiles
    chosen = (lax.broadcasted_iota(jnp.int32, (padded, lanes), 0) == first + tile_of).astype(F32)
    ahead = contract(rows, chosen, ((1,), (0,)))
    first = (REACH - offset) * 2 * tiles + sub * tiles
    row_at = lax.broadcasted_iota(jnp.int32, (tiles, padded), 0)
    chosen = (lax.broadcasted_iota(jnp.int32, (tiles, padded), 1) == first + row_at).astype(F32)
    spread = (lax.broadcasted_iota(jnp.int32, (tiles, lanes), 0) == tile_of[:tiles]).astype(F32)
    back = contract(contract(chosen, cols, ((1,), (1,))), spread, ((1,), (0,)))
    return jnp.concatenate([ahead, back], axis=0)


def marks(ref, half):
    return ref[ref.shape[0] - MARK :, ref.shape[1] - TILE :].astype(F32)[: half // TILE]


def pieces(*refs):
    size = min(r.shape[0] for r in refs)
    return [(r[:size, : r.shape[1] - TILE], r[:size, r.shape[1] - TILE :]) for r in refs]


def apart(features, panel):
    size = features.shape[0] // 2
    return [(features[rows], panel[rows]) for rows in (slice(0, size), slice(size, 2 * size))]


def squares(features):
    wide = features.astype(F32)
    return jnp.sum(wide * wide, axis=1, keepdims=True)


def as_row(column):
    return jnp.broadcast_to(column, (column.shape[0], TILE)).T[:1]


def as_column(row):
    return jnp.broadcast_to(row, (TILE, row.shape[1])).T[:, :1]


SPLIT = 3


def square_rows(ref):
    size = ref.shape[0] - MARK
    parts = ref[size:, : 2 * size].astype(F32)
    row = (parts[0:1] + parts[1:2]) + parts[2:3]
    return [row[:, :size], row[:, size:]]


def columns_of(own, other, sq_rows, masks):
    out = []
    for half, mask in zip((own, other), masks):
        for k, (features, panel) in enumerate(half):
            size = features.shape[0]
            out.append((features, panel, sq_rows[len(out)], mask[:, k * size : (k + 1) * size]))
    return out


def products(inverse, rows, squares_of, columns, back, first=0):
    panels = jnp.concatenate([panel for _, panel, _, _ in columns], axis=0)
    images = []
    for r, (features, panel) in enumerate(rows):
        size = features.shape[0]
        row_sq = squares_of[r]
        doubled = features * 2
        tile = (first + r) * size // TILE
        ahead, behind = [], []
        for other, _, col_sq, mask in columns:
            tiles = mask.shape[0] // 2
            gram2 = contract(doubled, other, ((1,), (1,)))
            kernel = jnp.exp(-inverse * jnp.maximum(row_sq + col_sq - gram2, 0.0))

            def masked(first):
                parts = [kernel[i * TILE : (i + 1) * TILE] * mask[first + i : first + i + 1] for i in range(size // TILE)]
                return jnp.concatenate(parts, axis=0).astype(BF16)

            ahead.append(masked(tile))
            if back is not None:
                behind.append(masked(tiles + tile))
        images.append(contract(jnp.concatenate(ahead, axis=1), panels, ((1,), (0,))))
        if back is not None:
            panel_t = panel.astype(F32).T.astype(BF16)
            back = back + contract(panel_t, jnp.concatenate(behind, axis=1), ((1,), (0,)))
    return jnp.concatenate(images, axis=0), back


def pack_body(embeddings, panel, tile_mask, first, last, panel_mark):
    half, features = embeddings.shape
    size = half // 2
    tiles, window = tile_mask.shape
    at = lax.broadcasted_iota(jnp.int32, (window, TILE), 0) == lax.broadcasted_iota(jnp.int32, (window, TILE), 1)
    mask = contract(tile_mask[...].astype(F32), at.astype(F32), ((1,), (0,)))
    mask = jnp.concatenate([mask, jnp.zeros((MARK - tiles, TILE), F32)], axis=0).astype(BF16)
    for ref, start in ((first, 0), (last, size)):
        ref[:size, :features] = embeddings[start : start + size]
        ref[:size, features:] = panel[start : start + size]
    row = as_row(jnp.concatenate([squares(r[:size, :features]) for r in (first, last)], axis=0))
    carried = []
    for _ in range(SPLIT):
        carried.append(row.astype(BF16).astype(F32))
        row = row - carried[-1]
    carried = jnp.concatenate(carried + [jnp.zeros((MARK - SPLIT, half), F32)], axis=0).astype(BF16)
    first[size:, :features] = jnp.concatenate([carried, jnp.zeros((MARK, features - half), BF16)], axis=1)
    first[size:, features:] = mask
    panel_mark[:half] = panel[...]
    panel_mark[half:] = mask


def width_of(numbers):
    return numbers[0:1, 0:1]


def place(numbers):
    return jnp.where(numbers[1:2, 0:1] > 0.5, 1, 0)


def masks_of(sub, rows, others, offset):
    return [pair_mask(sub, rows, r, offset, h) for h, r in enumerate(others)]


def self_body(numbers, first, last, other_first, other_last, image):
    half = 2 * last.shape[0]
    own, other = pieces(first, last), pieces(other_first, other_last)
    rows = square_rows(first)
    both = [marks(r, half) for r in (first, other_first)]
    columns = columns_of(own, other, rows + square_rows(other_first), masks_of(place(numbers), both[0], both, OWN))
    image[...], _ = products(width_of(numbers), own, [as_column(r) for r in rows], columns, None)


def own_columns(sub, mark, first, last, other_first, other_last, offset):
    half = 2 * last.shape[0]
    masks = masks_of(sub, mark, [marks(r, half) for r in (first, other_first)], offset)
    rows = square_rows(first) + square_rows(other_first)
    return columns_of(pieces(first, last), pieces(other_first, other_last), rows, masks)


def above_own_body(numbers, above, panel, first, last, other_first, other_last, image, back, above_sq, kept_panel):
    half = above.shape[0]
    size = half // 2
    columns = own_columns(place(numbers), marks(panel, half), first, last, other_first, other_last, ABOVE)
    kept_panel[...] = panel[...]
    rows = apart(above, panel)
    columns_sq = [squares(features) for features, _ in rows]
    for k, column in enumerate(columns_sq):
        above_sq[k * size : (k + 1) * size] = jnp.broadcast_to(column, (size, TILE))
    image[...], back[...] = products(width_of(numbers), rows, columns_sq, columns, jnp.zeros(back.shape, F32))


def below_first_body(numbers, below, first, last, other_first, other_last, back, image, total):
    half = 2 * last.shape[0]
    columns = own_columns(place(numbers), marks(below, half), first, last, other_first, other_last, BELOW)
    rows_sq = [as_column(square_rows(below)[0])]
    image[...], total[...] = products(width_of(numbers), [pieces(below, last)[0]], rows_sq, columns, back[...])


def below_last_body(
    numbers, marked, below, first, last, other_first, other_last, self_image, back, image, own_image, own_cross
):
    half = 2 * last.shape[0]
    columns = own_columns(place(numbers), marks(marked, half), first, last, other_first, other_last, BELOW)
    rows_sq = [as_column(square_rows(marked)[1])]
    image[...], total = products(width_of(numbers), pieces(below), rows_sq, columns, back[...], 1)
    own_image[...] = self_image[...] + total[:, :half].T
    own_cross[...] = total[:, half:].T


def above_below_body(numbers, above, panel, above_sq, below0, below1, other0, other1, above_image, image, below_image, cross):
    half = image.shape[0]
    size = half // 2
    columns = own_columns(place(numbers), marks(panel, half), below0, below1, other0, other1, ABOVE - BELOW)
    rows_sq = [above_sq[k * size : (k + 1) * size, :1] for k in range(2)]
    products_image, total = products(width_of(numbers), apart(above, panel), rows_sq, columns, jnp.zeros((TILE, 2 * half), F32))
    image[...] = above_image[...] + products_image
    below_image[...] = total[:, :half].T
    cross[...] = total[:, half:].T


def gram_body(own, cross, below, *refs):
    *above, image, gram = refs
    total = own[...] + cross[...] + below[...]
    for part in above:
        total = total + part[...]
    image[...] = total
    gram[...] = contract(total, total, ((0,), (0,)), HIGHEST)


GROUP = 8


def full(value):
    return jnp.broadcast_to(value, (GROUP, value.shape[1] if value.shape[1] > 1 else TILE))


def factor(gram, block):
    size = gram.shape[0]
    groups = size // GROUP
    upper = [gram[GROUP * r : GROUP * (r + 1)] for r in range(groups)]
    row = lax.broadcasted_iota(jnp.int32, (GROUP, size), 0)
    col = lax.broadcasted_iota(jnp.int32, (GROUP, size), 1)
    inverse = [jnp.where(col == row + GROUP * r, 1.0, 0.0).astype(F32) for r in range(groups)]
    for b in range(0, groups, block):
        if b:
            done_upper, done_inverse = jnp.concatenate(upper[:b], axis=0), jnp.concatenate(inverse[:b], axis=0)
            coefficients = done_upper[:, GROUP * b : GROUP * (b + block)]
            less_upper = contract(coefficients, done_upper, ((0,), (0,)), HIGHEST)
            less_inverse = contract(coefficients, done_inverse, ((0,), (0,)), HIGHEST)
            for k in range(block):
                upper[b + k] = upper[b + k] - less_upper[GROUP * k : GROUP * (k + 1)]
                inverse[b + k] = inverse[b + k] - less_inverse[GROUP * k : GROUP * (k + 1)]
        for r in range(b, b + block):
            lane = GROUP * r
            columns = [full(upper[r][:, lane + k : lane + k + 1]) for k in range(GROUP)]
            diag = [[full(columns[j][i : i + 1]) for j in range(i + 1)] for i in range(GROUP)]
            lower = [[None] * GROUP for _ in range(GROUP)]
            scale = [None] * GROUP
            for i in range(GROUP):
                scale[i] = lax.rsqrt(diag[i][i])
                for k in range(i + 1, GROUP):
                    lower[k][i] = diag[k][i] * scale[i]
                for k in range(i + 1, GROUP):
                    for j in range(i + 1, k + 1):
                        diag[k][j] = diag[k][j] - lower[k][i] * lower[j][i]
            u = [full(upper[r][i : i + 1]) for i in range(GROUP)]
            v = [full(inverse[r][i : i + 1]) for i in range(GROUP)]
            for i in range(GROUP):
                u[i], v[i] = u[i] * scale[i], v[i] * scale[i]
                for k in range(i + 1, GROUP):
                    u[k], v[k] = u[k] - lower[k][i] * u[i], v[k] - lower[k][i] * v[i]
            upper[r], inverse[r] = u[0], v[0]
            for i in range(1, GROUP):
                upper[r] = jnp.where(row == i, u[i], upper[r])
                inverse[r] = jnp.where(row == i, v[i], inverse[r])
            for later in range(r + 1, b + block):
                left = [full(upper[later][:, lane + k : lane + k + 1]) for k in range(GROUP)]
                for i in range(GROUP):
                    left[i] = left[i] * scale[i]
                    for k in range(i + 1, GROUP):
                        left[k] = left[k] - lower[k][i] * left[i]
                    upper[later] = upper[later] - left[i] * u[i]
                    inverse[later] = inverse[later] - left[i] * v[i]
    at_row = lax.broadcasted_iota(jnp.int32, (size, size), 0)
    at_col = lax.broadcasted_iota(jnp.int32, (size, size), 1)
    return jnp.where(at_col >= at_row, jnp.concatenate(upper, axis=0), 0.0), jnp.concatenate(inverse, axis=0)


def basis_body(image, gram, basis, upper):
    upper[...], inverse = factor(gram[...], 4)
    basis[...] = contract(image[...], inverse, ((1,), (1,)), HIGHEST)


def per_device(embeddings, start_panel, tile_mask, inv_width):
    n_blk = lax.axis_size("blk")
    half, width = start_panel.shape
    size = half // 2
    sub_move = lambda v: lax.ppermute(v, "sub", [(0, 1), (1, 0)])
    blk_route = lambda v, to: lax.ppermute(v, "blk", [(i, to(i) % n_blk) for i in range(n_blk)])
    blk_move = lambda v, by: blk_route(v, lambda i: i + by)

    after = lambda v, *earlier: lax.optimization_barrier((v, *earlier))[0]
    numbers = jnp.concatenate([inv_width, lax.axis_index("sub").astype(F32).reshape(1)])
    numbers = jnp.broadcast_to(numbers[:, None], (2, TILE))
    wide = embeddings.shape[1] + width
    packed = lambda rows, lanes: jax.ShapeDtypeStruct((rows, lanes), BF16)
    above = blk_move(embeddings, -2)
    first, last, panel_mark = vmem_call(
        pack_body,
        (packed(size + MARK, wide), packed(size, wide), packed(half + MARK, width)),
        embeddings,
        start_panel,
        tile_mask,
        long=False,
    )
    relayed = n_blk == 8
    swapped = blk_route(last, lambda i: i ^ 1) if relayed else last
    above_panel = blk_move(panel_mark, -2)
    own = (first, last, sub_move(first), sub_move(last))
    image, turned = shape(half, width), shape(width, 2 * half)
    self_image = vmem_call(self_body, image, numbers, *own, long=False)
    below0 = blk_move(after(first, swapped, self_image), 1)
    swapped = after(swapped, self_image)
    below1 = blk_route(swapped, lambda i: i if i & 1 else i + 2) if relayed else blk_move(swapped, 1)
    above_image, back, above_sq, above_panel = vmem_call(
        above_own_body,
        (image, turned, image, packed(half + MARK, width)),
        numbers,
        above,
        above_panel,
        *own,
    )
    below0, below1 = after(below0, above_image, below1), after(below1, above_image, below0)
    below_other = (sub_move(below0), sub_move(below1))
    below_image0, back = vmem_call(
        below_first_body, (shape(size, width), turned), numbers, below0, *own, back
    )
    above_image, below_sum, below_cross = vmem_call(
        above_below_body,
        (image,) * 3,
        numbers,
        above,
        above_panel,
        above_sq,
        below0,
        below1,
        *below_other,
        after(above_image, below_image0),
    )
    below_image1, own_image, own_cross = vmem_call(
        below_last_body,
        (shape(size, width), image, image),
        numbers,
        below0,
        below1,
        *own,
        self_image,
        after(back, above_image),
    )
    if relayed:
        pair_route = lambda v, pairs: lax.ppermute(v, ("blk", "sub"), [((a[0] % n_blk) * 2 + a[1], (b[0] % n_blk) * 2 + b[1]) for a, b in pairs])
        aside = [i for i in range(n_blk) if not i & 1]
        straight = [((i, s), (i + 2, s)) for i in range(n_blk) for s in range(2) if i & 1 or s == 0]
        turned_aside = pair_route(above_image, [((i, 1), (i + 1, 1)) for i in aside])
        turned_aside = pair_route(turned_aside, [((i + 1, 1), (i + 2, 1)) for i in aside])
        above_parts = (pair_route(above_image, straight), turned_aside)
    else:
        above_parts = (blk_move(above_image, 2),)
    below_image = jnp.concatenate([below_image0, below_image1], axis=0)
    below_image = blk_move(below_sum + sub_move(below_cross) + below_image, -1)
    image_rows, gram = vmem_call(
        gram_body, (image, shape(width, width)), own_image, sub_move(own_cross), below_image, *above_parts
    )
    if n_blk & (n_blk - 1):
        gram = lax.psum(gram, ("blk", "sub"))
    else:
        gram = gram + sub_move(gram)
        hop = 1
        while hop < n_blk:
            gram = gram + blk_route(gram, lambda i: i ^ hop)
            hop *= 2
    return vmem_call(basis_body, (image, shape(width, width)), image_rows, gram)


def solution(mesh):
    return jax.shard_map(
        per_device,
        mesh=mesh,
        in_specs=(
            P(("groups", "blk", "sub"), None),
            P(("groups", "blk", "sub"), None),
            P(("groups", "blk", "sub"), None),
            P(),
        ),
        out_specs=(P(("groups", "blk", "sub"), None), P("groups", None)),
        check_vma=False,
    )
```

```python
import jax
import jax.numpy as jnp
from jax import lax
from jax.experimental import pallas as pl
from jax.experimental.pallas import tpu as pltpu
from jax.sharding import PartitionSpec as P

TILE = 128
REACH = 3
F32 = jnp.float32
BF16 = jnp.bfloat16
HIGHEST = lax.Precision.HIGHEST


def vmem_call(body, out_shapes, *operands, long=True):
    in_vmem = pl.BlockSpec(memory_space=pltpu.VMEM)
    return pl.pallas_call(
        body,
        out_shape=out_shapes,
        in_specs=[in_vmem] * len(operands),
        out_specs=jax.tree.map(lambda _: in_vmem, out_shapes),
        compiler_params=pltpu.CompilerParams(vmem_limit_bytes=24 << 20),
        cost_estimate=pl.CostEstimate(flops=10**11 if long else 1, transcendentals=0, bytes_accessed=1),
    )(*operands)


def shape(*dims):
    return jax.ShapeDtypeStruct(dims, F32)


def contract(a, b, dims, precision=None):
    return lax.dot_general(a, b, (dims, ((), ())), precision=precision, preferred_element_type=F32)


MARK = 8
OWN, BELOW, ABOVE = 0, 1, -2


def pair_mask(sub, rows, cols, offset, which):
    tiles = rows.shape[0]
    padded, lanes = rows.shape[1], tiles * TILE
    tile_of = lax.broadcasted_iota(jnp.int32, (padded, lanes), 1) // TILE
    first = (REACH + offset) * 2 * tiles + (sub if which == 0 else 1 - sub) * tiles
    chosen = (lax.broadcasted_iota(jnp.int32, (padded, lanes), 0) == first + tile_of).astype(F32)
    ahead = contract(rows, chosen, ((1,), (0,)))
    first = (REACH - offset) * 2 * tiles + sub * tiles
    row_at = lax.broadcasted_iota(jnp.int32, (tiles, padded), 0)
    chosen = (lax.broadcasted_iota(jnp.int32, (tiles, padded), 1) == first + row_at).astype(F32)
    spread = (lax.broadcasted_iota(jnp.int32, (tiles, lanes), 0) == tile_of[:tiles]).astype(F32)
    back = contract(contract(chosen, cols, ((1,), (1,))), spread, ((1,), (0,)))
    return jnp.concatenate([ahead, back], axis=0)


def marks(ref, half):
    return ref[ref.shape[0] - MARK :, ref.shape[1] - TILE :].astype(F32)[: half // TILE]


def pieces(*refs):
    size = min(r.shape[0] for r in refs)
    return [(r[:size, : r.shape[1] - TILE], r[:size, r.shape[1] - TILE :]) for r in refs]


def apart(features, panel):
    size = features.shape[0] // 2
    return [(features[rows], panel[rows]) for rows in (slice(0, size), slice(size, 2 * size))]


def squares(features):
    wide = features.astype(F32)
    return jnp.sum(wide * wide, axis=1, keepdims=True)


def as_row(column):
    return jnp.broadcast_to(column, (column.shape[0], TILE)).T[:1]


def as_column(row):
    return jnp.broadcast_to(row, (TILE, row.shape[1])).T[:, :1]


SPLIT = 3


def square_rows(ref):
    size = ref.shape[0] - MARK
    parts = ref[size:, : 2 * size].astype(F32)
    row = (parts[0:1] + parts[1:2]) + parts[2:3]
    return [row[:, :size], row[:, size:]]


def columns_of(own, other, sq_rows, masks):
    out = []
    for half, mask in zip((own, other), masks):
        for k, (features, panel) in enumerate(half):
            size = features.shape[0]
            out.append((features, panel, sq_rows[len(out)], mask[:, k * size : (k + 1) * size]))
    return out


def products(inverse, rows, squares_of, columns, back, first=0):
    panels = jnp.concatenate([panel for _, panel, _, _ in columns], axis=0)
    images = []
    for r, (features, panel) in enumerate(rows):
        size = features.shape[0]
        row_sq = squares_of[r]
        doubled = features * 2
        tile = (first + r) * size // TILE
        ahead, behind = [], []
        for other, _, col_sq, mask in columns:
            tiles = mask.shape[0] // 2
            gram2 = contract(doubled, other, ((1,), (1,)))
            kernel = jnp.exp(-inverse * jnp.maximum(row_sq + col_sq - gram2, 0.0))

            def masked(first):
                parts = [kernel[i * TILE : (i + 1) * TILE] * mask[first + i : first + i + 1] for i in range(size // TILE)]
                return jnp.concatenate(parts, axis=0).astype(BF16)

            ahead.append(masked(tile))
            if back is not None:
                behind.append(masked(tiles + tile))
        images.append(contract(jnp.concatenate(ahead, axis=1), panels, ((1,), (0,))))
        if back is not None:
            panel_t = panel.astype(F32).T.astype(BF16)
            back = back + contract(panel_t, jnp.concatenate(behind, axis=1), ((1,), (0,)))
    return jnp.concatenate(images, axis=0), back


def pack_body(embeddings, panel, tile_mask, first, last, panel_mark):
    half, features = embeddings.shape
    size = half // 2
    tiles, window = tile_mask.shape
    at = lax.broadcasted_iota(jnp.int32, (window, TILE), 0) == lax.broadcasted_iota(jnp.int32, (window, TILE), 1)
    mask = contract(tile_mask[...].astype(F32), at.astype(F32), ((1,), (0,)))
    mask = jnp.concatenate([mask, jnp.zeros((MARK - tiles, TILE), F32)], axis=0).astype(BF16)
    for ref, start in ((first, 0), (last, size)):
        ref[:size, :features] = embeddings[start : start + size]
        ref[:size, features:] = panel[start : start + size]
    row = as_row(jnp.concatenate([squares(r[:size, :features]) for r in (first, last)], axis=0))
    carried = []
    for _ in range(SPLIT):
        carried.append(row.astype(BF16).astype(F32))
        row = row - carried[-1]
    carried = jnp.concatenate(carried + [jnp.zeros((MARK - SPLIT, half), F32)], axis=0).astype(BF16)
    last[size:, :features] = jnp.concatenate([carried, jnp.zeros((MARK, features - half), BF16)], axis=1)
    last[size:, features:] = mask
    panel_mark[:half] = panel[...]
    panel_mark[half:] = mask


def width_of(numbers):
    return numbers[0:1, 0:1]


def place(numbers):
    return jnp.where(numbers[1:2, 0:1] > 0.5, 1, 0)


def masks_of(sub, rows, others, offset):
    return [pair_mask(sub, rows, r, offset, h) for h, r in enumerate(others)]


def self_body(numbers, first, last, other_first, other_last, image):
    half = 2 * first.shape[0]
    own, other = pieces(first, last), pieces(other_first, other_last)
    rows = square_rows(last)
    both = [marks(r, half) for r in (last, other_last)]
    columns = columns_of(own, other, rows + square_rows(other_last), masks_of(place(numbers), both[0], both, OWN))
    image[...], _ = products(width_of(numbers), own, [as_column(r) for r in rows], columns, None)


def own_columns(place_here, mark, first, last, other_first, other_last, offset):
    half = 2 * first.shape[0]
    masks = masks_of(place_here, mark, [marks(r, half) for r in (last, other_last)], offset)
    rows = square_rows(last) + square_rows(other_last)
    return columns_of(pieces(first, last), pieces(other_first, other_last), rows, masks)


def above_own_body(numbers, above, panel, first, last, other_first, other_last, image, back, above_sq, kept_panel):
    half = above.shape[0]
    size = half // 2
    columns = own_columns(place(numbers), marks(panel, half), first, last, other_first, other_last, ABOVE)
    kept_panel[...] = panel[...]
    rows = apart(above, panel)
    columns_sq = [squares(features) for features, _ in rows]
    for k, column in enumerate(columns_sq):
        above_sq[k * size : (k + 1) * size] = jnp.broadcast_to(column, (size, TILE))
    image[...], back[...] = products(width_of(numbers), rows, columns_sq, columns, jnp.zeros(back.shape, F32))


def below_last_body(numbers, below, first, last, other_first, other_last, back, image, total):
    half = 2 * first.shape[0]
    columns = own_columns(place(numbers), marks(below, half), first, last, other_first, other_last, BELOW)
    rows_sq = [as_column(square_rows(below)[1])]
    image[...], total[...] = products(width_of(numbers), [pieces(below, first)[0]], rows_sq, columns, back[...], 1)


def below_first_body(
    numbers, marked, below, first, last, other_first, other_last, self_image, back, image, own_image, own_cross
):
    half = 2 * first.shape[0]
    columns = own_columns(place(numbers), marks(marked, half), first, last, other_first, other_last, BELOW)
    rows_sq = [as_column(square_rows(marked)[0])]
    image[...], total = products(width_of(numbers), pieces(below), rows_sq, columns, back[...])
    own_image[...] = self_image[...] + total[:, :half].T
    own_cross[...] = total[:, half:].T


def above_below(part, numbers, above, panel, above_sq, marked, other_marked, below, other, above_image, image, below_image, cross):
    half = image.shape[0]
    size = half // 2
    masks = masks_of(place(numbers), marks(panel, half), [marks(r, half) for r in (marked, other_marked)], ABOVE - BELOW)
    masks = [mask[:, part * size : (part + 1) * size] for mask in masks]
    columns_sq = [square_rows(r)[part] for r in (marked, other_marked)]
    columns = columns_of([(below[:size, :-TILE], below[:size, -TILE:])], [(other[:size, :-TILE], other[:size, -TILE:])], columns_sq, masks)
    rows_sq = [above_sq[k * size : (k + 1) * size, :1] for k in range(2)]
    products_image, total = products(width_of(numbers), apart(above, panel), rows_sq, columns, jnp.zeros((TILE, half), F32))
    image[...] = above_image[...] + products_image
    below_image[...] = total[:, :size].T
    cross[...] = total[:, size:].T


def above_below_last_body(numbers, above, panel, above_sq, below, other, above_image, *outs):
    above_below(1, numbers, above, panel, above_sq, below, other, below, other, above_image, *outs)


def above_below_first_body(numbers, above, panel, above_sq, marked, other_marked, below, other, above_image, *outs):
    above_below(0, numbers, above, panel, above_sq, marked, other_marked, below, other, above_image, *outs)


def gram_body(own, cross, below, above, image, gram):
    total = own[...] + cross[...] + below[...] + above[...]
    image[...] = total
    gram[...] = contract(total, total, ((0,), (0,)), HIGHEST)


GROUP = 8


def full(value):
    return jnp.broadcast_to(value, (GROUP, value.shape[1] if value.shape[1] > 1 else TILE))


def factor(gram, block):
    size = gram.shape[0]
    groups = size // GROUP
    upper = [gram[GROUP * r : GROUP * (r + 1)] for r in range(groups)]
    row = lax.broadcasted_iota(jnp.int32, (GROUP, size), 0)
    col = lax.broadcasted_iota(jnp.int32, (GROUP, size), 1)
    inverse = [jnp.where(col == row + GROUP * r, 1.0, 0.0).astype(F32) for r in range(groups)]
    for b in range(0, groups, block):
        if b:
            done_upper, done_inverse = jnp.concatenate(upper[:b], axis=0), jnp.concatenate(inverse[:b], axis=0)
            coefficients = done_upper[:, GROUP * b : GROUP * (b + block)]
            less_upper = contract(coefficients, done_upper, ((0,), (0,)), HIGHEST)
            less_inverse = contract(coefficients, done_inverse, ((0,), (0,)), HIGHEST)
            for k in range(block):
                upper[b + k] = upper[b + k] - less_upper[GROUP * k : GROUP * (k + 1)]
                inverse[b + k] = inverse[b + k] - less_inverse[GROUP * k : GROUP * (k + 1)]
        for r in range(b, b + block):
            lane = GROUP * r
            columns = [full(upper[r][:, lane + k : lane + k + 1]) for k in range(GROUP)]
            diag = [[full(columns[j][i : i + 1]) for j in range(i + 1)] for i in range(GROUP)]
            lower = [[None] * GROUP for _ in range(GROUP)]
            scale = [None] * GROUP
            for i in range(GROUP):
                scale[i] = lax.rsqrt(diag[i][i])
                for k in range(i + 1, GROUP):
                    lower[k][i] = diag[k][i] * scale[i]
                for k in range(i + 1, GROUP):
                    for j in range(i + 1, k + 1):
                        diag[k][j] = diag[k][j] - lower[k][i] * lower[j][i]
            u = [full(upper[r][i : i + 1]) for i in range(GROUP)]
            v = [full(inverse[r][i : i + 1]) for i in range(GROUP)]
            for i in range(GROUP):
                u[i], v[i] = u[i] * scale[i], v[i] * scale[i]
                for k in range(i + 1, GROUP):
                    u[k], v[k] = u[k] - lower[k][i] * u[i], v[k] - lower[k][i] * v[i]
            upper[r], inverse[r] = u[0], v[0]
            for i in range(1, GROUP):
                upper[r] = jnp.where(row == i, u[i], upper[r])
                inverse[r] = jnp.where(row == i, v[i], inverse[r])
            for later in range(r + 1, b + block):
                left = [full(upper[later][:, lane + k : lane + k + 1]) for k in range(GROUP)]
                for i in range(GROUP):
                    left[i] = left[i] * scale[i]
                    for k in range(i + 1, GROUP):
                        left[k] = left[k] - lower[k][i] * left[i]
                    upper[later] = upper[later] - left[i] * u[i]
                    inverse[later] = inverse[later] - left[i] * v[i]
    at_row = lax.broadcasted_iota(jnp.int32, (size, size), 0)
    at_col = lax.broadcasted_iota(jnp.int32, (size, size), 1)
    return jnp.where(at_col >= at_row, jnp.concatenate(upper, axis=0), 0.0), jnp.concatenate(inverse, axis=0)


def basis_body(image, gram, basis, upper):
    upper[...], inverse = factor(gram[...], 4)
    basis[...] = contract(image[...], inverse, ((1,), (1,)), HIGHEST)


def per_device(embeddings, start_panel, tile_mask, inv_width):
    n_blk = lax.axis_size("blk")
    half, width = start_panel.shape
    size = half // 2
    sub_move = lambda v: lax.ppermute(v, "sub", [(0, 1), (1, 0)])
    blk_route = lambda v, to: lax.ppermute(v, "blk", [(i, to(i) % n_blk) for i in range(n_blk)])
    blk_move = lambda v, by: blk_route(v, lambda i: i + by)

    after = lambda v, *earlier: lax.optimization_barrier((v, *earlier))[0]
    numbers = jnp.concatenate([inv_width, lax.axis_index("sub").astype(F32).reshape(1)])
    numbers = jnp.broadcast_to(numbers[:, None], (2, TILE))
    wide = embeddings.shape[1] + width
    packed = lambda rows, lanes: jax.ShapeDtypeStruct((rows, lanes), BF16)
    above = blk_move(embeddings, -2)
    first, last, panel_mark = vmem_call(
        pack_body,
        (packed(size, wide), packed(size + MARK, wide), packed(half + MARK, width)),
        embeddings,
        start_panel,
        tile_mask,
        long=False,
    )
    relayed = n_blk == 8
    swapped = blk_route(last, lambda i: i ^ 1) if relayed else last
    above_panel = blk_move(panel_mark, -2)
    own = (first, last, sub_move(first), sub_move(last))
    image, turned = shape(half, width), shape(width, 2 * half)
    self_image = vmem_call(self_body, image, numbers, *own, long=False)
    below0 = blk_move(after(first, swapped, self_image), 1)
    swapped = after(swapped, self_image)
    below1 = blk_route(swapped, lambda i: i if i & 1 else i + 2) if relayed else blk_move(swapped, 1)
    above_image, back, above_sq, above_panel = vmem_call(
        above_own_body,
        (image, turned, image, packed(half + MARK, width)),
        numbers,
        above,
        above_panel,
        *own,
    )
    piece = shape(size, width)
    below1 = after(below1, above_image)
    other1 = sub_move(below1)
    below_image1, back = vmem_call(below_last_body, (piece, turned), numbers, below1, *own, back)
    below0 = after(below0, below_image1)
    other0 = sub_move(below0)
    here = (numbers, above, above_panel, above_sq)
    above_image, below_sum1, below_cross1 = vmem_call(
        above_below_last_body, (image, piece, piece), *here, below1, other1, after(above_image, below0)
    )
    above_image, below_sum0, below_cross0 = vmem_call(
        above_below_first_body, (image, piece, piece), *here, below1, other1, below0, other0, above_image
    )
    below_image0, own_image, own_cross = vmem_call(
        below_first_body, (piece, image, image), numbers, below1, below0, *own, self_image, after(back, above_image)
    )
    above_image = blk_move(above_image, 2)
    join = lambda *parts: jnp.concatenate(parts, axis=0)
    below_cross = sub_move(join(below_cross0, below_cross1))
    below_image = join(below_sum0, below_sum1) + below_cross + join(below_image0, below_image1)
    below_image = blk_move(below_image, -1)
    image_rows, gram = vmem_call(
        gram_body, (image, shape(width, width)), own_image, sub_move(own_cross), below_image, above_image
    )
    if n_blk & (n_blk - 1):
        gram = lax.psum(gram, ("blk", "sub"))
    else:
        gram = gram + sub_move(gram)
        hop = 1
        while hop < n_blk:
            gram = gram + blk_route(gram, lambda i: i ^ hop)
            hop *= 2
    return vmem_call(basis_body, (image, shape(width, width)), image_rows, gram)


def solution(mesh):
    return jax.shard_map(
        per_device,
        mesh=mesh,
        in_specs=(
            P(("groups", "blk", "sub"), None),
            P(("groups", "blk", "sub"), None),
            P(("groups", "blk", "sub"), None),
            P(),
        ),
        out_specs=(P(("groups", "blk", "sub"), None), P("groups", None)),
        check_vma=False,
    )
```

```python
import jax
import jax.numpy as jnp
from jax import lax
from jax.experimental import pallas as pl
from jax.experimental.pallas import tpu as pltpu
from jax.sharding import PartitionSpec as P

TILE = 128
REACH = 3
F32 = jnp.float32
BF16 = jnp.bfloat16
HIGHEST = lax.Precision.HIGHEST


def vmem_call(body, out_shapes, *operands, long=True):
    in_vmem = pl.BlockSpec(memory_space=pltpu.VMEM)
    return pl.pallas_call(
        body,
        out_shape=out_shapes,
        in_specs=[in_vmem] * len(operands),
        out_specs=jax.tree.map(lambda _: in_vmem, out_shapes),
        compiler_params=pltpu.CompilerParams(vmem_limit_bytes=24 << 20),
        cost_estimate=pl.CostEstimate(flops=10**11 if long else 1, transcendentals=0, bytes_accessed=1),
    )(*operands)


def shape(*dims):
    return jax.ShapeDtypeStruct(dims, F32)


def contract(a, b, dims, precision=None):
    return lax.dot_general(a, b, (dims, ((), ())), precision=precision, preferred_element_type=F32)


MARK = 8
OWN, BELOW, ABOVE = 0, 1, -2


def pair_mask(sub, rows, cols, offset, which):
    tiles = rows.shape[0]
    padded, lanes = rows.shape[1], tiles * TILE
    tile_of = lax.broadcasted_iota(jnp.int32, (padded, lanes), 1) // TILE
    first = (REACH + offset) * 2 * tiles + (sub if which == 0 else 1 - sub) * tiles
    chosen = (lax.broadcasted_iota(jnp.int32, (padded, lanes), 0) == first + tile_of).astype(F32)
    ahead = contract(rows, chosen, ((1,), (0,)))
    first = (REACH - offset) * 2 * tiles + sub * tiles
    row_at = lax.broadcasted_iota(jnp.int32, (tiles, padded), 0)
    chosen = (lax.broadcasted_iota(jnp.int32, (tiles, padded), 1) == first + row_at).astype(F32)
    spread = (lax.broadcasted_iota(jnp.int32, (tiles, lanes), 0) == tile_of[:tiles]).astype(F32)
    back = contract(contract(chosen, cols, ((1,), (1,))), spread, ((1,), (0,)))
    return jnp.concatenate([ahead, back], axis=0)


def marks(ref, half):
    return ref[ref.shape[0] - MARK :, ref.shape[1] - TILE :].astype(F32)[: half // TILE]


def pieces(*refs):
    size = min(r.shape[0] for r in refs)
    return [(r[:size, : r.shape[1] - TILE], r[:size, r.shape[1] - TILE :]) for r in refs]


def apart(features, panel):
    size = features.shape[0] // 2
    return [(features[rows], panel[rows]) for rows in (slice(0, size), slice(size, 2 * size))]


def squares(features):
    wide = features.astype(F32)
    return jnp.sum(wide * wide, axis=1, keepdims=True)


def as_row(column):
    return jnp.broadcast_to(column, (column.shape[0], TILE)).T[:1]


def as_column(row):
    return jnp.broadcast_to(row, (TILE, row.shape[1])).T[:, :1]


SPLIT = 3


def square_rows(ref):
    size = ref.shape[0] - MARK
    parts = ref[size:, : 2 * size].astype(F32)
    row = (parts[0:1] + parts[1:2]) + parts[2:3]
    return [row[:, :size], row[:, size:]]


def columns_of(own, other, sq_rows, masks):
    out = []
    for half, mask in zip((own, other), masks):
        for k, (features, panel) in enumerate(half):
            size = features.shape[0]
            out.append((features, panel, sq_rows[len(out)], mask[:, k * size : (k + 1) * size]))
    return out


def products(inverse, rows, squares_of, columns, back, first=0):
    panels = jnp.concatenate([panel for _, panel, _, _ in columns], axis=0)
    images = []
    for r, (features, panel) in enumerate(rows):
        size = features.shape[0]
        row_sq = squares_of[r]
        doubled = features * 2
        tile = (first + r) * size // TILE
        ahead, behind = [], []
        for other, _, col_sq, mask in columns:
            tiles = mask.shape[0] // 2
            gram2 = contract(doubled, other, ((1,), (1,)))
            kernel = jnp.exp(-inverse * jnp.maximum(row_sq + col_sq - gram2, 0.0))

            def masked(first):
                parts = [kernel[i * TILE : (i + 1) * TILE] * mask[first + i : first + i + 1] for i in range(size // TILE)]
                return jnp.concatenate(parts, axis=0).astype(BF16)

            ahead.append(masked(tile))
            if back is not None:
                behind.append(masked(tiles + tile))
        images.append(contract(jnp.concatenate(ahead, axis=1), panels, ((1,), (0,))))
        if back is not None:
            panel_t = panel.astype(F32).T.astype(BF16)
            back = back + contract(panel_t, jnp.concatenate(behind, axis=1), ((1,), (0,)))
    return jnp.concatenate(images, axis=0), back


def pack_body(embeddings, panel, tile_mask, first, last, panel_mark):
    half, features = embeddings.shape
    size = half // 2
    tiles, window = tile_mask.shape
    at = lax.broadcasted_iota(jnp.int32, (window, TILE), 0) == lax.broadcasted_iota(jnp.int32, (window, TILE), 1)
    mask = contract(tile_mask[...].astype(F32), at.astype(F32), ((1,), (0,)))
    mask = jnp.concatenate([mask, jnp.zeros((MARK - tiles, TILE), F32)], axis=0).astype(BF16)
    for ref, start in ((first, 0), (last, size)):
        ref[:size, :features] = embeddings[start : start + size]
        ref[:size, features:] = panel[start : start + size]
    row = as_row(jnp.concatenate([squares(r[:size, :features]) for r in (first, last)], axis=0))
    carried = []
    for _ in range(SPLIT):
        carried.append(row.astype(BF16).astype(F32))
        row = row - carried[-1]
    carried = jnp.concatenate(carried + [jnp.zeros((MARK - SPLIT, half), F32)], axis=0).astype(BF16)
    first[size:, :features] = jnp.concatenate([carried, jnp.zeros((MARK, features - half), BF16)], axis=1)
    first[size:, features:] = mask
    panel_mark[:half] = panel[...]
    panel_mark[half:] = mask


def width_of(numbers):
    return numbers[0:1, 0:1]


def place(numbers):
    return jnp.where(numbers[1:2, 0:1] > 0.5, 1, 0)


def masks_of(sub, rows, others, offset):
    return [pair_mask(sub, rows, r, offset, h) for h, r in enumerate(others)]


def self_body(numbers, first, last, other_first, other_last, image):
    half = 2 * last.shape[0]
    own, other = pieces(first, last), pieces(other_first, other_last)
    rows = square_rows(first)
    both = [marks(r, half) for r in (first, other_first)]
    columns = columns_of(own, other, rows + square_rows(other_first), masks_of(place(numbers), both[0], both, OWN))
    image[...], _ = products(width_of(numbers), own, [as_column(r) for r in rows], columns, None)


def own_columns(place_here, mark, first, last, other_first, other_last, offset):
    half = 2 * last.shape[0]
    masks = masks_of(place_here, mark, [marks(r, half) for r in (first, other_first)], offset)
    rows = square_rows(first) + square_rows(other_first)
    return columns_of(pieces(first, last), pieces(other_first, other_last), rows, masks)


def above_own_body(numbers, above, panel, first, last, other_first, other_last, image, back, above_sq, kept_panel):
    half = above.shape[0]
    size = half // 2
    columns = own_columns(place(numbers), marks(panel, half), first, last, other_first, other_last, ABOVE)
    kept_panel[...] = panel[...]
    rows = apart(above, panel)
    columns_sq = [squares(features) for features, _ in rows]
    for k, column in enumerate(columns_sq):
        above_sq[k * size : (k + 1) * size] = jnp.broadcast_to(column, (size, TILE))
    image[...], back[...] = products(width_of(numbers), rows, columns_sq, columns, jnp.zeros(back.shape, F32))


def below_first_body(numbers, below, first, last, other_first, other_last, back, image, total):
    half = 2 * last.shape[0]
    columns = own_columns(place(numbers), marks(below, half), first, last, other_first, other_last, BELOW)
    rows_sq = [as_column(square_rows(below)[0])]
    image[...], total[...] = products(width_of(numbers), [pieces(below, last)[0]], rows_sq, columns, back[...])


def below_last_body(
    numbers, marked, below, first, last, other_first, other_last, self_image, back, image, own_image, own_cross
):
    half = 2 * last.shape[0]
    columns = own_columns(place(numbers), marks(marked, half), first, last, other_first, other_last, BELOW)
    rows_sq = [as_column(square_rows(marked)[1])]
    image[...], total = products(width_of(numbers), pieces(below), rows_sq, columns, back[...], 1)
    own_image[...] = self_image[...] + total[:, :half].T
    own_cross[...] = total[:, half:].T


def above_below(part, numbers, above, panel, above_sq, marked, other_marked, below, other, above_image, image, below_image, cross):
    half = image.shape[0]
    size = half // 2
    masks = masks_of(place(numbers), marks(panel, half), [marks(r, half) for r in (marked, other_marked)], ABOVE - BELOW)
    masks = [mask[:, part * size : (part + 1) * size] for mask in masks]
    columns_sq = [square_rows(r)[part] for r in (marked, other_marked)]
    columns = columns_of([(below[:size, :-TILE], below[:size, -TILE:])], [(other[:size, :-TILE], other[:size, -TILE:])], columns_sq, masks)
    rows_sq = [above_sq[k * size : (k + 1) * size, :1] for k in range(2)]
    products_image, total = products(width_of(numbers), apart(above, panel), rows_sq, columns, jnp.zeros((TILE, half), F32))
    image[...] = above_image[...] + products_image
    below_image[...] = total[:, :size].T
    cross[...] = total[:, size:].T


def above_below_first_body(numbers, above, panel, above_sq, below, other, above_image, *outs):
    above_below(0, numbers, above, panel, above_sq, below, other, below, other, above_image, *outs)


def above_below_last_body(numbers, above, panel, above_sq, marked, other_marked, below, other, above_image, *outs):
    above_below(1, numbers, above, panel, above_sq, marked, other_marked, below, other, above_image, *outs)


def gram_body(own, cross, below, above, image, gram):
    total = own[...] + cross[...] + below[...] + above[...]
    image[...] = total
    gram[...] = contract(total, total, ((0,), (0,)), HIGHEST)


GROUP = 8


def full(value):
    return jnp.broadcast_to(value, (GROUP, value.shape[1] if value.shape[1] > 1 else TILE))


def factor(gram, block):
    size = gram.shape[0]
    groups = size // GROUP
    upper = [gram[GROUP * r : GROUP * (r + 1)] for r in range(groups)]
    row = lax.broadcasted_iota(jnp.int32, (GROUP, size), 0)
    col = lax.broadcasted_iota(jnp.int32, (GROUP, size), 1)
    inverse = [jnp.where(col == row + GROUP * r, 1.0, 0.0).astype(F32) for r in range(groups)]
    for b in range(0, groups, block):
        if b:
            done_upper, done_inverse = jnp.concatenate(upper[:b], axis=0), jnp.concatenate(inverse[:b], axis=0)
            coefficients = done_upper[:, GROUP * b : GROUP * (b + block)]
            less_upper = contract(coefficients, done_upper, ((0,), (0,)), HIGHEST)
            less_inverse = contract(coefficients, done_inverse, ((0,), (0,)), HIGHEST)
            for k in range(block):
                upper[b + k] = upper[b + k] - less_upper[GROUP * k : GROUP * (k + 1)]
                inverse[b + k] = inverse[b + k] - less_inverse[GROUP * k : GROUP * (k + 1)]
        for r in range(b, b + block):
            lane = GROUP * r
            columns = [full(upper[r][:, lane + k : lane + k + 1]) for k in range(GROUP)]
            diag = [[full(columns[j][i : i + 1]) for j in range(i + 1)] for i in range(GROUP)]
            lower = [[None] * GROUP for _ in range(GROUP)]
            scale = [None] * GROUP
            for i in range(GROUP):
                scale[i] = lax.rsqrt(diag[i][i])
                for k in range(i + 1, GROUP):
                    lower[k][i] = diag[k][i] * scale[i]
                for k in range(i + 1, GROUP):
                    for j in range(i + 1, k + 1):
                        diag[k][j] = diag[k][j] - lower[k][i] * lower[j][i]
            u = [full(upper[r][i : i + 1]) for i in range(GROUP)]
            v = [full(inverse[r][i : i + 1]) for i in range(GROUP)]
            for i in range(GROUP):
                u[i], v[i] = u[i] * scale[i], v[i] * scale[i]
                for k in range(i + 1, GROUP):
                    u[k], v[k] = u[k] - lower[k][i] * u[i], v[k] - lower[k][i] * v[i]
            upper[r], inverse[r] = u[0], v[0]
            for i in range(1, GROUP):
                upper[r] = jnp.where(row == i, u[i], upper[r])
                inverse[r] = jnp.where(row == i, v[i], inverse[r])
            for later in range(r + 1, b + block):
                left = [full(upper[later][:, lane + k : lane + k + 1]) for k in range(GROUP)]
                for i in range(GROUP):
                    left[i] = left[i] * scale[i]
                    for k in range(i + 1, GROUP):
                        left[k] = left[k] - lower[k][i] * left[i]
                    upper[later] = upper[later] - left[i] * u[i]
                    inverse[later] = inverse[later] - left[i] * v[i]
    at_row = lax.broadcasted_iota(jnp.int32, (size, size), 0)
    at_col = lax.broadcasted_iota(jnp.int32, (size, size), 1)
    return jnp.where(at_col >= at_row, jnp.concatenate(upper, axis=0), 0.0), jnp.concatenate(inverse, axis=0)


def basis_body(image, gram, basis, upper):
    upper[...], inverse = factor(gram[...], 4)
    basis[...] = contract(image[...], inverse, ((1,), (1,)), HIGHEST)


def per_device(embeddings, start_panel, tile_mask, inv_width):
    n_blk = lax.axis_size("blk")
    half, width = start_panel.shape
    size = half // 2
    sub_move = lambda v: lax.ppermute(v, "sub", [(0, 1), (1, 0)])
    blk_route = lambda v, to: lax.ppermute(v, "blk", [(i, to(i) % n_blk) for i in range(n_blk)])
    blk_move = lambda v, by: blk_route(v, lambda i: i + by)

    after = lambda v, *earlier: lax.optimization_barrier((v, *earlier))[0]
    numbers = jnp.concatenate([inv_width, lax.axis_index("sub").astype(F32).reshape(1)])
    numbers = jnp.broadcast_to(numbers[:, None], (2, TILE))
    wide = embeddings.shape[1] + width
    packed = lambda rows, lanes: jax.ShapeDtypeStruct((rows, lanes), BF16)
    above = blk_move(embeddings, -2)
    first, last, panel_mark = vmem_call(
        pack_body,
        (packed(size + MARK, wide), packed(size, wide), packed(half + MARK, width)),
        embeddings,
        start_panel,
        tile_mask,
        long=False,
    )
    relayed = n_blk == 8
    swapped = blk_route(last, lambda i: i ^ 1) if relayed else last
    above_panel = blk_move(panel_mark, -2)
    own = (first, last, sub_move(first), sub_move(last))
    image, turned = shape(half, width), shape(width, 2 * half)
    self_image = vmem_call(self_body, image, numbers, *own, long=False)
    below0 = blk_move(after(first, swapped, self_image), 1)
    swapped = after(swapped, self_image)
    below1 = blk_route(swapped, lambda i: i if i & 1 else i + 2) if relayed else blk_move(swapped, 1)
    above_image, back, above_sq, above_panel = vmem_call(
        above_own_body,
        (image, turned, image, packed(half + MARK, width)),
        numbers,
        above,
        above_panel,
        *own,
    )
    piece = shape(size, width)
    below0 = after(below0, above_image)
    other0 = sub_move(below0)
    below_image0, back = vmem_call(below_first_body, (piece, turned), numbers, below0, *own, back)
    below1 = after(below1, below_image0)
    other1 = sub_move(below1)
    here = (numbers, above, above_panel, above_sq)
    above_image, below_sum0, below_cross0 = vmem_call(
        above_below_first_body, (image, piece, piece), *here, below0, other0, after(above_image, below1)
    )
    above_image, below_sum1, below_cross1 = vmem_call(
        above_below_last_body, (image, piece, piece), *here, below0, other0, below1, other1, above_image
    )
    below_image1, own_image, own_cross = vmem_call(
        below_last_body, (piece, image, image), numbers, below0, below1, *own, self_image, after(back, above_image)
    )
    above_image = blk_move(above_image, 2)
    join = lambda *parts: jnp.concatenate(parts, axis=0)
    below_cross = sub_move(join(below_cross0, below_cross1))
    below_image = join(below_sum0, below_sum1) + below_cross + join(below_image0, below_image1)
    below_image = blk_move(below_image, -1)
    image_rows, gram = vmem_call(
        gram_body, (image, shape(width, width)), own_image, sub_move(own_cross), below_image, above_image
    )
    if n_blk & (n_blk - 1):
        gram = lax.psum(gram, ("blk", "sub"))
    else:
        gram = gram + sub_move(gram)
        hop = 1
        while hop < n_blk:
            gram = gram + blk_route(gram, lambda i: i ^ hop)
            hop *= 2
    return vmem_call(basis_body, (image, shape(width, width)), image_rows, gram)


def solution(mesh):
    return jax.shard_map(
        per_device,
        mesh=mesh,
        in_specs=(
            P(("groups", "blk", "sub"), None),
            P(("groups", "blk", "sub"), None),
            P(("groups", "blk", "sub"), None),
            P(),
        ),
        out_specs=(P(("groups", "blk", "sub"), None), P("groups", None)),
        check_vma=False,
    )
```

```python
import jax
import jax.numpy as jnp
from jax import lax
from jax.experimental import pallas as pl
from jax.experimental.pallas import tpu as pltpu
from jax.sharding import PartitionSpec as P

TILE = 128
REACH = 3
F32 = jnp.float32
BF16 = jnp.bfloat16
HIGHEST = lax.Precision.HIGHEST


def vmem_call(body, out_shapes, *operands, long=True):
    in_vmem = pl.BlockSpec(memory_space=pltpu.VMEM)
    return pl.pallas_call(
        body,
        out_shape=out_shapes,
        in_specs=[in_vmem] * len(operands),
        out_specs=jax.tree.map(lambda _: in_vmem, out_shapes),
        compiler_params=pltpu.CompilerParams(vmem_limit_bytes=24 << 20),
        cost_estimate=pl.CostEstimate(flops=2 * 10**10 if long else 1, transcendentals=0, bytes_accessed=1),
    )(*operands)


def shape(*dims):
    return jax.ShapeDtypeStruct(dims, F32)


def contract(a, b, dims, precision=None):
    return lax.dot_general(a, b, (dims, ((), ())), precision=precision, preferred_element_type=F32)


MARK = 8
OWN, BELOW, ABOVE = 0, 1, -2


def pair_mask(sub, rows, cols, offset, which):
    tiles = rows.shape[0]
    padded, lanes = rows.shape[1], tiles * TILE
    tile_of = lax.broadcasted_iota(jnp.int32, (padded, lanes), 1) // TILE
    first = (REACH + offset) * 2 * tiles + (sub if which == 0 else 1 - sub) * tiles
    chosen = (lax.broadcasted_iota(jnp.int32, (padded, lanes), 0) == first + tile_of).astype(F32)
    ahead = contract(rows, chosen, ((1,), (0,)))
    first = (REACH - offset) * 2 * tiles + sub * tiles
    row_at = lax.broadcasted_iota(jnp.int32, (tiles, padded), 0)
    chosen = (lax.broadcasted_iota(jnp.int32, (tiles, padded), 1) == first + row_at).astype(F32)
    spread = (lax.broadcasted_iota(jnp.int32, (tiles, lanes), 0) == tile_of[:tiles]).astype(F32)
    back = contract(contract(chosen, cols, ((1,), (1,))), spread, ((1,), (0,)))
    return jnp.concatenate([ahead, back], axis=0)


def marks(ref, half):
    return ref[ref.shape[0] - MARK :, ref.shape[1] - TILE :].astype(F32)[: half // TILE]


def pieces(*refs):
    size = min(r.shape[0] for r in refs)
    return [(r[:size, : r.shape[1] - TILE], r[:size, r.shape[1] - TILE :]) for r in refs]


def apart(features, panel):
    size = features.shape[0] // 2
    return [(features[rows], panel[rows]) for rows in (slice(0, size), slice(size, 2 * size))]


def squares(features):
    wide = features.astype(F32)
    return jnp.sum(wide * wide, axis=1, keepdims=True)


def as_row(column):
    return jnp.broadcast_to(column, (column.shape[0], TILE)).T[:1]


def as_column(row):
    return jnp.broadcast_to(row, (TILE, row.shape[1])).T[:, :1]


SPLIT = 3


def square_rows(ref):
    size = ref.shape[0] - MARK
    parts = ref[size:, : 2 * size].astype(F32)
    row = (parts[0:1] + parts[1:2]) + parts[2:3]
    return [row[:, :size], row[:, size:]]


def columns_of(own, other, sq_rows, masks):
    out = []
    for half, mask in zip((own, other), masks):
        for k, (features, panel) in enumerate(half):
            size = features.shape[0]
            out.append((features, panel, sq_rows[len(out)], mask[:, k * size : (k + 1) * size]))
    return out


def products(inverse, rows, squares_of, columns, back, first=0):
    panels = jnp.concatenate([panel for _, panel, _, _ in columns], axis=0)
    images = []
    for r, (features, panel) in enumerate(rows):
        size = features.shape[0]
        row_sq = squares_of[r]
        doubled = features * 2
        tile = (first + r) * size // TILE
        ahead, behind = [], []
        for other, _, col_sq, mask in columns:
            tiles = mask.shape[0] // 2
            gram2 = contract(doubled, other, ((1,), (1,)))
            kernel = jnp.exp(-inverse * jnp.maximum(row_sq + col_sq - gram2, 0.0))

            def masked(first):
                parts = [kernel[i * TILE : (i + 1) * TILE] * mask[first + i : first + i + 1] for i in range(size // TILE)]
                return jnp.concatenate(parts, axis=0).astype(BF16)

            ahead.append(masked(tile))
            if back is not None:
                behind.append(masked(tiles + tile))
        images.append(contract(jnp.concatenate(ahead, axis=1), panels, ((1,), (0,))))
        if back is not None:
            panel_t = panel.astype(F32).T.astype(BF16)
            back = back + contract(panel_t, jnp.concatenate(behind, axis=1), ((1,), (0,)))
    return jnp.concatenate(images, axis=0), back


def pack_body(embeddings, panel, tile_mask, first, last, panel_mark):
    half, features = embeddings.shape
    size = half // 2
    tiles, window = tile_mask.shape
    at = lax.broadcasted_iota(jnp.int32, (window, TILE), 0) == lax.broadcasted_iota(jnp.int32, (window, TILE), 1)
    mask = contract(tile_mask[...].astype(F32), at.astype(F32), ((1,), (0,)))
    mask = jnp.concatenate([mask, jnp.zeros((MARK - tiles, TILE), F32)], axis=0).astype(BF16)
    for ref, start in ((first, 0), (last, size)):
        ref[:size, :features] = embeddings[start : start + size]
        ref[:size, features:] = panel[start : start + size]
    row = as_row(jnp.concatenate([squares(r[:size, :features]) for r in (first, last)], axis=0))
    carried = []
    for _ in range(SPLIT):
        carried.append(row.astype(BF16).astype(F32))
        row = row - carried[-1]
    carried = jnp.concatenate(carried + [jnp.zeros((MARK - SPLIT, half), F32)], axis=0).astype(BF16)
    first[size:, :features] = jnp.concatenate([carried, jnp.zeros((MARK, features - half), BF16)], axis=1)
    first[size:, features:] = mask
    panel_mark[:half] = panel[...]
    panel_mark[half:] = mask


def width_of(numbers):
    return numbers[0:1, 0:1]


def place(numbers):
    return jnp.where(numbers[1:2, 0:1] > 0.5, 1, 0)


def masks_of(sub, rows, others, offset):
    return [pair_mask(sub, rows, r, offset, h) for h, r in enumerate(others)]


def self_body(numbers, first, last, other_first, other_last, image):
    half = 2 * last.shape[0]
    own, other = pieces(first, last), pieces(other_first, other_last)
    rows = square_rows(first)
    both = [marks(r, half) for r in (first, other_first)]
    columns = columns_of(own, other, rows + square_rows(other_first), masks_of(place(numbers), both[0], both, OWN))
    image[...], _ = products(width_of(numbers), own, [as_column(r) for r in rows], columns, None)


def own_columns(place_here, mark, first, last, other_first, other_last, offset):
    half = 2 * last.shape[0]
    masks = masks_of(place_here, mark, [marks(r, half) for r in (first, other_first)], offset)
    rows = square_rows(first) + square_rows(other_first)
    return columns_of(pieces(first, last), pieces(other_first, other_last), rows, masks)


def above_own_body(numbers, above, panel, first, last, other_first, other_last, image, back, above_sq, kept_panel):
    half = above.shape[0]
    size = half // 2
    columns = own_columns(place(numbers), marks(panel, half), first, last, other_first, other_last, ABOVE)
    kept_panel[...] = panel[...]
    rows = apart(above, panel)
    columns_sq = [squares(features) for features, _ in rows]
    for k, column in enumerate(columns_sq):
        above_sq[k * size : (k + 1) * size] = jnp.broadcast_to(column, (size, TILE))
    image[...], back[...] = products(width_of(numbers), rows, columns_sq, columns, jnp.zeros(back.shape, F32))


def below_first_body(numbers, below, first, last, other_first, other_last, back, image, total):
    half = 2 * last.shape[0]
    columns = own_columns(place(numbers), marks(below, half), first, last, other_first, other_last, BELOW)
    rows_sq = [as_column(square_rows(below)[0])]
    image[...], total[...] = products(width_of(numbers), [pieces(below, last)[0]], rows_sq, columns, back[...])


def below_last_body(
    numbers, marked, below, first, last, other_first, other_last, self_image, back, image, own_image, own_cross
):
    half = 2 * last.shape[0]
    columns = own_columns(place(numbers), marks(marked, half), first, last, other_first, other_last, BELOW)
    rows_sq = [as_column(square_rows(marked)[1])]
    image[...], total = products(width_of(numbers), pieces(below), rows_sq, columns, back[...], 1)
    own_image[...] = self_image[...] + total[:, :half].T
    own_cross[...] = total[:, half:].T


def above_below(part, numbers, above, panel, above_sq, marked, other_marked, below, other, above_image, image, below_image, cross):
    half = image.shape[0]
    size = half // 2
    masks = masks_of(place(numbers), marks(panel, half), [marks(r, half) for r in (marked, other_marked)], ABOVE - BELOW)
    masks = [mask[:, part * size : (part + 1) * size] for mask in masks]
    columns_sq = [square_rows(r)[part] for r in (marked, other_marked)]
    columns = columns_of([(below[:size, :-TILE], below[:size, -TILE:])], [(other[:size, :-TILE], other[:size, -TILE:])], columns_sq, masks)
    rows_sq = [above_sq[k * size : (k + 1) * size, :1] for k in range(2)]
    products_image, total = products(width_of(numbers), apart(above, panel), rows_sq, columns, jnp.zeros((TILE, half), F32))
    image[...] = above_image[...] + products_image
    below_image[...] = total[:, :size].T
    cross[...] = total[:, size:].T


def above_below_first_body(numbers, above, panel, above_sq, below, other, above_image, *outs):
    above_below(0, numbers, above, panel, above_sq, below, other, below, other, above_image, *outs)


def above_below_last_body(numbers, above, panel, above_sq, marked, other_marked, below, other, above_image, *outs):
    above_below(1, numbers, above, panel, above_sq, marked, other_marked, below, other, above_image, *outs)


def gram_body(own, cross, below, above, image, gram):
    total = own[...] + cross[...] + below[...] + above[...]
    image[...] = total
    gram[...] = contract(total, total, ((0,), (0,)), HIGHEST)


GROUP = 8


def full(value):
    return jnp.broadcast_to(value, (GROUP, value.shape[1] if value.shape[1] > 1 else TILE))


def factor(gram, block):
    size = gram.shape[0]
    groups = size // GROUP
    upper = [gram[GROUP * r : GROUP * (r + 1)] for r in range(groups)]
    row = lax.broadcasted_iota(jnp.int32, (GROUP, size), 0)
    col = lax.broadcasted_iota(jnp.int32, (GROUP, size), 1)
    inverse = [jnp.where(col == row + GROUP * r, 1.0, 0.0).astype(F32) for r in range(groups)]
    for b in range(0, groups, block):
        if b:
            done_upper, done_inverse = jnp.concatenate(upper[:b], axis=0), jnp.concatenate(inverse[:b], axis=0)
            coefficients = done_upper[:, GROUP * b : GROUP * (b + block)]
            less_upper = contract(coefficients, done_upper, ((0,), (0,)), HIGHEST)
            less_inverse = contract(coefficients, done_inverse, ((0,), (0,)), HIGHEST)
            for k in range(block):
                upper[b + k] = upper[b + k] - less_upper[GROUP * k : GROUP * (k + 1)]
                inverse[b + k] = inverse[b + k] - less_inverse[GROUP * k : GROUP * (k + 1)]
        for r in range(b, b + block):
            lane = GROUP * r
            columns = [full(upper[r][:, lane + k : lane + k + 1]) for k in range(GROUP)]
            diag = [[full(columns[j][i : i + 1]) for j in range(i + 1)] for i in range(GROUP)]
            lower = [[None] * GROUP for _ in range(GROUP)]
            scale = [None] * GROUP
            for i in range(GROUP):
                scale[i] = lax.rsqrt(diag[i][i])
                for k in range(i + 1, GROUP):
                    lower[k][i] = diag[k][i] * scale[i]
                for k in range(i + 1, GROUP):
                    for j in range(i + 1, k + 1):
                        diag[k][j] = diag[k][j] - lower[k][i] * lower[j][i]
            u = [full(upper[r][i : i + 1]) for i in range(GROUP)]
            v = [full(inverse[r][i : i + 1]) for i in range(GROUP)]
            for i in range(GROUP):
                u[i], v[i] = u[i] * scale[i], v[i] * scale[i]
                for k in range(i + 1, GROUP):
                    u[k], v[k] = u[k] - lower[k][i] * u[i], v[k] - lower[k][i] * v[i]
            upper[r], inverse[r] = u[0], v[0]
            for i in range(1, GROUP):
                upper[r] = jnp.where(row == i, u[i], upper[r])
                inverse[r] = jnp.where(row == i, v[i], inverse[r])
            for later in range(r + 1, b + block):
                left = [full(upper[later][:, lane + k : lane + k + 1]) for k in range(GROUP)]
                for i in range(GROUP):
                    left[i] = left[i] * scale[i]
                    for k in range(i + 1, GROUP):
                        left[k] = left[k] - lower[k][i] * left[i]
                    upper[later] = upper[later] - left[i] * u[i]
                    inverse[later] = inverse[later] - left[i] * v[i]
    at_row = lax.broadcasted_iota(jnp.int32, (size, size), 0)
    at_col = lax.broadcasted_iota(jnp.int32, (size, size), 1)
    return jnp.where(at_col >= at_row, jnp.concatenate(upper, axis=0), 0.0), jnp.concatenate(inverse, axis=0)


def basis_body(image, gram, basis, upper):
    upper[...], inverse = factor(gram[...], 4)
    basis[...] = contract(image[...], inverse, ((1,), (1,)), HIGHEST)


def per_device(embeddings, start_panel, tile_mask, inv_width):
    n_blk = lax.axis_size("blk")
    half, width = start_panel.shape
    size = half // 2
    sub_move = lambda v: lax.ppermute(v, "sub", [(0, 1), (1, 0)])
    blk_route = lambda v, to: lax.ppermute(v, "blk", [(i, to(i) % n_blk) for i in range(n_blk)])
    blk_move = lambda v, by: blk_route(v, lambda i: i + by)

    after = lambda v, *earlier: lax.optimization_barrier((v, *earlier))[0]
    numbers = jnp.concatenate([inv_width, lax.axis_index("sub").astype(F32).reshape(1)])
    numbers = jnp.broadcast_to(numbers[:, None], (2, TILE))
    wide = embeddings.shape[1] + width
    packed = lambda rows, lanes: jax.ShapeDtypeStruct((rows, lanes), BF16)
    above = blk_move(embeddings, -2)
    first, last, panel_mark = vmem_call(
        pack_body,
        (packed(size + MARK, wide), packed(size, wide), packed(half + MARK, width)),
        embeddings,
        start_panel,
        tile_mask,
        long=False,
    )
    relayed = n_blk == 8
    swapped = blk_route(last, lambda i: i ^ 1) if relayed else last
    above_panel = blk_move(panel_mark, -2)
    own = (first, last, sub_move(first), sub_move(last))
    image, turned = shape(half, width), shape(width, 2 * half)
    self_image = vmem_call(self_body, image, numbers, *own, long=False)
    below0 = blk_move(after(first, swapped, self_image), 1)
    swapped = after(swapped, self_image)
    below1 = blk_route(swapped, lambda i: i if i & 1 else i + 2) if relayed else blk_move(swapped, 1)
    above_image, back, above_sq, above_panel = vmem_call(
        above_own_body,
        (image, turned, image, packed(half + MARK, width)),
        numbers,
        above,
        above_panel,
        *own,
    )
    piece = shape(size, width)
    below0 = after(below0, above_image)
    other0 = sub_move(below0)
    below_image0, back = vmem_call(below_first_body, (piece, turned), numbers, below0, *own, back)
    below1 = after(below1, below_image0)
    other1 = sub_move(below1)
    here = (numbers, above, above_panel, above_sq)
    above_image, below_sum0, below_cross0 = vmem_call(
        above_below_first_body, (image, piece, piece), *here, below0, other0, after(above_image, below1)
    )
    above_image, below_sum1, below_cross1 = vmem_call(
        above_below_last_body, (image, piece, piece), *here, below0, other0, below1, other1, above_image
    )
    below_image1, own_image, own_cross = vmem_call(
        below_last_body, (piece, image, image), numbers, below0, below1, *own, self_image, after(back, above_image)
    )
    above_image = blk_move(above_image, 2)
    join = lambda *parts: jnp.concatenate(parts, axis=0)
    below_cross = sub_move(join(below_cross0, below_cross1))
    below_image = join(below_sum0, below_sum1) + below_cross + join(below_image0, below_image1)
    below_image = blk_move(below_image, -1)
    image_rows, gram = vmem_call(
        gram_body, (image, shape(width, width)), own_image, sub_move(own_cross), below_image, above_image
    )
    if n_blk & (n_blk - 1):
        gram = lax.psum(gram, ("blk", "sub"))
    else:
        gram = gram + sub_move(gram)
        hop = 1
        while hop < n_blk:
            gram = gram + blk_route(gram, lambda i: i ^ hop)
            hop *= 2
    return vmem_call(basis_body, (image, shape(width, width)), image_rows, gram)


def solution(mesh):
    return jax.shard_map(
        per_device,
        mesh=mesh,
        in_specs=(
            P(("groups", "blk", "sub"), None),
            P(("groups", "blk", "sub"), None),
            P(("groups", "blk", "sub"), None),
            P(),
        ),
        out_specs=(P(("groups", "blk", "sub"), None), P("groups", None)),
        check_vma=False,
    )
```

```python
import jax
import jax.numpy as jnp
from jax import lax
from jax.experimental import pallas as pl
from jax.experimental.pallas import tpu as pltpu
from jax.sharding import PartitionSpec as P

TILE = 128
REACH = 3
F32 = jnp.float32
BF16 = jnp.bfloat16
HIGHEST = lax.Precision.HIGHEST


def vmem_call(body, out_shapes, *operands, long=True):
    in_vmem = pl.BlockSpec(memory_space=pltpu.VMEM)
    return pl.pallas_call(
        body,
        out_shape=out_shapes,
        in_specs=[in_vmem] * len(operands),
        out_specs=jax.tree.map(lambda _: in_vmem, out_shapes),
        compiler_params=pltpu.CompilerParams(vmem_limit_bytes=24 << 20),
        cost_estimate=pl.CostEstimate(flops=2 * 10**10 if long else 1, transcendentals=0, bytes_accessed=1),
    )(*operands)


def shape(*dims):
    return jax.ShapeDtypeStruct(dims, F32)


def contract(a, b, dims, precision=None):
    return lax.dot_general(a, b, (dims, ((), ())), precision=precision, preferred_element_type=F32)


MARK = 8
OWN, BELOW, ABOVE = 0, 1, -2


def pair_mask(sub, rows, cols, offset, which):
    tiles = rows.shape[0]
    padded, lanes = rows.shape[1], tiles * TILE
    tile_of = lax.broadcasted_iota(jnp.int32, (padded, lanes), 1) // TILE
    first = (REACH + offset) * 2 * tiles + (sub if which == 0 else 1 - sub) * tiles
    chosen = (lax.broadcasted_iota(jnp.int32, (padded, lanes), 0) == first + tile_of).astype(F32)
    ahead = contract(rows, chosen, ((1,), (0,)))
    first = (REACH - offset) * 2 * tiles + sub * tiles
    row_at = lax.broadcasted_iota(jnp.int32, (tiles, padded), 0)
    chosen = (lax.broadcasted_iota(jnp.int32, (tiles, padded), 1) == first + row_at).astype(F32)
    spread = (lax.broadcasted_iota(jnp.int32, (tiles, lanes), 0) == tile_of[:tiles]).astype(F32)
    back = contract(contract(chosen, cols, ((1,), (1,))), spread, ((1,), (0,)))
    return jnp.concatenate([ahead, back], axis=0)


def marks(ref, half):
    return ref[ref.shape[0] - MARK :, ref.shape[1] - TILE :].astype(F32)[: half // TILE]


def pieces(*refs):
    size = min(r.shape[0] for r in refs)
    return [(r[:size, : r.shape[1] - TILE], r[:size, r.shape[1] - TILE :]) for r in refs]


def apart(features, panel):
    size = features.shape[0] // 2
    return [(features[rows], panel[rows]) for rows in (slice(0, size), slice(size, 2 * size))]


def squares(features):
    wide = features.astype(F32)
    return jnp.sum(wide * wide, axis=1, keepdims=True)


def as_row(column):
    return jnp.broadcast_to(column, (column.shape[0], TILE)).T[:1]


def as_column(row):
    return jnp.broadcast_to(row, (TILE, row.shape[1])).T[:, :1]


SPLIT = 3


def square_rows(ref):
    size = ref.shape[0] - MARK
    parts = ref[size:, : 2 * size].astype(F32)
    row = (parts[0:1] + parts[1:2]) + parts[2:3]
    return [row[:, :size], row[:, size:]]


def columns_of(own, other, sq_rows, masks):
    out = []
    for half, mask in zip((own, other), masks):
        for k, (features, panel) in enumerate(half):
            size = features.shape[0]
            out.append((features, panel, sq_rows[len(out)], mask[:, k * size : (k + 1) * size]))
    return out


def products(inverse, rows, squares_of, columns, back, first=0):
    panels = jnp.concatenate([panel for _, panel, _, _ in columns], axis=0)
    images = []
    for r, (features, panel) in enumerate(rows):
        size = features.shape[0]
        row_sq = squares_of[r]
        doubled = features * 2
        tile = (first + r) * size // TILE
        ahead, behind = [], []
        for other, _, col_sq, mask in columns:
            tiles = mask.shape[0] // 2
            gram2 = contract(doubled, other, ((1,), (1,)))
            kernel = jnp.exp(-inverse * jnp.maximum(row_sq + col_sq - gram2, 0.0))

            def masked(first):
                parts = [kernel[i * TILE : (i + 1) * TILE] * mask[first + i : first + i + 1] for i in range(size // TILE)]
                return jnp.concatenate(parts, axis=0).astype(BF16)

            ahead.append(masked(tile))
            if back is not None:
                behind.append(masked(tiles + tile))
        images.append(contract(jnp.concatenate(ahead, axis=1), panels, ((1,), (0,))))
        if back is not None:
            panel_t = panel.astype(F32).T.astype(BF16)
            back = back + contract(panel_t, jnp.concatenate(behind, axis=1), ((1,), (0,)))
    return jnp.concatenate(images, axis=0), back


def pack_body(embeddings, panel, tile_mask, first, last, panel_mark):
    half, features = embeddings.shape
    size = half // 2
    tiles, window = tile_mask.shape
    at = lax.broadcasted_iota(jnp.int32, (window, TILE), 0) == lax.broadcasted_iota(jnp.int32, (window, TILE), 1)
    mask = contract(tile_mask[...].astype(F32), at.astype(F32), ((1,), (0,)))
    mask = jnp.concatenate([mask, jnp.zeros((MARK - tiles, TILE), F32)], axis=0).astype(BF16)
    for ref, start in ((first, 0), (last, size)):
        ref[:size, :features] = embeddings[start : start + size]
        ref[:size, features:] = panel[start : start + size]
    row = as_row(jnp.concatenate([squares(r[:size, :features]) for r in (first, last)], axis=0))
    carried = []
    for _ in range(SPLIT):
        carried.append(row.astype(BF16).astype(F32))
        row = row - carried[-1]
    carried = jnp.concatenate(carried + [jnp.zeros((MARK - SPLIT, half), F32)], axis=0).astype(BF16)
    last[size:, :features] = jnp.concatenate([carried, jnp.zeros((MARK, features - half), BF16)], axis=1)
    last[size:, features:] = mask
    panel_mark[:half] = panel[...]
    panel_mark[half:] = mask


def width_of(numbers):
    return numbers[0:1, 0:1]


def place(numbers):
    return jnp.where(numbers[1:2, 0:1] > 0.5, 1, 0)


def masks_of(sub, rows, others, offset):
    return [pair_mask(sub, rows, r, offset, h) for h, r in enumerate(others)]


def self_body(numbers, first, last, other_first, other_last, image):
    half = 2 * first.shape[0]
    own, other = pieces(first, last), pieces(other_first, other_last)
    rows = square_rows(last)
    both = [marks(r, half) for r in (last, other_last)]
    columns = columns_of(own, other, rows + square_rows(other_last), masks_of(place(numbers), both[0], both, OWN))
    image[...], _ = products(width_of(numbers), own, [as_column(r) for r in rows], columns, None)


def own_columns(place_here, mark, first, last, other_first, other_last, offset):
    half = 2 * first.shape[0]
    masks = masks_of(place_here, mark, [marks(r, half) for r in (last, other_last)], offset)
    rows = square_rows(last) + square_rows(other_last)
    return columns_of(pieces(first, last), pieces(other_first, other_last), rows, masks)


def above_own_body(numbers, above, panel, first, last, other_first, other_last, image, back, above_sq, kept_panel):
    half = above.shape[0]
    size = half // 2
    columns = own_columns(place(numbers), marks(panel, half), first, last, other_first, other_last, ABOVE)
    kept_panel[...] = panel[...]
    rows = apart(above, panel)
    columns_sq = [squares(features) for features, _ in rows]
    for k, column in enumerate(columns_sq):
        above_sq[k * size : (k + 1) * size] = jnp.broadcast_to(column, (size, TILE))
    image[...], back[...] = products(width_of(numbers), rows, columns_sq, columns, jnp.zeros(back.shape, F32))


def below_last_body(numbers, below, first, last, other_first, other_last, back, image, total):
    half = 2 * first.shape[0]
    columns = own_columns(place(numbers), marks(below, half), first, last, other_first, other_last, BELOW)
    rows_sq = [as_column(square_rows(below)[1])]
    image[...], total[...] = products(width_of(numbers), [pieces(below, first)[0]], rows_sq, columns, back[...], 1)


def below_first_body(
    numbers, marked, below, first, last, other_first, other_last, self_image, back, image, own_image, own_cross
):
    half = 2 * first.shape[0]
    columns = own_columns(place(numbers), marks(marked, half), first, last, other_first, other_last, BELOW)
    rows_sq = [as_column(square_rows(marked)[0])]
    image[...], total = products(width_of(numbers), pieces(below), rows_sq, columns, back[...])
    own_image[...] = self_image[...] + total[:, :half].T
    own_cross[...] = total[:, half:].T


def above_below(part, numbers, above, panel, above_sq, marked, other_marked, below, other, above_image, image, below_image, cross):
    half = image.shape[0]
    size = half // 2
    masks = masks_of(place(numbers), marks(panel, half), [marks(r, half) for r in (marked, other_marked)], ABOVE - BELOW)
    masks = [mask[:, part * size : (part + 1) * size] for mask in masks]
    columns_sq = [square_rows(r)[part] for r in (marked, other_marked)]
    columns = columns_of([(below[:size, :-TILE], below[:size, -TILE:])], [(other[:size, :-TILE], other[:size, -TILE:])], columns_sq, masks)
    rows_sq = [above_sq[k * size : (k + 1) * size, :1] for k in range(2)]
    products_image, total = products(width_of(numbers), apart(above, panel), rows_sq, columns, jnp.zeros((TILE, half), F32))
    image[...] = above_image[...] + products_image
    below_image[...] = total[:, :size].T
    cross[...] = total[:, size:].T


def above_below_last_body(numbers, above, panel, above_sq, below, other, above_image, *outs):
    above_below(1, numbers, above, panel, above_sq, below, other, below, other, above_image, *outs)


def above_below_first_body(numbers, above, panel, above_sq, marked, other_marked, below, other, above_image, *outs):
    above_below(0, numbers, above, panel, above_sq, marked, other_marked, below, other, above_image, *outs)


def gram_body(own, cross, below, above, image, gram):
    total = own[...] + cross[...] + below[...] + above[...]
    image[...] = total
    gram[...] = contract(total, total, ((0,), (0,)), HIGHEST)


GROUP = 8


def full(value):
    return jnp.broadcast_to(value, (GROUP, value.shape[1] if value.shape[1] > 1 else TILE))


def factor(gram, block):
    size = gram.shape[0]
    groups = size // GROUP
    upper = [gram[GROUP * r : GROUP * (r + 1)] for r in range(groups)]
    row = lax.broadcasted_iota(jnp.int32, (GROUP, size), 0)
    col = lax.broadcasted_iota(jnp.int32, (GROUP, size), 1)
    inverse = [jnp.where(col == row + GROUP * r, 1.0, 0.0).astype(F32) for r in range(groups)]
    for b in range(0, groups, block):
        if b:
            done_upper, done_inverse = jnp.concatenate(upper[:b], axis=0), jnp.concatenate(inverse[:b], axis=0)
            coefficients = done_upper[:, GROUP * b : GROUP * (b + block)]
            less_upper = contract(coefficients, done_upper, ((0,), (0,)), HIGHEST)
            less_inverse = contract(coefficients, done_inverse, ((0,), (0,)), HIGHEST)
            for k in range(block):
                upper[b + k] = upper[b + k] - less_upper[GROUP * k : GROUP * (k + 1)]
                inverse[b + k] = inverse[b + k] - less_inverse[GROUP * k : GROUP * (k + 1)]
        for r in range(b, b + block):
            lane = GROUP * r
            columns = [full(upper[r][:, lane + k : lane + k + 1]) for k in range(GROUP)]
            diag = [[full(columns[j][i : i + 1]) for j in range(i + 1)] for i in range(GROUP)]
            lower = [[None] * GROUP for _ in range(GROUP)]
            scale = [None] * GROUP
            for i in range(GROUP):
                scale[i] = lax.rsqrt(diag[i][i])
                for k in range(i + 1, GROUP):
                    lower[k][i] = diag[k][i] * scale[i]
                for k in range(i + 1, GROUP):
                    for j in range(i + 1, k + 1):
                        diag[k][j] = diag[k][j] - lower[k][i] * lower[j][i]
            u = [full(upper[r][i : i + 1]) for i in range(GROUP)]
            v = [full(inverse[r][i : i + 1]) for i in range(GROUP)]
            for i in range(GROUP):
                u[i], v[i] = u[i] * scale[i], v[i] * scale[i]
                for k in range(i + 1, GROUP):
                    u[k], v[k] = u[k] - lower[k][i] * u[i], v[k] - lower[k][i] * v[i]
            upper[r], inverse[r] = u[0], v[0]
            for i in range(1, GROUP):
                upper[r] = jnp.where(row == i, u[i], upper[r])
                inverse[r] = jnp.where(row == i, v[i], inverse[r])
            for later in range(r + 1, b + block):
                left = [full(upper[later][:, lane + k : lane + k + 1]) for k in range(GROUP)]
                for i in range(GROUP):
                    left[i] = left[i] * scale[i]
                    for k in range(i + 1, GROUP):
                        left[k] = left[k] - lower[k][i] * left[i]
                    upper[later] = upper[later] - left[i] * u[i]
                    inverse[later] = inverse[later] - left[i] * v[i]
    at_row = lax.broadcasted_iota(jnp.int32, (size, size), 0)
    at_col = lax.broadcasted_iota(jnp.int32, (size, size), 1)
    return jnp.where(at_col >= at_row, jnp.concatenate(upper, axis=0), 0.0), jnp.concatenate(inverse, axis=0)


def basis_body(image, gram, basis, upper):
    upper[...], inverse = factor(gram[...], 4)
    basis[...] = contract(image[...], inverse, ((1,), (1,)), HIGHEST)


def per_device(embeddings, start_panel, tile_mask, inv_width):
    n_blk = lax.axis_size("blk")
    half, width = start_panel.shape
    size = half // 2
    sub_move = lambda v: lax.ppermute(v, "sub", [(0, 1), (1, 0)])
    blk_route = lambda v, to: lax.ppermute(v, "blk", [(i, to(i) % n_blk) for i in range(n_blk)])
    blk_move = lambda v, by: blk_route(v, lambda i: i + by)

    after = lambda v, *earlier: lax.optimization_barrier((v, *earlier))[0]
    numbers = jnp.concatenate([inv_width, lax.axis_index("sub").astype(F32).reshape(1)])
    numbers = jnp.broadcast_to(numbers[:, None], (2, TILE))
    wide = embeddings.shape[1] + width
    packed = lambda rows, lanes: jax.ShapeDtypeStruct((rows, lanes), BF16)
    above = blk_move(embeddings, -2)
    first, last, panel_mark = vmem_call(
        pack_body,
        (packed(size, wide), packed(size + MARK, wide), packed(half + MARK, width)),
        embeddings,
        start_panel,
        tile_mask,
        long=False,
    )
    relayed = n_blk == 8
    swapped = blk_route(last, lambda i: i ^ 1) if relayed else last
    above_panel = blk_move(panel_mark, -2)
    own = (first, last, sub_move(first), sub_move(last))
    image, turned = shape(half, width), shape(width, 2 * half)
    self_image = vmem_call(self_body, image, numbers, *own, long=False)
    below0 = blk_move(after(first, swapped, self_image), 1)
    swapped = after(swapped, self_image)
    below1 = blk_route(swapped, lambda i: i if i & 1 else i + 2) if relayed else blk_move(swapped, 1)
    above_image, back, above_sq, above_panel = vmem_call(
        above_own_body,
        (image, turned, image, packed(half + MARK, width)),
        numbers,
        above,
        above_panel,
        *own,
    )
    piece = shape(size, width)
    below1 = after(below1, above_image)
    other1 = sub_move(below1)
    below_image1, back = vmem_call(below_last_body, (piece, turned), numbers, below1, *own, back)
    below0 = after(below0, below_image1)
    other0 = sub_move(below0)
    here = (numbers, above, above_panel, above_sq)
    above_image, below_sum1, below_cross1 = vmem_call(
        above_below_last_body, (image, piece, piece), *here, below1, other1, after(above_image, below0)
    )
    above_image, below_sum0, below_cross0 = vmem_call(
        above_below_first_body, (image, piece, piece), *here, below1, other1, below0, other0, above_image
    )
    below_image0, own_image, own_cross = vmem_call(
        below_first_body, (piece, image, image), numbers, below1, below0, *own, self_image, after(back, above_image)
    )
    above_image = blk_move(above_image, 2)
    join = lambda *parts: jnp.concatenate(parts, axis=0)
    below_cross = sub_move(join(below_cross0, below_cross1))
    below_image = join(below_sum0, below_sum1) + below_cross + join(below_image0, below_image1)
    below_image = blk_move(below_image, -1)
    image_rows, gram = vmem_call(
        gram_body, (image, shape(width, width)), own_image, sub_move(own_cross), below_image, above_image
    )
    if n_blk & (n_blk - 1):
        gram = lax.psum(gram, ("blk", "sub"))
    else:
        gram = gram + sub_move(gram)
        hop = 1
        while hop < n_blk:
            gram = gram + blk_route(gram, lambda i: i ^ hop)
            hop *= 2
    return vmem_call(basis_body, (image, shape(width, width)), image_rows, gram)


def solution(mesh):
    return jax.shard_map(
        per_device,
        mesh=mesh,
        in_specs=(
            P(("groups", "blk", "sub"), None),
            P(("groups", "blk", "sub"), None),
            P(("groups", "blk", "sub"), None),
            P(),
        ),
        out_specs=(P(("groups", "blk", "sub"), None), P("groups", None)),
        check_vma=False,
    )
```

```python
import jax
import jax.numpy as jnp
from jax import lax
from jax.experimental import pallas as pl
from jax.experimental.pallas import tpu as pltpu
from jax.sharding import PartitionSpec as P

TILE = 128
REACH = 3
F32 = jnp.float32
BF16 = jnp.bfloat16
HIGHEST = lax.Precision.HIGHEST


def vmem_call(body, out_shapes, *operands, long=True):
    in_vmem = pl.BlockSpec(memory_space=pltpu.VMEM)
    return pl.pallas_call(
        body,
        out_shape=out_shapes,
        in_specs=[in_vmem] * len(operands),
        out_specs=jax.tree.map(lambda _: in_vmem, out_shapes),
        compiler_params=pltpu.CompilerParams(vmem_limit_bytes=24 << 20),
        cost_estimate=pl.CostEstimate(flops=2 * 10**10 if long else 1, transcendentals=0, bytes_accessed=1),
    )(*operands)


def shape(*dims):
    return jax.ShapeDtypeStruct(dims, F32)


def contract(a, b, dims, precision=None):
    return lax.dot_general(a, b, (dims, ((), ())), precision=precision, preferred_element_type=F32)


MARK = 8
OWN, BELOW, ABOVE = 0, 1, -2


def pair_mask(sub, rows, cols, offset, which):
    tiles = rows.shape[0]
    padded, lanes = rows.shape[1], tiles * TILE
    tile_of = lax.broadcasted_iota(jnp.int32, (padded, lanes), 1) // TILE
    first = (REACH + offset) * 2 * tiles + (sub if which == 0 else 1 - sub) * tiles
    chosen = (lax.broadcasted_iota(jnp.int32, (padded, lanes), 0) == first + tile_of).astype(F32)
    ahead = contract(rows, chosen, ((1,), (0,)))
    first = (REACH - offset) * 2 * tiles + sub * tiles
    row_at = lax.broadcasted_iota(jnp.int32, (tiles, padded), 0)
    chosen = (lax.broadcasted_iota(jnp.int32, (tiles, padded), 1) == first + row_at).astype(F32)
    spread = (lax.broadcasted_iota(jnp.int32, (tiles, lanes), 0) == tile_of[:tiles]).astype(F32)
    back = contract(contract(chosen, cols, ((1,), (1,))), spread, ((1,), (0,)))
    return jnp.concatenate([ahead, back], axis=0)


def marks(ref, half):
    return ref[ref.shape[0] - MARK :, ref.shape[1] - TILE :].astype(F32)[: half // TILE]


def pieces(*refs):
    size = min(r.shape[0] for r in refs)
    return [(r[:size, : r.shape[1] - TILE], r[:size, r.shape[1] - TILE :]) for r in refs]


def apart(features, panel):
    size = features.shape[0] // 2
    return [(features[rows], panel[rows]) for rows in (slice(0, size), slice(size, 2 * size))]


def squares(features):
    wide = features.astype(F32)
    return jnp.sum(wide * wide, axis=1, keepdims=True)


def as_row(column):
    return jnp.broadcast_to(column, (column.shape[0], TILE)).T[:1]


def as_column(row):
    return jnp.broadcast_to(row, (TILE, row.shape[1])).T[:, :1]


SPLIT = 3


def square_rows(ref):
    size = ref.shape[0] - MARK
    parts = ref[size:, : 2 * size].astype(F32)
    row = (parts[0:1] + parts[1:2]) + parts[2:3]
    return [row[:, :size], row[:, size:]]


def columns_of(own, other, sq_rows, masks):
    out = []
    for half, mask in zip((own, other), masks):
        for k, (features, panel) in enumerate(half):
            size = features.shape[0]
            out.append((features, panel, sq_rows[len(out)], mask[:, k * size : (k + 1) * size]))
    return out


def products(inverse, rows, squares_of, columns, back, first=0):
    panels = jnp.concatenate([panel for _, panel, _, _ in columns], axis=0)
    images = []
    for r, (features, panel) in enumerate(rows):
        size = features.shape[0]
        row_sq = squares_of[r]
        doubled = features * 2
        tile = (first + r) * size // TILE
        ahead, behind = [], []
        for other, _, col_sq, mask in columns:
            tiles = mask.shape[0] // 2
            gram2 = contract(doubled, other, ((1,), (1,)))
            kernel = jnp.exp(-inverse * jnp.maximum(row_sq + col_sq - gram2, 0.0))

            def masked(first):
                parts = [kernel[i * TILE : (i + 1) * TILE] * mask[first + i : first + i + 1] for i in range(size // TILE)]
                return jnp.concatenate(parts, axis=0).astype(BF16)

            ahead.append(masked(tile))
            if back is not None:
                behind.append(masked(tiles + tile))
        images.append(contract(jnp.concatenate(ahead, axis=1), panels, ((1,), (0,))))
        if back is not None:
            panel_t = panel.astype(F32).T.astype(BF16)
            back = back + contract(panel_t, jnp.concatenate(behind, axis=1), ((1,), (0,)))
    return jnp.concatenate(images, axis=0), back


def pack_body(embeddings, panel, tile_mask, first, last, panel_mark):
    half, features = embeddings.shape
    size = half // 2
    tiles, window = tile_mask.shape
    at = lax.broadcasted_iota(jnp.int32, (window, TILE), 0) == lax.broadcasted_iota(jnp.int32, (window, TILE), 1)
    mask = contract(tile_mask[...].astype(F32), at.astype(F32), ((1,), (0,)))
    mask = jnp.concatenate([mask, jnp.zeros((MARK - tiles, TILE), F32)], axis=0).astype(BF16)
    for ref, start in ((first, 0), (last, size)):
        ref[:size, :features] = embeddings[start : start + size]
        ref[:size, features:] = panel[start : start + size]
    row = as_row(jnp.concatenate([squares(r[:size, :features]) for r in (first, last)], axis=0))
    carried = []
    for _ in range(SPLIT):
        carried.append(row.astype(BF16).astype(F32))
        row = row - carried[-1]
    carried = jnp.concatenate(carried + [jnp.zeros((MARK - SPLIT, half), F32)], axis=0).astype(BF16)
    first[size:, :features] = jnp.concatenate([carried, jnp.zeros((MARK, features - half), BF16)], axis=1)
    first[size:, features:] = mask
    panel_mark[:half] = panel[...]
    panel_mark[half:] = mask


def width_of(numbers):
    return numbers[0:1, 0:1]


def place(numbers):
    return jnp.where(numbers[1:2, 0:1] > 0.5, 1, 0)


def masks_of(sub, rows, others, offset):
    return [pair_mask(sub, rows, r, offset, h) for h, r in enumerate(others)]


def self_body(numbers, first, last, other_first, other_last, image):
    half = 2 * last.shape[0]
    own, other = pieces(first, last), pieces(other_first, other_last)
    rows = square_rows(first)
    both = [marks(r, half) for r in (first, other_first)]
    columns = columns_of(own, other, rows + square_rows(other_first), masks_of(place(numbers), both[0], both, OWN))
    image[...], _ = products(width_of(numbers), own, [as_column(r) for r in rows], columns, None)


def own_columns(place_here, mark, first, last, other_first, other_last, offset):
    half = 2 * last.shape[0]
    masks = masks_of(place_here, mark, [marks(r, half) for r in (first, other_first)], offset)
    rows = square_rows(first) + square_rows(other_first)
    return columns_of(pieces(first, last), pieces(other_first, other_last), rows, masks)


def above_own_body(numbers, above, panel, first, last, other_first, other_last, image, back, above_sq, kept_panel):
    half = above.shape[0]
    size = half // 2
    columns = own_columns(place(numbers), marks(panel, half), first, last, other_first, other_last, ABOVE)
    kept_panel[...] = panel[...]
    rows = apart(above, panel)
    columns_sq = [squares(features) for features, _ in rows]
    for k, column in enumerate(columns_sq):
        above_sq[k * size : (k + 1) * size] = jnp.broadcast_to(column, (size, TILE))
    image[...], back[...] = products(width_of(numbers), rows, columns_sq, columns, jnp.zeros(back.shape, F32))


def below_first_body(numbers, below, first, last, other_first, other_last, back, image, total):
    half = 2 * last.shape[0]
    columns = own_columns(place(numbers), marks(below, half), first, last, other_first, other_last, BELOW)
    rows_sq = [as_column(square_rows(below)[0])]
    image[...], total[...] = products(width_of(numbers), [pieces(below, last)[0]], rows_sq, columns, back[...])


def below_last_body(
    numbers, marked, below, first, last, other_first, other_last, back, image, total
):
    half = 2 * last.shape[0]
    columns = own_columns(place(numbers), marks(marked, half), first, last, other_first, other_last, BELOW)
    rows_sq = [as_column(square_rows(marked)[1])]
    image[...], total[...] = products(width_of(numbers), pieces(below), rows_sq, columns, back[...], 1)


def own_body(self_image, back, image, cross):
    half = image.shape[0]
    image[...] = self_image[...] + back[:, :half].T
    cross[...] = back[:, half:].T


def above_below(part, numbers, above, panel, above_sq, marked, other_marked, below, other, above_image, image, below_image, cross):
    half = image.shape[0]
    size = half // 2
    masks = masks_of(place(numbers), marks(panel, half), [marks(r, half) for r in (marked, other_marked)], ABOVE - BELOW)
    masks = [mask[:, part * size : (part + 1) * size] for mask in masks]
    columns_sq = [square_rows(r)[part] for r in (marked, other_marked)]
    columns = columns_of([(below[:size, :-TILE], below[:size, -TILE:])], [(other[:size, :-TILE], other[:size, -TILE:])], columns_sq, masks)
    rows_sq = [above_sq[k * size : (k + 1) * size, :1] for k in range(2)]
    products_image, total = products(width_of(numbers), apart(above, panel), rows_sq, columns, jnp.zeros((TILE, half), F32))
    image[...] = above_image[...] + products_image
    below_image[...] = total[:, :size].T
    cross[...] = total[:, size:].T


def above_below_first_body(numbers, above, panel, above_sq, below, other, above_image, *outs):
    above_below(0, numbers, above, panel, above_sq, below, other, below, other, above_image, *outs)


def above_below_last_body(numbers, above, panel, above_sq, marked, other_marked, below, other, above_image, *outs):
    above_below(1, numbers, above, panel, above_sq, marked, other_marked, below, other, above_image, *outs)


def gram_body(own, cross, below, above, image, gram):
    total = own[...] + cross[...] + below[...] + above[...]
    image[...] = total
    gram[...] = contract(total, total, ((0,), (0,)), HIGHEST)


GROUP = 8


def full(value):
    return jnp.broadcast_to(value, (GROUP, value.shape[1] if value.shape[1] > 1 else TILE))


def factor(gram, block):
    size = gram.shape[0]
    groups = size // GROUP
    upper = [gram[GROUP * r : GROUP * (r + 1)] for r in range(groups)]
    row = lax.broadcasted_iota(jnp.int32, (GROUP, size), 0)
    col = lax.broadcasted_iota(jnp.int32, (GROUP, size), 1)
    inverse = [jnp.where(col == row + GROUP * r, 1.0, 0.0).astype(F32) for r in range(groups)]
    for b in range(0, groups, block):
        if b:
            done_upper, done_inverse = jnp.concatenate(upper[:b], axis=0), jnp.concatenate(inverse[:b], axis=0)
            coefficients = done_upper[:, GROUP * b : GROUP * (b + block)]
            less_upper = contract(coefficients, done_upper, ((0,), (0,)), HIGHEST)
            less_inverse = contract(coefficients, done_inverse, ((0,), (0,)), HIGHEST)
            for k in range(block):
                upper[b + k] = upper[b + k] - less_upper[GROUP * k : GROUP * (k + 1)]
                inverse[b + k] = inverse[b + k] - less_inverse[GROUP * k : GROUP * (k + 1)]
        for r in range(b, b + block):
            lane = GROUP * r
            columns = [full(upper[r][:, lane + k : lane + k + 1]) for k in range(GROUP)]
            diag = [[full(columns[j][i : i + 1]) for j in range(i + 1)] for i in range(GROUP)]
            lower = [[None] * GROUP for _ in range(GROUP)]
            scale = [None] * GROUP
            for i in range(GROUP):
                scale[i] = lax.rsqrt(diag[i][i])
                for k in range(i + 1, GROUP):
                    lower[k][i] = diag[k][i] * scale[i]
                for k in range(i + 1, GROUP):
                    for j in range(i + 1, k + 1):
                        diag[k][j] = diag[k][j] - lower[k][i] * lower[j][i]
            u = [full(upper[r][i : i + 1]) for i in range(GROUP)]
            v = [full(inverse[r][i : i + 1]) for i in range(GROUP)]
            for i in range(GROUP):
                u[i], v[i] = u[i] * scale[i], v[i] * scale[i]
                for k in range(i + 1, GROUP):
                    u[k], v[k] = u[k] - lower[k][i] * u[i], v[k] - lower[k][i] * v[i]
            upper[r], inverse[r] = u[0], v[0]
            for i in range(1, GROUP):
                upper[r] = jnp.where(row == i, u[i], upper[r])
                inverse[r] = jnp.where(row == i, v[i], inverse[r])
            for later in range(r + 1, b + block):
                left = [full(upper[later][:, lane + k : lane + k + 1]) for k in range(GROUP)]
                for i in range(GROUP):
                    left[i] = left[i] * scale[i]
                    for k in range(i + 1, GROUP):
                        left[k] = left[k] - lower[k][i] * left[i]
                    upper[later] = upper[later] - left[i] * u[i]
                    inverse[later] = inverse[later] - left[i] * v[i]
    at_row = lax.broadcasted_iota(jnp.int32, (size, size), 0)
    at_col = lax.broadcasted_iota(jnp.int32, (size, size), 1)
    return jnp.where(at_col >= at_row, jnp.concatenate(upper, axis=0), 0.0), jnp.concatenate(inverse, axis=0)


def basis_body(image, gram, basis, upper):
    upper[...], inverse = factor(gram[...], 4)
    basis[...] = contract(image[...], inverse, ((1,), (1,)), HIGHEST)


def per_device(embeddings, start_panel, tile_mask, inv_width):
    n_blk = lax.axis_size("blk")
    half, width = start_panel.shape
    size = half // 2
    sub_move = lambda v: lax.ppermute(v, "sub", [(0, 1), (1, 0)])
    blk_route = lambda v, to: lax.ppermute(v, "blk", [(i, to(i) % n_blk) for i in range(n_blk)])
    blk_move = lambda v, by: blk_route(v, lambda i: i + by)

    after = lambda v, *earlier: lax.optimization_barrier((v, *earlier))[0]
    numbers = jnp.concatenate([inv_width, lax.axis_index("sub").astype(F32).reshape(1)])
    numbers = jnp.broadcast_to(numbers[:, None], (2, TILE))
    wide = embeddings.shape[1] + width
    packed = lambda rows, lanes: jax.ShapeDtypeStruct((rows, lanes), BF16)
    above = blk_move(embeddings, -2)
    first, last, panel_mark = vmem_call(
        pack_body,
        (packed(size + MARK, wide), packed(size, wide), packed(half + MARK, width)),
        embeddings,
        start_panel,
        tile_mask,
        long=False,
    )
    relayed = n_blk == 8
    swapped = blk_route(last, lambda i: i ^ 1) if relayed else last
    above_panel = blk_move(panel_mark, -2)
    own = (first, last, sub_move(first), sub_move(last))
    image, turned = shape(half, width), shape(width, 2 * half)
    self_image = vmem_call(self_body, image, numbers, *own, long=False)
    below0 = blk_move(after(first, swapped, self_image), 1)
    swapped = after(swapped, self_image)
    below1 = blk_route(swapped, lambda i: i if i & 1 else i + 2) if relayed else blk_move(swapped, 1)
    above_image, back, above_sq, above_panel = vmem_call(
        above_own_body,
        (image, turned, image, packed(half + MARK, width)),
        numbers,
        above,
        above_panel,
        *own,
    )
    piece = shape(size, width)
    below0 = after(below0, above_image)
    other0 = sub_move(below0)
    below_image0, back = vmem_call(below_first_body, (piece, turned), numbers, below0, *own, back)
    below1 = after(below1, below_image0)
    other1 = sub_move(below1)
    here = (numbers, above, above_panel, above_sq)
    above_image, below_sum0, below_cross0 = vmem_call(
        above_below_first_body, (image, piece, piece), *here, below0, other0, after(above_image, below1)
    )
    above_image, below_sum1, below_cross1 = vmem_call(
        above_below_last_body, (image, piece, piece), *here, below0, other0, below1, other1, above_image
    )
    below_image1, back = vmem_call(
        below_last_body, (piece, turned), numbers, below0, below1, *own, after(back, above_image)
    )
    above_image = blk_move(above_image, 2)
    join = lambda *parts: jnp.concatenate(parts, axis=0)
    below_cross = sub_move(join(below_cross0, below_cross1))
    below_image = join(below_sum0, below_sum1) + below_cross + join(below_image0, below_image1)
    own_image, own_cross = vmem_call(own_body, (image, image), self_image, after(back, above_image))
    below_image = blk_move(below_image, -1)
    image_rows, gram = vmem_call(
        gram_body, (image, shape(width, width)), own_image, sub_move(own_cross), below_image, above_image
    )
    if n_blk & (n_blk - 1):
        gram = lax.psum(gram, ("blk", "sub"))
    else:
        gram = gram + sub_move(gram)
        hop = 1
        while hop < n_blk:
            gram = gram + blk_route(gram, lambda i: i ^ hop)
            hop *= 2
    return vmem_call(basis_body, (image, shape(width, width)), image_rows, gram)


def solution(mesh):
    return jax.shard_map(
        per_device,
        mesh=mesh,
        in_specs=(
            P(("groups", "blk", "sub"), None),
            P(("groups", "blk", "sub"), None),
            P(("groups", "blk", "sub"), None),
            P(),
        ),
        out_specs=(P(("groups", "blk", "sub"), None), P("groups", None)),
        check_vma=False,
    )
```

```python
import jax
import jax.numpy as jnp
from jax import lax
from jax.experimental import pallas as pl
from jax.experimental.pallas import tpu as pltpu
from jax.sharding import PartitionSpec as P

TILE = 128
REACH = 3
F32 = jnp.float32
BF16 = jnp.bfloat16
HIGHEST = lax.Precision.HIGHEST


def vmem_call(body, out_shapes, *operands, long=True):
    in_vmem = pl.BlockSpec(memory_space=pltpu.VMEM)
    return pl.pallas_call(
        body,
        out_shape=out_shapes,
        in_specs=[in_vmem] * len(operands),
        out_specs=jax.tree.map(lambda _: in_vmem, out_shapes),
        compiler_params=pltpu.CompilerParams(vmem_limit_bytes=24 << 20),
        cost_estimate=pl.CostEstimate(flops=2 * 10**10 if long else 1, transcendentals=0, bytes_accessed=1),
    )(*operands)


def shape(*dims):
    return jax.ShapeDtypeStruct(dims, F32)


def contract(a, b, dims, precision=None):
    return lax.dot_general(a, b, (dims, ((), ())), precision=precision, preferred_element_type=F32)


MARK = 8
OWN, BELOW, ABOVE = 0, 1, -2


def pair_mask(sub, rows, cols, offset, which):
    tiles = rows.shape[0]
    padded, lanes = rows.shape[1], tiles * TILE
    tile_of = lax.broadcasted_iota(jnp.int32, (padded, lanes), 1) // TILE
    first = (REACH + offset) * 2 * tiles + (sub if which == 0 else 1 - sub) * tiles
    chosen = (lax.broadcasted_iota(jnp.int32, (padded, lanes), 0) == first + tile_of).astype(F32)
    ahead = contract(rows, chosen, ((1,), (0,)))
    first = (REACH - offset) * 2 * tiles + sub * tiles
    row_at = lax.broadcasted_iota(jnp.int32, (tiles, padded), 0)
    chosen = (lax.broadcasted_iota(jnp.int32, (tiles, padded), 1) == first + row_at).astype(F32)
    spread = (lax.broadcasted_iota(jnp.int32, (tiles, lanes), 0) == tile_of[:tiles]).astype(F32)
    back = contract(contract(chosen, cols, ((1,), (1,))), spread, ((1,), (0,)))
    return jnp.concatenate([ahead, back], axis=0)


def marks(ref, half):
    return ref[ref.shape[0] - MARK :, ref.shape[1] - TILE :].astype(F32)[: half // TILE]


def pieces(*refs):
    size = min(r.shape[0] for r in refs)
    return [(r[:size, : r.shape[1] - TILE], r[:size, r.shape[1] - TILE :]) for r in refs]


def apart(features, panel):
    size = features.shape[0] // 2
    return [(features[rows], panel[rows]) for rows in (slice(0, size), slice(size, 2 * size))]


def squares(features):
    wide = features.astype(F32)
    return jnp.sum(wide * wide, axis=1, keepdims=True)


def as_row(column):
    return jnp.broadcast_to(column, (column.shape[0], TILE)).T[:1]


def as_column(row):
    return jnp.broadcast_to(row, (TILE, row.shape[1])).T[:, :1]


SPLIT = 3


def square_rows(ref):
    size = ref.shape[0] - MARK
    parts = ref[size:, : 2 * size].astype(F32)
    row = (parts[0:1] + parts[1:2]) + parts[2:3]
    return [row[:, :size], row[:, size:]]


def columns_of(own, other, sq_rows, masks):
    out = []
    for half, mask in zip((own, other), masks):
        for k, (features, panel) in enumerate(half):
            size = features.shape[0]
            out.append((features, panel, sq_rows[len(out)], mask[:, k * size : (k + 1) * size]))
    return out


def products(inverse, rows, squares_of, columns, back, first=0):
    panels = jnp.concatenate([panel for _, panel, _, _ in columns], axis=0)
    images = []
    for r, (features, panel) in enumerate(rows):
        size = features.shape[0]
        row_sq = squares_of[r]
        doubled = features * 2
        tile = (first + r) * size // TILE
        ahead, behind = [], []
        for other, _, col_sq, mask in columns:
            tiles = mask.shape[0] // 2
            gram2 = contract(doubled, other, ((1,), (1,)))
            kernel = jnp.exp(-inverse * jnp.maximum(row_sq + col_sq - gram2, 0.0))

            def masked(first):
                parts = [kernel[i * TILE : (i + 1) * TILE] * mask[first + i : first + i + 1] for i in range(size // TILE)]
                return jnp.concatenate(parts, axis=0).astype(BF16)

            ahead.append(masked(tile))
            if back is not None:
                behind.append(masked(tiles + tile))
        images.append(contract(jnp.concatenate(ahead, axis=1), panels, ((1,), (0,))))
        if back is not None:
            panel_t = panel.astype(F32).T.astype(BF16)
            back = back + contract(panel_t, jnp.concatenate(behind, axis=1), ((1,), (0,)))
    return jnp.concatenate(images, axis=0), back


def pack_body(embeddings, panel, tile_mask, first, last, panel_mark):
    half, features = embeddings.shape
    size = half // 2
    tiles, window = tile_mask.shape
    at = lax.broadcasted_iota(jnp.int32, (window, TILE), 0) == lax.broadcasted_iota(jnp.int32, (window, TILE), 1)
    mask = contract(tile_mask[...].astype(F32), at.astype(F32), ((1,), (0,)))
    mask = jnp.concatenate([mask, jnp.zeros((MARK - tiles, TILE), F32)], axis=0).astype(BF16)
    for ref, start in ((first, 0), (last, size)):
        ref[:size, :features] = embeddings[start : start + size]
        ref[:size, features:] = panel[start : start + size]
    row = as_row(jnp.concatenate([squares(r[:size, :features]) for r in (first, last)], axis=0))
    carried = []
    for _ in range(SPLIT):
        carried.append(row.astype(BF16).astype(F32))
        row = row - carried[-1]
    carried = jnp.concatenate(carried + [jnp.zeros((MARK - SPLIT, half), F32)], axis=0).astype(BF16)
    first[size:, :features] = jnp.concatenate([carried, jnp.zeros((MARK, features - half), BF16)], axis=1)
    first[size:, features:] = mask
    panel_mark[:half] = panel[...]
    panel_mark[half:] = mask


def width_of(numbers):
    return numbers[0:1, 0:1]


def place(numbers):
    return jnp.where(numbers[1:2, 0:1] > 0.5, 1, 0)


def masks_of(sub, rows, others, offset):
    return [pair_mask(sub, rows, r, offset, h) for h, r in enumerate(others)]


def self_body(numbers, first, last, other_first, other_last, image):
    half = 2 * last.shape[0]
    own, other = pieces(first, last), pieces(other_first, other_last)
    rows = square_rows(first)
    both = [marks(r, half) for r in (first, other_first)]
    columns = columns_of(own, other, rows + square_rows(other_first), masks_of(place(numbers), both[0], both, OWN))
    image[...], _ = products(width_of(numbers), own, [as_column(r) for r in rows], columns, None)


def own_columns(place_here, mark, first, last, other_first, other_last, offset):
    half = 2 * last.shape[0]
    masks = masks_of(place_here, mark, [marks(r, half) for r in (first, other_first)], offset)
    rows = square_rows(first) + square_rows(other_first)
    return columns_of(pieces(first, last), pieces(other_first, other_last), rows, masks)


def above_own_body(numbers, above, panel, first, last, other_first, other_last, image, back, above_sq, kept_panel):
    half = above.shape[0]
    size = half // 2
    columns = own_columns(place(numbers), marks(panel, half), first, last, other_first, other_last, ABOVE)
    kept_panel[...] = panel[...]
    rows = apart(above, panel)
    columns_sq = [squares(features) for features, _ in rows]
    for k, column in enumerate(columns_sq):
        above_sq[k * size : (k + 1) * size] = jnp.broadcast_to(column, (size, TILE))
    image[...], back[...] = products(width_of(numbers), rows, columns_sq, columns, jnp.zeros(back.shape, F32))


def below_first_body(numbers, below, first, last, other_first, other_last, back, image, total):
    half = 2 * last.shape[0]
    columns = own_columns(place(numbers), marks(below, half), first, last, other_first, other_last, BELOW)
    rows_sq = [as_column(square_rows(below)[0])]
    image[...], total[...] = products(width_of(numbers), [pieces(below, last)[0]], rows_sq, columns, back[...])


def below_last_body(
    numbers, marked, below, first, last, other_first, other_last, self_image, back, image, own_image, own_cross
):
    half = 2 * last.shape[0]
    columns = own_columns(place(numbers), marks(marked, half), first, last, other_first, other_last, BELOW)
    rows_sq = [as_column(square_rows(marked)[1])]
    image[...], total = products(width_of(numbers), pieces(below), rows_sq, columns, back[...], 1)
    own_image[...] = self_image[...] + total[:, :half].T
    own_cross[...] = total[:, half:].T


def above_below(part, numbers, above, panel, above_sq, marked, other_marked, below, other, above_image, image, below_image, cross):
    half = image.shape[0]
    size = half // 2
    masks = masks_of(place(numbers), marks(panel, half), [marks(r, half) for r in (marked, other_marked)], ABOVE - BELOW)
    masks = [mask[:, part * size : (part + 1) * size] for mask in masks]
    columns_sq = [square_rows(r)[part] for r in (marked, other_marked)]
    columns = columns_of([(below[:size, :-TILE], below[:size, -TILE:])], [(other[:size, :-TILE], other[:size, -TILE:])], columns_sq, masks)
    rows_sq = [above_sq[k * size : (k + 1) * size, :1] for k in range(2)]
    products_image, total = products(width_of(numbers), apart(above, panel), rows_sq, columns, jnp.zeros((TILE, half), F32))
    image[...] = above_image[...] + products_image
    below_image[...] = total[:, :size].T
    cross[...] = total[:, size:].T


def above_below_first_body(numbers, above, panel, above_sq, below, other, above_image, *outs):
    above_below(0, numbers, above, panel, above_sq, below, other, below, other, above_image, *outs)


def above_below_last_body(numbers, above, panel, above_sq, marked, other_marked, below, other, above_image, *outs):
    above_below(1, numbers, above, panel, above_sq, marked, other_marked, below, other, above_image, *outs)


def gram_body(own, cross, below, above, image, gram):
    total = own[...] + cross[...] + below[...] + above[...]
    image[...] = total
    gram[...] = contract(total, total, ((0,), (0,)), HIGHEST)


GROUP = 8


def full(value):
    return jnp.broadcast_to(value, (GROUP, value.shape[1] if value.shape[1] > 1 else TILE))


def factor(gram, block):
    size = gram.shape[0]
    groups = size // GROUP
    upper = [gram[GROUP * r : GROUP * (r + 1)] for r in range(groups)]
    row = lax.broadcasted_iota(jnp.int32, (GROUP, size), 0)
    col = lax.broadcasted_iota(jnp.int32, (GROUP, size), 1)
    inverse = [jnp.where(col == row + GROUP * r, 1.0, 0.0).astype(F32) for r in range(groups)]
    for b in range(0, groups, block):
        if b:
            done_upper, done_inverse = jnp.concatenate(upper[:b], axis=0), jnp.concatenate(inverse[:b], axis=0)
            coefficients = done_upper[:, GROUP * b : GROUP * (b + block)]
            less_upper = contract(coefficients, done_upper, ((0,), (0,)), HIGHEST)
            less_inverse = contract(coefficients, done_inverse, ((0,), (0,)), HIGHEST)
            for k in range(block):
                upper[b + k] = upper[b + k] - less_upper[GROUP * k : GROUP * (k + 1)]
                inverse[b + k] = inverse[b + k] - less_inverse[GROUP * k : GROUP * (k + 1)]
        for r in range(b, b + block):
            lane = GROUP * r
            columns = [full(upper[r][:, lane + k : lane + k + 1]) for k in range(GROUP)]
            diag = [[full(columns[j][i : i + 1]) for j in range(i + 1)] for i in range(GROUP)]
            lower = [[None] * GROUP for _ in range(GROUP)]
            scale = [None] * GROUP
            for i in range(GROUP):
                scale[i] = lax.rsqrt(diag[i][i])
                for k in range(i + 1, GROUP):
                    lower[k][i] = diag[k][i] * scale[i]
                for k in range(i + 1, GROUP):
                    for j in range(i + 1, k + 1):
                        diag[k][j] = diag[k][j] - lower[k][i] * lower[j][i]
            u = [full(upper[r][i : i + 1]) for i in range(GROUP)]
            v = [full(inverse[r][i : i + 1]) for i in range(GROUP)]
            for i in range(GROUP):
                u[i], v[i] = u[i] * scale[i], v[i] * scale[i]
                for k in range(i + 1, GROUP):
                    u[k], v[k] = u[k] - lower[k][i] * u[i], v[k] - lower[k][i] * v[i]
            upper[r], inverse[r] = u[0], v[0]
            for i in range(1, GROUP):
                upper[r] = jnp.where(row == i, u[i], upper[r])
                inverse[r] = jnp.where(row == i, v[i], inverse[r])
            for later in range(r + 1, b + block):
                left = [full(upper[later][:, lane + k : lane + k + 1]) for k in range(GROUP)]
                for i in range(GROUP):
                    left[i] = left[i] * scale[i]
                    for k in range(i + 1, GROUP):
                        left[k] = left[k] - lower[k][i] * left[i]
                    upper[later] = upper[later] - left[i] * u[i]
                    inverse[later] = inverse[later] - left[i] * v[i]
    at_row = lax.broadcasted_iota(jnp.int32, (size, size), 0)
    at_col = lax.broadcasted_iota(jnp.int32, (size, size), 1)
    return jnp.where(at_col >= at_row, jnp.concatenate(upper, axis=0), 0.0), jnp.concatenate(inverse, axis=0)


def basis_body(image, gram, basis, upper):
    upper[...], inverse = factor(gram[...], 8)
    basis[...] = contract(image[...], inverse, ((1,), (1,)), HIGHEST)


def per_device(embeddings, start_panel, tile_mask, inv_width):
    n_blk = lax.axis_size("blk")
    half, width = start_panel.shape
    size = half // 2
    sub_move = lambda v: lax.ppermute(v, "sub", [(0, 1), (1, 0)])
    blk_route = lambda v, to: lax.ppermute(v, "blk", [(i, to(i) % n_blk) for i in range(n_blk)])
    blk_move = lambda v, by: blk_route(v, lambda i: i + by)

    after = lambda v, *earlier: lax.optimization_barrier((v, *earlier))[0]
    numbers = jnp.concatenate([inv_width, lax.axis_index("sub").astype(F32).reshape(1)])
    numbers = jnp.broadcast_to(numbers[:, None], (2, TILE))
    wide = embeddings.shape[1] + width
    packed = lambda rows, lanes: jax.ShapeDtypeStruct((rows, lanes), BF16)
    above = blk_move(embeddings, -2)
    first, last, panel_mark = vmem_call(
        pack_body,
        (packed(size + MARK, wide), packed(size, wide), packed(half + MARK, width)),
        embeddings,
        start_panel,
        tile_mask,
        long=False,
    )
    relayed = n_blk == 8
    swapped = blk_route(last, lambda i: i ^ 1) if relayed else last
    above_panel = blk_move(panel_mark, -2)
    own = (first, last, sub_move(first), sub_move(last))
    image, turned = shape(half, width), shape(width, 2 * half)
    self_image = vmem_call(self_body, image, numbers, *own, long=False)
    below0 = blk_move(after(first, swapped, self_image), 1)
    swapped = after(swapped, self_image)
    below1 = blk_route(swapped, lambda i: i if i & 1 else i + 2) if relayed else blk_move(swapped, 1)
    above_image, back, above_sq, above_panel = vmem_call(
        above_own_body,
        (image, turned, image, packed(half + MARK, width)),
        numbers,
        above,
        above_panel,
        *own,
    )
    piece = shape(size, width)
    below0 = after(below0, above_image)
    other0 = sub_move(below0)
    below_image0, back = vmem_call(below_first_body, (piece, turned), numbers, below0, *own, back)
    below1 = after(below1, below_image0)
    other1 = sub_move(below1)
    here = (numbers, above, above_panel, above_sq)
    above_image, below_sum0, below_cross0 = vmem_call(
        above_below_first_body, (image, piece, piece), *here, below0, other0, after(above_image, below1)
    )
    above_image, below_sum1, below_cross1 = vmem_call(
        above_below_last_body, (image, piece, piece), *here, below0, other0, below1, other1, above_image
    )
    below_image1, own_image, own_cross = vmem_call(
        below_last_body, (piece, image, image), numbers, below0, below1, *own, self_image, after(back, above_image)
    )
    above_image = blk_move(above_image, 2)
    join = lambda *parts: jnp.concatenate(parts, axis=0)
    below_cross = sub_move(join(below_cross0, below_cross1))
    below_image = join(below_sum0, below_sum1) + below_cross + join(below_image0, below_image1)
    below_image = blk_move(below_image, -1)
    image_rows, gram = vmem_call(
        gram_body, (image, shape(width, width)), own_image, sub_move(own_cross), below_image, above_image
    )
    if n_blk & (n_blk - 1):
        gram = lax.psum(gram, ("blk", "sub"))
    else:
        gram = gram + sub_move(gram)
        hop = 1
        while hop < n_blk:
            gram = gram + blk_route(gram, lambda i: i ^ hop)
            hop *= 2
    return vmem_call(basis_body, (image, shape(width, width)), image_rows, gram)


def solution(mesh):
    return jax.shard_map(
        per_device,
        mesh=mesh,
        in_specs=(
            P(("groups", "blk", "sub"), None),
            P(("groups", "blk", "sub"), None),
            P(("groups", "blk", "sub"), None),
            P(),
        ),
        out_specs=(P(("groups", "blk", "sub"), None), P("groups", None)),
        check_vma=False,
    )
```
